256 devices in a mesh: lon: 16 (over x, y_lo, core), lat: 8 (over z), tm: 2 (over y_hi).
Axes of the slice: x: 4, y: 4 (y_hi: 2, y_lo: 2; y = y_hi * 2 + y_lo), z: 8, core: 2. Of those that a mesh axis runs over, the one named last changes fastest.
Arguments:
- snapshots: float32 [16, 8, 128, 2048], P('tm', None, 'lat', 'lon'), may hold values from -6 to 6
- basis: float32 [64, 8, 128, 2048], P(None, None, 'lat', 'lon'), may hold values from -6 to 6
Outputs:
- new_basis: float32 [64, 8, 128, 2048], P(None, None, 'lat', 'lon')
- coeffs: float32 [64, 16], P(None, 'tm')
The draws below stay inside these ranges and needn't reach their ends.
All inputs are finite; a program needn't handle non-finite values.
Results may differ from the reference program's by a relative error of at most 0.00011.
Values sent between devices are 32-bit elements; how exact they have to be, the bound alone decides.
No kernel may reach another device: no remote copies, remote signals or barrier semaphores. Data moves between devices by JAX's collectives and lax.ppermute only.
A program may use at most 64 MiB of HBM per device.

```python
import math
import jax
import jax.numpy as jnp
from jax import lax

EOFS = 64
LEV = 8
NLAT = 128
NLON = 2048
SNAPS = 16
CELLS = 2097152


def steps_of(own_key, dims, split, low, high):
    def one(dim, parts):
        steps = jax.random.uniform(jax.random.fold_in(jax.random.fold_in(own_key, 6), dim), (parts,), jnp.float32, low / len(split), high / len(split))
        return jnp.repeat(jnp.exp(steps), dims[dim] // parts).reshape((-1,) + (1,) * (len(dims) - dim - 1))

    gain = one(*split[0])
    for cut in split[1:]:
        gain = gain * one(*cut)
    return gain


def noise(key, shape, deviation, most, split=(), held_as=jnp.bfloat16):
    values = deviation * jax.random.normal(key, shape, jnp.float32)
    if split:
        values = values * steps_of(key, shape, split, -0.22, 0.18)
    return jnp.clip(values, -most, most).astype(held_as)


def setup_inputs(seed: int = 0) -> dict:
    splits = jax.random.split(jax.random.key(seed), 3)
    return {
        "snapshots": noise(splits[0], (SNAPS, LEV, NLAT, NLON), 1.0, 6.0, ((0, 2), (2, 8), (3, 16)), jnp.float32),
        "basis": noise(splits[1], (EOFS, LEV, NLAT, NLON), 1.0, 6.0, ((2, 8), (3, 16)), jnp.float32),
    }


SMOOTH_RATE = 0.1
STEP_SIZE = 0.25

def product(left, right):
    return jnp.dot(left.astype(jnp.float32), right.astype(jnp.float32), precision=lax.Precision.HIGHEST, preferred_element_type=jnp.float32)

def smooth_pass(values):
    padded_lev = jnp.pad(values, ((0, 0), (1, 1), (0, 0), (0, 0)))
    padded_lat = jnp.pad(values, ((0, 0), (0, 0), (1, 1), (0, 0)))
    neighbours = padded_lev[:, 2:] + padded_lev[:, :-2] + padded_lat[:, :, 2:] + padded_lat[:, :, :-2]
    neighbours = neighbours + jnp.roll(values, 1, 3) + jnp.roll(values, -1, 3)
    return values + SMOOTH_RATE * (neighbours - 6.0 * values)

def reference(snapshots, basis):
    smoothed = snapshots
    for sweep in range(3):
        smoothed = smooth_pass(smoothed)
    flattened = smoothed.reshape(SNAPS, CELLS)
    columns = basis.reshape(EOFS, CELLS)
    inv_root = 1.0 / math.sqrt(CELLS)
    coeffs = product(columns, flattened.T) * inv_root
    grown = columns + STEP_SIZE * product(coeffs, flattened)
    gram_matrix = product(grown, grown.T) / CELLS
    factor = jnp.linalg.cholesky(gram_matrix)
    new_basis = jax.scipy.linalg.solve_triangular(factor, grown, lower=True)
    return (new_basis.reshape(basis.shape), coeffs)
```

```python
import functools
import math

import jax
import jax.numpy as jnp
from jax import lax
from jax.experimental import pallas as pl
from jax.experimental.pallas import tpu as pltpu
from jax.sharding import PartitionSpec as P

SMOOTH_RATE = 0.1
STEP_SIZE = 0.25
SNAPS = 8
LEVELS = 8
ROWS = 16
LANES = 128
EOFS = 64
CELL_ROWS = LEVELS * ROWS
HALF_ROWS = CELL_ROWS // 2
SLOTS = 16
PAYLOAD = 48
F32 = jnp.float32
BF16 = jnp.bfloat16
HIGHEST = lax.Precision.HIGHEST


def lanes_of(shape):
    return lax.broadcasted_iota(jnp.int32, shape, len(shape) - 1)


def pack_kernel(x_ref, packed_ref):
    lane = lanes_of((64, LANES))
    packed = jnp.zeros((64, LANES), F32)
    for slot in range(SLOTS):
        turned = pltpu.roll(x_ref[pl.ds(64 * slot, 64), :], (3 + 8 * slot) % LANES, 1)
        packed = jnp.where((lane >= 8 * slot) & (lane < 8 * slot + 6), turned, packed)
    packed_ref[...] = packed


def edges_kernel(x_ref, west_ref, east_ref, ghosts_ref, low_ref, high_ref):
    lane = lanes_of((64, LANES))
    ghosts = jnp.where(lane % 8 < 3, west_ref[...], east_ref[...])
    ghosts_ref[...] = ghosts
    for row in range(3):
        low_ref[pl.ds(64 * row, 64), :] = x_ref[pl.ds(row, 64, stride=ROWS), :]
        high_ref[pl.ds(64 * row, 64), :] = x_ref[pl.ds(ROWS - 3 + row, 64, stride=ROWS), :]
    low_ref[pl.ds(192, 64), :] = ghosts
    high_ref[pl.ds(192, 64), :] = ghosts


def smooth_kernel(flags_ref, x_ref, ghosts_ref, south_ref, north_ref, keep_ref, send_ref, own, ghost):
    half = flags_ref[0]
    row = lax.broadcasted_iota(jnp.int32, (32, LANES), 0)
    lane = lanes_of((32, LANES))
    first, last = lane == 0, lane == LANES - 1
    outside = ((row < 8) & (flags_ref[1] == 1)) | ((row >= 24) & (flags_ref[2] == 1))

    def snapshot(snap, carry):
        for level in range(LEVELS):
            own[pl.ds(32 * level + 8, ROWS), :] = x_ref[pl.ds(pl.multiple_of(snap * 128 + 16 * level, 16), ROWS), :]
        for edge in range(3):
            at = pl.ds(pl.multiple_of(64 * edge + 8 * snap, 8), LEVELS)
            own[pl.ds(5 + edge, LEVELS, stride=32), :] = south_ref[at, :]
            own[pl.ds(24 + edge, LEVELS, stride=32), :] = north_ref[at, :]
        for level in range(LEVELS):
            slot = 2 * snap + level // 4
            shift = lax.rem(253 - 8 * slot, LANES)
            at = 16 * (level % 4)
            strip = jnp.concatenate(
                [
                    south_ref[pl.ds(192 + at + 8, 8), :],
                    ghosts_ref[pl.ds(at, 16), :],
                    north_ref[pl.ds(192 + at, 8), :],
                ],
                axis=0,
            )
            ghost[pl.ds(32 * level, 32), :] = pltpu.roll(strip, shift, 1)
        for sweep in range(3):
            below_own = below_ghost = None
            for level in range(LEVELS):
                at = pl.ds(32 * level, 32)
                here_own, here_ghost = own[at, :], ghost[at, :]
                left_own, left_ghost = pltpu.roll(here_own, 1, 1), pltpu.roll(here_ghost, 1, 1)
                right_own, right_ghost = pltpu.roll(here_own, LANES - 1, 1), pltpu.roll(here_ghost, LANES - 1, 1)
                sums = []
                for here, below, ref, left, other_left, right, other_right in (
                    (here_own, below_own, own, left_own, left_ghost, right_own, right_ghost),
                    (here_ghost, below_ghost, ghost, left_ghost, left_own, right_ghost, right_own),
                ):
                    near = pltpu.roll(here, 1, 0) + pltpu.roll(here, 31, 0)
                    if level < LEVELS - 1:
                        near = near + ref[pl.ds(32 * level + 32, 32), :]
                    if level > 0:
                        near = near + below
                    near = near + jnp.where(first, other_left, left) + jnp.where(last, other_right, right)
                    fresh = here + SMOOTH_RATE * (near - 6.0 * here)
                    if sweep < 2:
                        fresh = jnp.where(outside, 0.0, fresh)
                    sums.append(fresh)
                below_own, below_ghost = here_own, here_ghost
                own[at, :] = sums[0]
                if sweep < 2:
                    ghost[at, :] = sums[1]
        for level in range(LEVELS // 2):
            to = pl.ds(pl.multiple_of(64 * snap + 16 * level, 16), ROWS)
            keep_at = pl.multiple_of(32 * (4 * half + level) + 8, 8)
            send_at = pl.multiple_of(32 * (4 * (1 - half) + level) + 8, 8)
            keep_ref[to, :] = own[pl.ds(keep_at, ROWS), :]
            send_ref[to, :] = own[pl.ds(send_at, ROWS), :]
        return carry

    lax.fori_loop(0, SNAPS, snapshot, 0)


def in_order(flags_ref, mine, other):
    early = jnp.where(flags_ref[0] == 0, mine, other)
    late = jnp.where(flags_ref[0] == 0, other, mine)
    return early, late


def take(ref, row):
    fields, rows, lanes = ref.shape
    return ref.reshape(fields * rows, lanes)[pl.ds(row, fields, stride=rows), :]


def put(ref, row, values):
    fields, rows, lanes = ref.shape
    ref.reshape(fields * rows, lanes)[pl.ds(row, fields, stride=rows), :] = values


def pieces(values, count):
    out = []
    for index in range(count):
        piece = values.astype(BF16)
        out.append(piece)
        if index < count - 1:
            values = values - piece.astype(F32)
    return out


def gram_kernel(flags_ref, q_ref, mine_ref, other_ref, out_ref, stack, total):
    total[...] = jnp.zeros_like(total)

    def block(step, carry):
        for inner in range(8):
            row = 8 * step + inner
            early, late = in_order(
                flags_ref,
                mine_ref[pl.ds(row, SNAPS, stride=HALF_ROWS), :],
                other_ref[pl.ds(row, SNAPS, stride=HALF_ROWS), :],
            )
            joined = jnp.concatenate([take(q_ref, row), early, late], axis=0)
            for index, piece in enumerate(pieces(joined, 3)):
                stack[pl.ds(80 * index, 80), pl.ds(LANES * inner, LANES)] = piece
        total[...] += lax.dot_general(
            stack[...], stack[...], (((1,), (1,)), ((), ())), preferred_element_type=F32
        )
        return carry

    lax.fori_loop(0, HALF_ROWS // 8, block, 0)
    down = total[pl.ds(0, 80), :] + total[pl.ds(80, 80), :] + total[pl.ds(160, 80), :]
    gram = down[:, 0:80] + down[:, 80:160] + down[:, 160:240]
    out_ref[pl.ds(0, 32), pl.ds(0, 64)] = gram[0:32, 0:64]
    out_ref[pl.ds(0, 32), pl.ds(64, 64)] = gram[32:64, 0:64]
    out_ref[pl.ds(32, 16), :] = jnp.concatenate([gram[64:80, :], jnp.zeros((16, 48), F32)], axis=1)


def factor_kernel(cells, flags_ref, sums_ref, maps_ref, coeffs_ref):
    totals = sums_ref[0]
    for index in range(1, sums_ref.shape[0]):
        totals = totals + sums_ref[index]
    basis_gram = jnp.concatenate([totals[0:32, 0:64], totals[0:32, 64:128]], axis=0)
    root = math.sqrt(cells)
    coeffs_t = totals[32:48, 0:64] * (1.0 / root)
    snap_gram = totals[32:48, 64:80]
    half = flags_ref[0]
    coeffs_ref[...] = jnp.where(half == 0, coeffs_t[0:8, :], coeffs_t[8:16, :])
    mixed = (2.0 * STEP_SIZE * root) * coeffs_t + (STEP_SIZE * STEP_SIZE) * jnp.dot(
        snap_gram, coeffs_t, precision=HIGHEST, preferred_element_type=F32
    )
    grown = lax.dot_general(
        coeffs_t, mixed, (((0,), (0,)), ((), ())), precision=HIGHEST, preferred_element_type=F32
    )
    gram = (basis_gram + grown) * (1.0 / cells)
    rows = lax.broadcasted_iota(jnp.int32, (EOFS, EOFS), 0)
    columns = lax.broadcasted_iota(jnp.int32, (EOFS, EOFS), 1)
    work = jnp.concatenate([gram, (rows == columns).astype(F32)], axis=1)
    row_index = lax.broadcasted_iota(jnp.int32, (EOFS, LANES), 0)
    scale = jnp.zeros((EOFS, LANES), F32)
    for step in range(EOFS):
        row = work[step : step + 1, :]
        pivot = work[step : step + 1, step : step + 1]
        column = work[:, step : step + 1]
        scaled = row * (1.0 / pivot)
        work = work - jnp.where(row_index > step, column * scaled, 0.0)
        scale = jnp.where(row_index == step, lax.rsqrt(pivot), scale)
    inverse = (work * scale)[:, EOFS:]
    update = lax.dot_general(
        inverse, coeffs_t, (((1,), (1,)), ((), ())), precision=HIGHEST, preferred_element_type=F32
    )
    maps = jnp.concatenate([inverse, STEP_SIZE * update], axis=1)
    high, low = pieces(maps, 2)
    maps_ref[pl.ds(0, EOFS), :] = jnp.concatenate([high, high], axis=1)
    maps_ref[pl.ds(EOFS, EOFS), :] = jnp.concatenate([low, low], axis=1)


FINAL_ROWS = 16


def final_kernel(flags_ref, maps_ref, q_ref, keep_ref, here_ref, send_ref, late_ref, out_ref, stack):
    step = pl.program_id(0)
    per_half = HALF_ROWS // FINAL_ROWS

    def work(mine_ref, other_ref):
        base = lax.rem(step, per_half) * FINAL_ROWS
        for inner in range(FINAL_ROWS):
            at = pl.ds(base + inner, SNAPS, stride=HALF_ROWS)
            early, late = in_order(flags_ref, mine_ref[at, :], other_ref[at, :])
            joined = jnp.concatenate([take(q_ref, inner), early, late], axis=0)
            for index, piece in enumerate(pieces(joined, 2)):
                stack[pl.ds(80 * index, 80), pl.ds(LANES * inner, LANES)] = piece

    @pl.when(step < per_half)
    def _():
        work(keep_ref, here_ref)

    @pl.when(step >= per_half)
    def _():
        work(send_ref, late_ref)

    both = jnp.dot(maps_ref[...], stack[...], preferred_element_type=F32)
    result = both[0:EOFS, :] + both[EOFS:, :]
    for inner in range(FINAL_ROWS):
        put(out_ref, inner, result[:, LANES * inner : LANES * (inner + 1)])


SMEM = pl.BlockSpec(memory_space=pltpu.SMEM)
VMEM = pl.BlockSpec(memory_space=pltpu.VMEM)


def call(kernel, inputs, outputs, scratch=(), flops=1000000, traffic=1000000):
    return pl.pallas_call(
        kernel,
        out_shape=outputs,
        in_specs=inputs,
        out_specs=jax.tree.map(lambda _: VMEM, outputs),
        scratch_shapes=scratch,
        cost_estimate=pl.CostEstimate(flops=flops, bytes_accessed=traffic, transcendentals=0),
    )


def shape(*dims, dtype=F32):
    return jax.ShapeDtypeStruct(dims, dtype)


def neighbours(values_up, values_down, axis, closed):
    count = lax.axis_size(axis)
    ends = count if closed else count - 1
    from_below = lax.ppermute(values_up, axis, [(i, (i + 1) % count) for i in range(ends)])
    from_above = lax.ppermute(values_down, axis, [((i + 1) % count, i) for i in range(ends)])
    return from_below, from_above


def across_tm(values):
    return lax.ppermute(values, "tm", [(0, 1), (1, 0)])


def gathered(values, axes, count):
    return lax.all_to_all(jnp.broadcast_to(values, (count,) + values.shape), axes, 0, 0)


def shards(snapshots, basis):
    lat_count, lon_count = lax.axis_size("lat"), lax.axis_size("lon")
    cells = LEVELS * ROWS * LANES * lat_count * lon_count
    lat = lax.axis_index("lat")
    flags = jnp.stack([lax.axis_index("tm"), (lat == 0).astype(jnp.int32), (lat == lat_count - 1).astype(jnp.int32)]).astype(jnp.int32)
    x = snapshots.reshape(SNAPS * CELL_ROWS, LANES)
    q = basis.reshape(EOFS, CELL_ROWS, LANES)

    packed = call(pack_kernel, [VMEM], shape(64, LANES))(x)
    west, east = neighbours(packed, packed, "lon", True)
    ghosts, low, high = call(edges_kernel, [VMEM] * 3, (shape(64, LANES), shape(256, LANES), shape(256, LANES)))(x, west, east)
    south, north = neighbours(high, low, "lat", False)
    keep, send = call(
        smooth_kernel,
        [SMEM] + [VMEM] * 4,
        (shape(SNAPS * HALF_ROWS, LANES),) * 2,
        [pltpu.VMEM((32 * LEVELS, LANES), F32)] * 2,
    )(flags, x, ghosts, south, north)
    here = across_tm(send)
    late = across_tm(keep)
    partial = pl.pallas_call(
        gram_kernel,
        grid_spec=pltpu.PrefetchScalarGridSpec(
            num_scalar_prefetch=1,
            grid=(1,),
            in_specs=[
                pl.BlockSpec((EOFS, HALF_ROWS, LANES), lambda i, flags: (0, flags[0], 0)),
                pl.BlockSpec((SNAPS * HALF_ROWS, LANES), lambda i, flags: (0, 0)),
                pl.BlockSpec((SNAPS * HALF_ROWS, LANES), lambda i, flags: (0, 0)),
            ],
            out_specs=pl.BlockSpec((PAYLOAD, LANES), lambda i, flags: (0, 0)),
            scratch_shapes=[pltpu.VMEM((240, 1024), BF16), pltpu.VMEM((240, 240), F32)],
        ),
        out_shape=shape(PAYLOAD, LANES),
    )(flags, q, keep, here)
    first = gathered(partial, ("lon", "tm"), lon_count * 2).sum(0)
    second = gathered(first, "lat", lat_count)
    maps, coeffs_t = call(
        functools.partial(factor_kernel, cells), [SMEM, VMEM], (shape(2 * EOFS, 160, dtype=BF16), shape(SNAPS, EOFS))
    )(flags, second)
    per_half = HALF_ROWS // FINAL_ROWS
    whole = pl.BlockSpec((SNAPS * HALF_ROWS, LANES), lambda i, flags: (0, 0))

    def basis_block(i, flags):
        half = jnp.where(i < per_half, flags[0], 1 - flags[0])
        return (0, half * per_half + lax.rem(i, per_half), 0)

    new_basis = pl.pallas_call(
        final_kernel,
        grid_spec=pltpu.PrefetchScalarGridSpec(
            num_scalar_prefetch=1,
            grid=(2 * per_half,),
            in_specs=[
                pl.BlockSpec((2 * EOFS, 160), lambda i, flags: (0, 0)),
                pl.BlockSpec((EOFS, FINAL_ROWS, LANES), basis_block),
                whole,
                whole,
                whole,
                whole,
            ],
            out_specs=pl.BlockSpec((EOFS, FINAL_ROWS, LANES), basis_block),
            scratch_shapes=[pltpu.VMEM((160, FINAL_ROWS * LANES), BF16)],
        ),
        out_shape=shape(EOFS, CELL_ROWS, LANES),
    )(flags, maps, q, keep, here, send, late)
    return (new_basis.reshape(basis.shape), coeffs_t.T)


def solution(mesh):
    placed = (P("tm", None, "lat", "lon"), P(None, None, "lat", "lon"))
    return jax.shard_map(
        shards,
        mesh=mesh,
        in_specs=placed,
        out_specs=(P(None, None, "lat", "lon"), P(None, "tm")),
        check_vma=False,
    )
```

```python
import functools
import math

import jax
import jax.numpy as jnp
from jax import lax
from jax.experimental import pallas as pl
from jax.experimental.pallas import tpu as pltpu
from jax.sharding import Mesh, PartitionSpec as P

SMOOTH_RATE = 0.1
STEP_SIZE = 0.25
SNAPS = 8
LEVELS = 8
ROWS = 16
LANES = 128
EOFS = 64
CELL_ROWS = LEVELS * ROWS
HALF_ROWS = CELL_ROWS // 2
HALF_CELLS = HALF_ROWS * LANES
CHUNK = 8
PAYLOAD = 48
LON = ("pair", "core")
F32 = jnp.float32
BF16 = jnp.bfloat16
HIGHEST = lax.Precision.HIGHEST
SMEM = pl.BlockSpec(memory_space=pltpu.SMEM)
VMEM = pl.BlockSpec(memory_space=pltpu.VMEM)


def lanes_of(shape):
    return lax.broadcasted_iota(jnp.int32, shape, len(shape) - 1)


def shape(*dims, dtype=F32):
    return jax.ShapeDtypeStruct(dims, dtype)


def call(kernel, inputs, outputs, scratch=(), flops=1000000, traffic=1000000, megabytes=8):
    return pl.pallas_call(
        kernel,
        out_shape=outputs,
        in_specs=inputs,
        out_specs=jax.tree.map(lambda _: VMEM, outputs),
        scratch_shapes=scratch,
        cost_estimate=pl.CostEstimate(flops=flops, bytes_accessed=traffic, transcendentals=0),
        compiler_params=pltpu.CompilerParams(vmem_limit_bytes=megabytes << 20),
    )


def pack_kernel(x_ref, packed_ref, low_ref, high_ref):
    lane = lanes_of((ROWS, LANES))
    for snap in range(SNAPS):
        packed = jnp.zeros((ROWS, LANES), F32)
        for level in range(LEVELS):
            turned = pltpu.roll(x_ref[snap, level], 16 * level + 3, 1)
            packed = jnp.where((lane >= 16 * level) & (lane < 16 * level + 6), turned, packed)
        packed_ref[pl.ds(ROWS * snap, ROWS), :] = packed
        low = jnp.swapaxes(x_ref[snap, :, pl.ds(0, 8), :], 0, 1)
        high = jnp.swapaxes(x_ref[snap, :, pl.ds(8, 8), :], 0, 1)
        for row in range(3):
            low_ref[row, pl.ds(LEVELS * snap, LEVELS), :] = low[row]
            high_ref[row, pl.ds(LEVELS * snap, LEVELS), :] = high[5 + row]


def seam_kernel(packed_ref, west_ref, east_ref, seam_ref, low_ref, high_ref):
    packed = packed_ref[...]
    lane = lanes_of(packed.shape) % 16
    west = jnp.where(lane < 3, west_ref[...] - packed, 0.0)
    east = pltpu.roll(jnp.where((lane >= 3) & (lane < 6), east_ref[...] - packed, 0.0), 8, 1)
    seam_ref[...] = west + east
    for snap in range(SNAPS):
        low_ref[pl.ds(8 * snap, 8), :] = seam_ref[pl.ds(ROWS * snap, 8), :]
        high_ref[pl.ds(8 * snap, 8), :] = seam_ref[pl.ds(ROWS * snap + 8, 8), :]


def smooth_kernel(
    flags_ref, x_ref, seam_ref, south_ref, north_ref, seam_south_ref, seam_north_ref, keep_ref, send_ref
):
    half = flags_ref[0]
    row = lax.broadcasted_iota(jnp.int32, (8, LANES), 0)
    lane = lanes_of((8, LANES))
    inside = jnp.where(row < 4, 1 - flags_ref[2], 1 - flags_ref[1]) == 1
    zero = jnp.zeros((8, LANES), F32)
    wide_lane = lanes_of((ROWS, LANES))

    def along_rows(field):
        tall = jnp.concatenate(field, axis=0)
        near = pltpu.roll(tall, 1, 0) + pltpu.roll(tall, 23, 0)
        return near[0:8], near[8:16], near[16:24]

    def snapshot(snap, carry):
        edges = jnp.swapaxes(
            jnp.stack(
                [north_ref[i, pl.ds(8 * snap, 8), :] for i in range(3)]
                + [zero, zero]
                + [south_ref[i, pl.ds(8 * snap, 8), :] for i in range(3)]
            ),
            0,
            1,
        )
        fields = [
            (x_ref[snap, level, pl.ds(0, 8), :], x_ref[snap, level, pl.ds(8, 8), :], edges[level])
            for level in range(LEVELS)
        ]
        at = pl.ds(pl.multiple_of(8 * snap, 8), 8)
        seam = (
            seam_ref[pl.ds(pl.multiple_of(ROWS * snap, 8), 8), :],
            seam_ref[pl.ds(pl.multiple_of(ROWS * snap + 8, 8), 8), :],
            jnp.where(row < 4, seam_north_ref[at, :], seam_south_ref[at, :]),
        )
        for sweep in range(3):
            tiles = 3 if sweep < 2 else 2
            fresh_fields = []
            for level in range(LEVELS):
                here = fields[level]
                rows = along_rows(here)
                fresh = []
                for tile in range(tiles):
                    near = rows[tile] + pltpu.roll(here[tile], 1, 1) + pltpu.roll(here[tile], LANES - 1, 1)
                    if level > 0:
                        near = near + fields[level - 1][tile]
                    if level < LEVELS - 1:
                        near = near + fields[level + 1][tile]
                    value = here[tile] + SMOOTH_RATE * (near - 6.0 * here[tile])
                    fresh.append(jnp.where(inside, value, 0.0) if tile == 2 else value)
                fresh_fields.append(tuple(fresh))
            rows = along_rows(seam)
            fresh = []
            for tile in range(tiles):
                here = seam[tile]
                near = rows[tile] + pltpu.roll(here, 1, 1) + pltpu.roll(here, LANES - 1, 1)
                near = near + jnp.where(lane >= 16, pltpu.roll(here, 16, 1), 0.0)
                near = near + jnp.where(lane < LANES - 16, pltpu.roll(here, LANES - 16, 1), 0.0)
                value = here + SMOOTH_RATE * (near - 6.0 * here)
                fresh.append(jnp.where(inside, value, 0.0) if tile == 2 else value)
            fields, seam = fresh_fields, tuple(fresh)
        tall_seam = jnp.concatenate(seam, axis=0)
        for level in range(LEVELS):
            first = pltpu.roll(tall_seam, (LANES - 16 * level - 3) % LANES, 1)
            last = pltpu.roll(tall_seam, (117 - 16 * level) % LANES, 1)
            value = jnp.concatenate(fields[level], axis=0)
            value = value + jnp.where(wide_lane < 3, first, jnp.where(wide_lane >= LANES - 3, last, 0.0))
            to = pl.ds(ROWS * (level % 4), ROWS)
            mine = half == level // 4

            @pl.when(mine)
            def _():
                keep_ref[snap, to, :] = value

            @pl.when(jnp.logical_not(mine))
            def _():
                send_ref[snap, to, :] = value

        return carry

    lax.fori_loop(0, SNAPS, snapshot, 0)


def pieces(values, count):
    out = []
    for index in range(count):
        piece = values.astype(BF16)
        out.append(piece)
        if index < count - 1:
            values = values - piece.astype(F32)
    return out


def transposed_product(left, right):
    return lax.dot_general(left, right, (((1,), (1,)), ((), ())), preferred_element_type=F32)


def basis_gram_kernel(flags_ref, q_ref, stack_ref, gram_ref, total):
    @pl.when(pl.program_id(0) == 0)
    def _():
        total[...] = jnp.zeros_like(total)

    for part in range(q_ref.shape[1] // CHUNK):
        turned = jnp.swapaxes(q_ref[:, pl.ds(CHUNK * part, CHUNK), :], 0, 1)
        for inner in range(CHUNK):
            for index, piece in enumerate(pieces(turned[inner], 3)):
                stack_ref[pl.ds(EOFS * index, EOFS), pl.ds(LANES * (CHUNK * part + inner), LANES)] = piece
    total[...] += transposed_product(stack_ref[...], stack_ref[...])

    @pl.when(pl.program_id(0) == pl.num_programs(0) - 1)
    def _():
        down = total[pl.ds(0, 64), :] + total[pl.ds(64, 64), :] + total[pl.ds(128, 64), :]
        gram_ref[...] = down[:, 0:64] + down[:, 64:128] + down[:, 128:192]


def basis_stack_kernel(flags_ref, q_ref, stack_ref):
    for part in range(q_ref.shape[1] // CHUNK):
        turned = jnp.swapaxes(q_ref[:, pl.ds(CHUNK * part, CHUNK), :], 0, 1)
        for inner in range(CHUNK):
            for index, piece in enumerate(pieces(turned[inner], 2)):
                stack_ref[pl.ds(EOFS * index, EOFS), pl.ds(LANES * (CHUNK * part + inner), LANES)] = piece


def snapshot_columns(flags_ref, mine_ref, other_ref, start, count):
    at = pl.ds(start, CHUNK)
    mine = jnp.swapaxes(mine_ref[:, at, :], 0, 1)
    other = jnp.swapaxes(other_ref[:, at, :], 0, 1)
    first = flags_ref[0] == 0
    early, late = jnp.where(first, mine, other), jnp.where(first, other, mine)
    columns = [jnp.concatenate(pieces(jnp.concatenate([early[i], late[i]], axis=0), count), axis=0) for i in range(CHUNK)]
    return jnp.concatenate(columns, axis=1)


def snapshot_gram_kernel(flags_ref, stack_ref, gram_ref, mine_ref, other_ref, own_ref, partner_ref, cross, square, joined):
    cross[...] = jnp.zeros_like(cross)
    square[...] = jnp.zeros_like(square)

    def block(step, carry):
        columns = snapshot_columns(flags_ref, mine_ref, other_ref, pl.multiple_of(CHUNK * step, CHUNK), 3)
        width = CHUNK * LANES
        stack = stack_ref[:, pl.ds(pl.multiple_of(width * step, width), width)]
        cross[...] += transposed_product(stack, columns)
        square[...] += transposed_product(columns, columns)
        return carry

    lax.fori_loop(0, HALF_ROWS // CHUNK, block, 0)
    down = cross[pl.ds(0, 64), :] + cross[pl.ds(64, 64), :] + cross[pl.ds(128, 64), :]
    projection = down[:, 0:16] + down[:, 16:32] + down[:, 32:48]
    down = square[pl.ds(0, 16), :] + square[pl.ds(16, 16), :] + square[pl.ds(32, 16), :]
    square_sum = down[:, 0:16] + down[:, 16:32] + down[:, 32:48]
    gram = gram_ref[...]
    joined[pl.ds(0, 32), pl.ds(0, 64)] = gram[0:32, :]
    joined[pl.ds(0, 32), pl.ds(64, 64)] = gram[32:64, :]
    joined[pl.ds(32, 16), pl.ds(0, 64)] = jnp.transpose(projection)
    joined[pl.ds(32, 16), pl.ds(64, 64)] = jnp.concatenate([square_sum, jnp.zeros((16, 48), F32)], axis=1)
    side = PAYLOAD // 2
    core = flags_ref[3]
    own_ref[...] = joined[pl.ds(pl.multiple_of(side * core, 8), side), :]
    partner_ref[...] = joined[pl.ds(pl.multiple_of(side * (1 - core), 8), side), :]


def factor_kernel(cells, flags_ref, mine_ref, other_ref, maps_ref, coeffs_ref):
    mine, other = mine_ref[...], other_ref[...]
    first = flags_ref[3] == 0
    totals = jnp.concatenate([jnp.where(first, mine, other), jnp.where(first, other, mine)], axis=0)
    basis_gram = jnp.concatenate([totals[0:32, 0:64], totals[0:32, 64:128]], axis=0)
    root = math.sqrt(cells)
    coeffs_t = totals[32:48, 0:64] * (1.0 / root)
    snap_gram = totals[32:48, 64:80]
    coeffs_ref[...] = jnp.where(flags_ref[0] == 0, coeffs_t[0:8, :], coeffs_t[8:16, :])
    mixed = (2.0 * STEP_SIZE * root) * coeffs_t + (STEP_SIZE * STEP_SIZE) * jnp.dot(
        snap_gram, coeffs_t, precision=HIGHEST, preferred_element_type=F32
    )
    grown = lax.dot_general(
        coeffs_t, mixed, (((0,), (0,)), ((), ())), precision=HIGHEST, preferred_element_type=F32
    )
    gram = (basis_gram + grown) * (1.0 / cells)
    rows = lax.broadcasted_iota(jnp.int32, (EOFS, EOFS), 0)
    columns = lax.broadcasted_iota(jnp.int32, (EOFS, EOFS), 1)
    work = jnp.concatenate([gram, (rows == columns).astype(F32)], axis=1)
    row_index = lax.broadcasted_iota(jnp.int32, (EOFS, LANES), 0)
    scale = jnp.zeros((EOFS, LANES), F32)
    for step in range(EOFS):
        row = work[step : step + 1, :]
        pivot = work[step : step + 1, step : step + 1]
        column = work[:, step : step + 1]
        scaled = row * (1.0 / pivot)
        work = work - jnp.where(row_index > step, column * scaled, 0.0)
        scale = jnp.where(row_index == step, lax.rsqrt(pivot), scale)
    inverse = (work * scale)[:, EOFS:]
    update = lax.dot_general(
        inverse, coeffs_t, (((1,), (1,)), ((), ())), precision=HIGHEST, preferred_element_type=F32
    )
    rows = [
        jnp.concatenate([inverse_part, inverse_part, update_part, update_part], axis=1)
        for inverse_part, update_part in zip(pieces(inverse, 2), pieces(STEP_SIZE * update, 2))
    ]
    maps_ref[...] = jnp.concatenate(rows, axis=0)


FINAL_ROWS = 16
FINAL_STEPS = HALF_ROWS // FINAL_ROWS


def final_kernel(flags_ref, maps_ref, near_ref, far_ref, keep_ref, here_ref, send_ref, late_ref, out_ref):
    step = pl.program_id(0)

    def work(stack_ref, mine_ref, other_ref):
        for part in range(FINAL_ROWS // CHUNK):
            start = pl.multiple_of(lax.rem(step, FINAL_STEPS) * FINAL_ROWS + CHUNK * part, CHUNK)
            columns = snapshot_columns(flags_ref, mine_ref, other_ref, start, 2)
            stack = stack_ref[pl.ds(0, 2 * EOFS), pl.ds(pl.multiple_of(start * LANES, LANES), CHUNK * LANES)]
            both = jnp.dot(maps_ref[...], jnp.concatenate([stack, columns], axis=0), preferred_element_type=F32)
            result = both[0:EOFS, :] + both[EOFS:, :]
            result = jnp.stack([result[:, LANES * i : LANES * (i + 1)] for i in range(CHUNK)])
            out_ref[:, pl.ds(CHUNK * part, CHUNK), :] = jnp.swapaxes(result, 0, 1)

    @pl.when(step < FINAL_STEPS)
    def _():
        work(near_ref, keep_ref, here_ref)

    @pl.when(step >= FINAL_STEPS)
    def _():
        work(far_ref, send_ref, late_ref)


def neighbours(values_up, values_down, axis, closed):
    count = lax.axis_size(axis)
    ends = count if closed else count - 1
    from_below = lax.ppermute(values_up, axis, [(i, (i + 1) % count) for i in range(ends)])
    from_above = lax.ppermute(values_down, axis, [((i + 1) % count, i) for i in range(ends)])
    return from_below, from_above


def across(values, axis):
    return lax.ppermute(values, axis, [(0, 1), (1, 0)])


def gathered(values, axes):
    return lax.all_to_all(jnp.broadcast_to(values, (lax.axis_size(axes),) + values.shape), axes, 0, 0)


QSTEP = 16


def shards(snapshots, basis):
    lat_count = lax.axis_size("lat")
    cells = CELL_ROWS * LANES * lat_count * lax.axis_size(LON)
    lat = lax.axis_index("lat")
    flags = jnp.stack([lax.axis_index("tm"), lat == 0, lat == lat_count - 1, lax.axis_index("core")]).astype(jnp.int32)
    q = basis.reshape(EOFS, CELL_ROWS, LANES)

    packed, low, high = call(
        pack_kernel, [VMEM], (shape(CELL_ROWS, LANES), shape(3, 64, LANES), shape(3, 64, LANES))
    )(snapshots)
    west, east = neighbours(packed, packed, LON, True)
    south, north = neighbours(high, low, "lat", False)
    stack, gram = pl.pallas_call(
        basis_gram_kernel,
        grid_spec=pltpu.PrefetchScalarGridSpec(
            num_scalar_prefetch=1,
            grid=(HALF_ROWS // QSTEP,),
            in_specs=[pl.BlockSpec((EOFS, QSTEP, LANES), lambda i, flags: (0, flags[0] * (HALF_ROWS // QSTEP) + i, 0))],
            out_specs=[
                pl.BlockSpec((3 * EOFS, QSTEP * LANES), lambda i, flags: (0, i)),
                pl.BlockSpec((EOFS, EOFS), lambda i, flags: (0, 0)),
            ],
            scratch_shapes=[pltpu.VMEM((3 * EOFS, 3 * EOFS), F32)],
        ),
        out_shape=(shape(3 * EOFS, HALF_CELLS, dtype=BF16), shape(EOFS, EOFS)),
        cost_estimate=pl.CostEstimate(flops=600000000, bytes_accessed=5 << 20, transcendentals=0),
        compiler_params=pltpu.CompilerParams(vmem_limit_bytes=8 << 20),
    )(flags, q)
    seam, seam_low, seam_high = call(
        seam_kernel, [VMEM] * 3, (shape(CELL_ROWS, LANES), shape(64, LANES), shape(64, LANES))
    )(packed, west, east)
    seam_south, seam_north = neighbours(seam_high, seam_low, "lat", False)
    keep, send = call(
        smooth_kernel, [SMEM] + [VMEM] * 6, (shape(SNAPS, HALF_ROWS, LANES),) * 2
    )(flags, snapshots, seam, south, north, seam_south, seam_north)
    here = across(send, "tm")
    side = shape(PAYLOAD // 2, LANES)
    mine, theirs = call(
        snapshot_gram_kernel,
        [SMEM] + [VMEM] * 4,
        (side, side),
        [pltpu.VMEM((192, 48), F32), pltpu.VMEM((48, 48), F32), pltpu.VMEM((PAYLOAD, LANES), F32)],
    )(flags, stack, gram, keep, here)
    mine = mine + across(theirs, "core")
    mine = gathered(mine, ("pair", "tm")).sum(0)
    far = pl.pallas_call(
        basis_stack_kernel,
        grid_spec=pltpu.PrefetchScalarGridSpec(
            num_scalar_prefetch=1,
            grid=(HALF_ROWS // QSTEP,),
            in_specs=[
                pl.BlockSpec((EOFS, QSTEP, LANES), lambda i, flags: (0, (1 - flags[0]) * (HALF_ROWS // QSTEP) + i, 0))
            ],
            out_specs=pl.BlockSpec((2 * EOFS, QSTEP * LANES), lambda i, flags: (0, i)),
        ),
        out_shape=shape(2 * EOFS, HALF_CELLS, dtype=BF16),
        cost_estimate=pl.CostEstimate(flops=1000000, bytes_accessed=4 << 20, transcendentals=0),
        compiler_params=pltpu.CompilerParams(vmem_limit_bytes=8 << 20),
    )(flags, q)
    late = across(keep, "tm")
    mine = gathered(mine, "lat").sum(0)
    other = across(mine, "core")
    maps, coeffs_t = call(
        functools.partial(factor_kernel, cells),
        [SMEM, VMEM, VMEM],
        (shape(2 * EOFS, 160, dtype=BF16), shape(SNAPS, EOFS)),
    )(flags, mine, other)

    def basis_block(i, flags):
        half = jnp.where(i < FINAL_STEPS, flags[0], 1 - flags[0])
        return (0, half * FINAL_STEPS + lax.rem(i, FINAL_STEPS), 0)

    new_basis = pl.pallas_call(
        final_kernel,
        grid_spec=pltpu.PrefetchScalarGridSpec(
            num_scalar_prefetch=1,
            grid=(2 * FINAL_STEPS,),
            in_specs=[VMEM] * 7,
            out_specs=pl.BlockSpec((EOFS, FINAL_ROWS, LANES), basis_block),
        ),
        out_shape=shape(EOFS, CELL_ROWS, LANES),
        compiler_params=pltpu.CompilerParams(vmem_limit_bytes=8 << 20),
    )(flags, maps, stack, far, keep, here, send, late)
    return (new_basis.reshape(basis.shape), coeffs_t.T)


def solution(mesh):
    pairs = mesh.shape["lon"] // 2
    split = Mesh(mesh.devices.reshape(pairs, 2, *mesh.devices.shape[1:]), LON + tuple(mesh.axis_names[1:]))
    fields = P(None, None, "lat", LON)
    return jax.shard_map(
        shards,
        mesh=split,
        in_specs=(P("tm", None, "lat", LON), fields),
        out_specs=(fields, P(None, "tm")),
        check_vma=False,
    )
```

```python
import functools
import math

import jax
import jax.numpy as jnp
from jax import lax
from jax.experimental import pallas as pl
from jax.experimental.pallas import tpu as pltpu
from jax.sharding import Mesh, PartitionSpec as P

SMOOTH_RATE = 0.1
STEP_SIZE = 0.25
SNAPS = 8
LEVELS = 8
ROWS = 16
LANES = 128
EOFS = 64
CELL_ROWS = LEVELS * ROWS
HALF_ROWS = CELL_ROWS // 2
HALF_CELLS = HALF_ROWS * LANES
CHUNK = 8
PAYLOAD = 48
SIDE = PAYLOAD // 2
QROWS = 16
FINAL_ROWS = 16
LON = ("pair", "core")
F32 = jnp.float32
BF16 = jnp.bfloat16
HIGHEST = lax.Precision.HIGHEST
VMEM = pl.BlockSpec(memory_space=pltpu.VMEM)
ANY = pl.BlockSpec(memory_space=pl.ANY)


def lanes_of(shape):
    return lax.broadcasted_iota(jnp.int32, shape, len(shape) - 1)


def shape(*dims, dtype=F32):
    return jax.ShapeDtypeStruct(dims, dtype)


def call(kernel, inputs, outputs, scratch=(), flops=1000000, traffic=1000000, megabytes=8):
    return pl.pallas_call(
        kernel,
        out_shape=outputs,
        in_specs=inputs,
        out_specs=jax.tree.map(lambda _: VMEM, outputs),
        scratch_shapes=scratch,
        cost_estimate=pl.CostEstimate(flops=flops, bytes_accessed=traffic, transcendentals=0),
        compiler_params=pltpu.CompilerParams(vmem_limit_bytes=megabytes << 20),
    )


def pack_kernel(x_ref, packed_ref):
    lane = lanes_of((ROWS, LANES))
    for snap in range(SNAPS):
        packed = jnp.zeros((ROWS, LANES), F32)
        for level in range(LEVELS):
            turned = pltpu.roll(x_ref[snap, level], 16 * level + 3, 1)
            packed = jnp.where((lane >= 16 * level) & (lane < 16 * level + 6), turned, packed)
        packed_ref[pl.ds(ROWS * snap, ROWS), :] = packed


def seam_kernel(x_ref, packed_ref, west_ref, east_ref, seam_ref, low_ref, high_ref):
    packed = packed_ref[...]
    lane = lanes_of(packed.shape) % 16
    west = jnp.where(lane < 3, west_ref[...] - packed, 0.0)
    east = pltpu.roll(jnp.where((lane >= 3) & (lane < 6), east_ref[...] - packed, 0.0), 8, 1)
    seam_ref[...] = west + east
    for snap in range(SNAPS):
        at = pl.ds(8 * snap, 8)
        low = jnp.swapaxes(x_ref[snap, :, pl.ds(0, 8), :], 0, 1)
        high = jnp.swapaxes(x_ref[snap, :, pl.ds(8, 8), :], 0, 1)
        for row in range(3):
            low_ref[row, at, :] = low[row]
            high_ref[row, at, :] = high[5 + row]
        low_ref[3, at, :] = seam_ref[pl.ds(ROWS * snap, 8), :]
        high_ref[3, at, :] = seam_ref[pl.ds(ROWS * snap + 8, 8), :]


def smooth_kernel(x_ref, seam_ref, south_ref, north_ref, order_ref, keep_ref, send_ref, done):
    lat = lax.axis_index("lat")
    not_first = jnp.where(lat == 0, 0, 1)
    not_last = jnp.where(lat == lax.axis_size("lat") - 1, 0, 1)
    row = lax.broadcasted_iota(jnp.int32, (8, LANES), 0)
    lane = lanes_of((8, LANES))
    inside = jnp.where(row < 4, not_last, not_first) == 1
    zero = jnp.zeros((8, LANES), F32)
    wide_lane = lanes_of((ROWS, LANES))

    def along_rows(field):
        tall = jnp.concatenate(field, axis=0)
        near = pltpu.roll(tall, 1, 0) + pltpu.roll(tall, 23, 0)
        return near[0:8], near[8:16], near[16:24]

    def snapshot(snap, carry):
        edges = jnp.swapaxes(
            jnp.stack(
                [north_ref[i, pl.ds(8 * snap, 8), :] for i in range(3)]
                + [zero, zero]
                + [south_ref[i, pl.ds(8 * snap, 8), :] for i in range(3)]
            ),
            0,
            1,
        )
        fields = [
            (x_ref[snap, level, pl.ds(0, 8), :], x_ref[snap, level, pl.ds(8, 8), :], edges[level])
            for level in range(LEVELS)
        ]
        at = pl.ds(pl.multiple_of(8 * snap, 8), 8)
        seam = (
            seam_ref[pl.ds(pl.multiple_of(ROWS * snap, 8), 8), :],
            seam_ref[pl.ds(pl.multiple_of(ROWS * snap + 8, 8), 8), :],
            jnp.where(row < 4, north_ref[3, at, :], south_ref[3, at, :]),
        )
        for sweep in range(3):
            tiles = 3 if sweep < 2 else 2
            fresh_fields = []
            for level in range(LEVELS):
                here = fields[level]
                rows = along_rows(here)
                fresh = []
                for tile in range(tiles):
                    near = rows[tile] + pltpu.roll(here[tile], 1, 1) + pltpu.roll(here[tile], LANES - 1, 1)
                    if level > 0:
                        near = near + fields[level - 1][tile]
                    if level < LEVELS - 1:
                        near = near + fields[level + 1][tile]
                    value = here[tile] + SMOOTH_RATE * (near - 6.0 * here[tile])
                    fresh.append(jnp.where(inside, value, 0.0) if tile == 2 else value)
                fresh_fields.append(tuple(fresh))
            rows = along_rows(seam)
            fresh = []
            for tile in range(tiles):
                here = seam[tile]
                near = rows[tile] + pltpu.roll(here, 1, 1) + pltpu.roll(here, LANES - 1, 1)
                near = near + jnp.where(lane >= 16, pltpu.roll(here, 16, 1), 0.0)
                near = near + jnp.where(lane < LANES - 16, pltpu.roll(here, LANES - 16, 1), 0.0)
                value = here + SMOOTH_RATE * (near - 6.0 * here)
                fresh.append(jnp.where(inside, value, 0.0) if tile == 2 else value)
            fields, seam = fresh_fields, tuple(fresh)
        tall_seam = jnp.concatenate(seam, axis=0)
        for level in range(LEVELS):
            first = pltpu.roll(tall_seam, (LANES - 16 * level - 3) % LANES, 1)
            last = pltpu.roll(tall_seam, (117 - 16 * level) % LANES, 1)
            value = jnp.concatenate(fields[level], axis=0)
            value = value + jnp.where(wide_lane < 3, first, jnp.where(wide_lane >= LANES - 3, last, 0.0))
            done[snap, pl.ds(ROWS * level, ROWS), :] = value
        return carry

    lax.fori_loop(0, SNAPS, snapshot, 0)
    group = lax.axis_index("tm")
    for snap in range(SNAPS):
        keep_ref[snap] = done[snap, pl.ds(pl.multiple_of(HALF_ROWS * group, 8), HALF_ROWS), :]
        send_ref[snap] = done[snap, pl.ds(pl.multiple_of(HALF_ROWS * (1 - group), 8), HALF_ROWS), :]


def pieces(values, count):
    out = []
    for index in range(count):
        piece = values.astype(BF16)
        out.append(piece)
        if index < count - 1:
            values = values - piece.astype(F32)
    return out


def transposed_product(left, right):
    return lax.dot_general(left, right, (((1,), (1,)), ((), ())), preferred_element_type=F32)


def basis_copies(half, q_ref, blocks, sems):
    copies = [
        pltpu.make_async_copy(
            q_ref.at[:, pl.ds(pl.multiple_of(HALF_ROWS * half + QROWS * part, QROWS), QROWS), :],
            blocks.at[part],
            sems.at[part],
        )
        for part in range(HALF_ROWS // QROWS)
    ]
    for copy in copies:
        copy.start()
    return copies


def split_block(block, part, count, stack_ref):
    for sub in range(QROWS // CHUNK):
        turned = jnp.swapaxes(block[:, pl.ds(CHUNK * sub, CHUNK), :], 0, 1)
        for inner in range(CHUNK):
            at = pl.ds(LANES * (QROWS * part + CHUNK * sub + inner), LANES)
            for index, piece in enumerate(pieces(turned[inner], count)):
                stack_ref[pl.ds(EOFS * index, EOFS), at] = piece


def basis_gram_kernel(order_ref, q_ref, stack_ref, gram_ref, blocks, total, sems):
    copies = basis_copies(lax.axis_index("tm"), q_ref, blocks, sems)
    for part, copy in enumerate(copies):
        copy.wait()
        split_block(blocks.at[part], part, 3, stack_ref)
        stack = stack_ref[:, pl.ds(QROWS * LANES * part, QROWS * LANES)]
        product = transposed_product(stack, stack)
        total[...] = product if part == 0 else total[...] + product
    down = total[pl.ds(0, 64), :] + total[pl.ds(64, 64), :] + total[pl.ds(128, 64), :]
    gram_ref[...] = down[:, 0:64] + down[:, 64:128] + down[:, 128:192]


def basis_stack_kernel(order_ref, q_ref, stack_ref, blocks, sems):
    copies = basis_copies(1 - lax.axis_index("tm"), q_ref, blocks, sems)
    for part, copy in enumerate(copies):
        copy.wait()
        split_block(blocks.at[part], part, 2, stack_ref)


def snapshot_columns(ref, start, count):
    turned = jnp.swapaxes(ref[:, pl.ds(start, CHUNK), :], 0, 1)
    return [pieces(turned[i], count) for i in range(CHUNK)]


def side_by_side(early, late):
    columns = [
        jnp.concatenate([jnp.concatenate(pair, axis=0) for pair in zip(one, two)], axis=0) for one, two in zip(early, late)
    ]
    return jnp.concatenate(columns, axis=1)


def in_order(mine, other):
    first = lax.axis_index("tm") == 0
    return jnp.where(first, mine, other), jnp.where(first, other, mine)


def own_gram_kernel(stack_ref, mine_ref, cross_ref, square_ref):
    def block(step, carry):
        cross, square = carry
        columns = snapshot_columns(mine_ref, pl.multiple_of(CHUNK * step, CHUNK), 3)
        columns = jnp.concatenate([jnp.concatenate(c, axis=0) for c in columns], axis=1)
        width = CHUNK * LANES
        stack = stack_ref[:, pl.ds(pl.multiple_of(width * step, width), width)]
        return cross + transposed_product(stack, columns), square + transposed_product(columns, columns)

    zeros = (jnp.zeros((192, 24), F32), jnp.zeros((24, 24), F32))
    cross_ref[...], square_ref[...] = lax.fori_loop(0, HALF_ROWS // CHUNK, block, zeros)


def folded(sums, rows):
    down = sums[0:rows] + sums[rows : 2 * rows] + sums[2 * rows : 3 * rows]
    return down[:, 0:8] + down[:, 8:16] + down[:, 16:24]


def snapshot_gram_kernel(
    stack_ref, gram_ref, mine_ref, other_ref, cross_ref, square_ref, order_ref, own_ref, partner_ref, joined
):
    def block(step, carry):
        cross, square, mixed = carry
        start = pl.multiple_of(CHUNK * step, CHUNK)
        other = snapshot_columns(other_ref, start, 3)
        other = jnp.concatenate([jnp.concatenate(c, axis=0) for c in other], axis=1)
        mine = snapshot_columns(mine_ref, start, 3)
        mine = jnp.concatenate([jnp.concatenate(c, axis=0) for c in mine], axis=1)
        width = CHUNK * LANES
        stack = stack_ref[:, pl.ds(pl.multiple_of(width * step, width), width)]
        return (
            cross + transposed_product(stack, other),
            square + transposed_product(other, other),
            mixed + transposed_product(mine, other),
        )

    zeros = (jnp.zeros((192, 24), F32), jnp.zeros((24, 24), F32), jnp.zeros((24, 24), F32))
    cross, square, mixed = lax.fori_loop(0, HALF_ROWS // CHUNK, block, zeros)
    mixed = folded(mixed, 8)
    projection = jnp.concatenate(in_order(folded(cross_ref[...], 64), folded(cross, 64)), axis=1)
    early, late = in_order(folded(square_ref[...], 8), folded(square, 8))
    upper, _ = in_order(mixed, jnp.transpose(mixed))
    square = jnp.concatenate(
        [jnp.concatenate([early, upper], axis=1), jnp.concatenate([jnp.transpose(upper), late], axis=1)], axis=0
    )
    gram = gram_ref[...]
    joined[pl.ds(0, 32), pl.ds(0, 64)] = gram[0:32, :]
    joined[pl.ds(0, 32), pl.ds(64, 64)] = gram[32:64, :]
    joined[pl.ds(32, 16), pl.ds(0, 64)] = jnp.transpose(projection)
    joined[pl.ds(32, 16), pl.ds(64, 64)] = jnp.concatenate([square, jnp.zeros((16, 48), F32)], axis=1)
    core = lax.axis_index("core")
    own_ref[...] = joined[pl.ds(pl.multiple_of(SIDE * core, 8), SIDE), :]
    partner_ref[...] = joined[pl.ds(pl.multiple_of(SIDE * (1 - core), 8), SIDE), :]


def pair_kernel(one_ref, two_ref, out_ref):
    out_ref[...] = jnp.broadcast_to((one_ref[...] + two_ref[...])[None], out_ref.shape)


def group_kernel(parts_ref, out_ref):
    out_ref[...] = jnp.broadcast_to(jnp.sum(parts_ref[...], axis=0)[None], out_ref.shape)


def factor_kernel(cells, parts_ref, maps_ref, coeffs_ref):
    count = parts_ref.shape[0] // 2
    totals = jnp.concatenate(
        [jnp.sum(parts_ref[pl.ds(count * core, count)], axis=0) for core in range(2)], axis=0
    )
    basis_gram = jnp.concatenate([totals[0:32, 0:64], totals[0:32, 64:128]], axis=0)
    root = math.sqrt(cells)
    coeffs_t = totals[32:48, 0:64] * (1.0 / root)
    snap_gram = totals[32:48, 64:80]
    coeffs_ref[...] = jnp.where(lax.axis_index("tm") == 0, coeffs_t[0:8, :], coeffs_t[8:16, :])
    mixed = (2.0 * STEP_SIZE * root) * coeffs_t + (STEP_SIZE * STEP_SIZE) * jnp.dot(
        snap_gram, coeffs_t, precision=HIGHEST, preferred_element_type=F32
    )
    grown = lax.dot_general(
        coeffs_t, mixed, (((0,), (0,)), ((), ())), precision=HIGHEST, preferred_element_type=F32
    )
    gram = (basis_gram + grown) * (1.0 / cells)
    rows = lax.broadcasted_iota(jnp.int32, (EOFS, EOFS), 0)
    columns = lax.broadcasted_iota(jnp.int32, (EOFS, EOFS), 1)
    work = jnp.concatenate([gram, (rows == columns).astype(F32)], axis=1)
    blocks = [work[8 * i : 8 * i + 8, :] for i in range(8)]
    results = []
    for panel in range(8):
        lower = blocks[panel:]
        columns = [
            [jnp.broadcast_to(b[:, 8 * panel + k : 8 * panel + k + 1], (8, LANES)) for b in lower] for k in range(8)
        ]
        rows = [lower[0][k : k + 1, :] for k in range(8)]
        for k in range(8):
            pivot = columns[k][0][k : k + 1, :]
            inverse = 1.0 / pivot
            factors = [c * inverse for c in columns[k]]
            for m in range(k + 1, 8):
                entry = columns[m][0][k : k + 1, :]
                columns[m] = [c - f * entry for c, f in zip(columns[m], factors)]
                rows[m] = rows[m] - factors[0][m : m + 1, :] * rows[k]
            for i in range(panel + 1, 8):
                blocks[i] = blocks[i] - factors[i - panel] * rows[k]
            results.append(rows[k] * lax.rsqrt(pivot))
    inverse = jnp.concatenate(results, axis=0)[:, EOFS:]
    update = lax.dot_general(
        inverse, coeffs_t, (((1,), (1,)), ((), ())), precision=HIGHEST, preferred_element_type=F32
    )
    rows = [
        jnp.concatenate([inverse_part, inverse_part, update_part, update_part], axis=1)
        for inverse_part, update_part in zip(pieces(inverse, 2), pieces(STEP_SIZE * update, 2))
    ]
    maps_ref[...] = jnp.concatenate(rows, axis=0)


def final_kernel(maps_ref, near_ref, far_ref, keep_ref, here_ref, send_ref, late_ref, out_ref, blocks, sems):
    group = lax.axis_index("tm")
    steps = HALF_ROWS // FINAL_ROWS
    copies = []
    for step in range(2 * steps):
        near = step < steps
        half = group if near else 1 - group
        local = step % steps
        stack_ref, mine_ref, other_ref = (near_ref, keep_ref, here_ref) if near else (far_ref, send_ref, late_ref)
        for sub in range(FINAL_ROWS // CHUNK):
            start = local * FINAL_ROWS + CHUNK * sub
            at = pl.ds(start, CHUNK)
            early, late = in_order(
                jnp.swapaxes(mine_ref[:, at, :], 0, 1), jnp.swapaxes(other_ref[:, at, :], 0, 1)
            )
            columns = jnp.concatenate(
                [
                    jnp.concatenate(pieces(jnp.concatenate([early[i], late[i]], axis=0), 2), axis=0)
                    for i in range(CHUNK)
                ],
                axis=1,
            )
            stack = stack_ref[pl.ds(0, 2 * EOFS), pl.ds(start * LANES, CHUNK * LANES)]
            both = jnp.dot(maps_ref[...], jnp.concatenate([stack, columns], axis=0), preferred_element_type=F32)
            result = both[0:EOFS, :] + both[EOFS:, :]
            result = jnp.stack([result[:, LANES * i : LANES * (i + 1)] for i in range(CHUNK)])
            blocks[step, :, pl.ds(CHUNK * sub, CHUNK), :] = jnp.swapaxes(result, 0, 1)
        to = pl.ds(pl.multiple_of(HALF_ROWS * half + FINAL_ROWS * local, FINAL_ROWS), FINAL_ROWS)
        copy = pltpu.make_async_copy(blocks.at[step], out_ref.at[:, to, :], sems.at[step])
        copy.start()
        copies.append(copy)
    for copy in copies:
        copy.wait()


def neighbours(values_up, values_down, axis, closed):
    count = lax.axis_size(axis)
    ends = count if closed else count - 1
    from_below = lax.ppermute(values_up, axis, [(i, (i + 1) % count) for i in range(ends)])
    from_above = lax.ppermute(values_down, axis, [((i + 1) % count, i) for i in range(ends)])
    return from_below, from_above


def across(values, axis):
    return lax.ppermute(values, axis, [(0, 1), (1, 0)])


def gathered(values, axes):
    return lax.all_to_all(values, axes, 0, 0)


def shards(snapshots, basis):
    lat_count = lax.axis_size("lat")
    cells = CELL_ROWS * LANES * lat_count * lax.axis_size(LON)
    q = pltpu.with_memory_space_constraint(basis.reshape(EOFS, CELL_ROWS, LANES), pltpu.HBM)

    packed = call(pack_kernel, [VMEM], shape(CELL_ROWS, LANES))(snapshots)
    west, east = neighbours(packed, packed, LON, True)
    seam, low, high = call(
        seam_kernel, [VMEM] * 4, (shape(CELL_ROWS, LANES), shape(4, 64, LANES), shape(4, 64, LANES))
    )(snapshots, packed, west, east)
    south, north = neighbours(high, low, "lat", False)
    parts = HALF_ROWS // QROWS
    stack, gram = call(
        basis_gram_kernel,
        [VMEM, ANY],
        (shape(3 * EOFS, HALF_CELLS, dtype=BF16), shape(EOFS, EOFS)),
        [pltpu.VMEM((parts, EOFS, QROWS, LANES), F32), pltpu.VMEM((192, 192), F32), pltpu.SemaphoreType.DMA((parts,))],
        traffic=8 << 20,
    )(seam, q)
    keep, send = call(
        smooth_kernel,
        [VMEM] * 5,
        (shape(SNAPS, HALF_ROWS, LANES),) * 2,
        [pltpu.VMEM((SNAPS, CELL_ROWS, LANES), F32)],
    )(snapshots, seam, south, north, gram)
    here = across(send, "tm")
    far = call(
        basis_stack_kernel,
        [VMEM, ANY],
        shape(2 * EOFS, HALF_CELLS, dtype=BF16),
        [pltpu.VMEM((parts, EOFS, QROWS, LANES), F32), pltpu.SemaphoreType.DMA((parts,))],
        traffic=6 << 20,
    )(keep, q)
    cross, square = call(own_gram_kernel, [VMEM] * 2, (shape(192, 24), shape(24, 24)), traffic=4 << 20)(stack, keep)
    side = shape(SIDE, LANES)
    mine, theirs = call(
        snapshot_gram_kernel, [VMEM] * 7, (side, side), [pltpu.VMEM((PAYLOAD, LANES), F32)]
    )(stack, gram, keep, here, cross, square, far)
    group = lax.axis_size(("pair", "tm"))
    spread = call(pair_kernel, [VMEM] * 2, shape(group, SIDE, LANES))(mine, across(theirs, "core"))
    spread = gathered(spread, ("pair", "tm"))
    late = across(keep, "tm")
    spread = call(group_kernel, [VMEM], shape(2 * lat_count, SIDE, LANES))(spread)
    spread = gathered(spread, ("core", "lat"))
    maps, coeffs_t = call(
        functools.partial(factor_kernel, cells), [VMEM], (shape(2 * EOFS, 160, dtype=BF16), shape(SNAPS, EOFS))
    )(spread)
    final_steps = CELL_ROWS // FINAL_ROWS
    new_basis = pl.pallas_call(
        final_kernel,
        out_shape=shape(EOFS, CELL_ROWS, LANES),
        in_specs=[VMEM] * 7,
        out_specs=ANY,
        scratch_shapes=[
            pltpu.VMEM((final_steps, EOFS, FINAL_ROWS, LANES), F32),
            pltpu.SemaphoreType.DMA((final_steps,)),
        ],
        compiler_params=pltpu.CompilerParams(vmem_limit_bytes=8 << 20),
    )(maps, stack, far, keep, here, send, late)
    return (new_basis.reshape(basis.shape), coeffs_t.T)


def solution(mesh):
    pairs = mesh.shape["lon"] // 2
    split = Mesh(mesh.devices.reshape(pairs, 2, *mesh.devices.shape[1:]), LON + tuple(mesh.axis_names[1:]))
    fields = P(None, None, "lat", LON)
    return jax.shard_map(
        shards,
        mesh=split,
        in_specs=(P("tm", None, "lat", LON), fields),
        out_specs=(fields, P(None, "tm")),
        check_vma=False,
    )
```

```python
import functools
import math

import jax
import jax.numpy as jnp
from jax import lax
from jax.experimental import pallas as pl
from jax.experimental.pallas import tpu as pltpu
from jax.sharding import Mesh, PartitionSpec as P


SMOOTH_RATE = 0.1
STEP_SIZE = 0.25
SNAPS = 8
LEVELS = 8
ROWS = 16
LANES = 128
EOFS = 64
CELL_ROWS = LEVELS * ROWS
HALF_ROWS = CELL_ROWS // 2
HALF_CELLS = HALF_ROWS * LANES
CHUNK = 8
PAYLOAD = 32
SIDE = PAYLOAD // 2
QROWS = 16
FINAL_ROWS = 16
LON = ("pair", "core")
F32 = jnp.float32
BF16 = jnp.bfloat16
HIGHEST = lax.Precision.HIGHEST
VMEM = pl.BlockSpec(memory_space=pltpu.VMEM)
ANY = pl.BlockSpec(memory_space=pl.ANY)


def lanes_of(shape):
    return lax.broadcasted_iota(jnp.int32, shape, len(shape) - 1)


def shape(*dims, dtype=F32):
    return jax.ShapeDtypeStruct(dims, dtype)


def call(kernel, inputs, outputs, scratch=(), flops=1000000, traffic=1000000, megabytes=8):
    return pl.pallas_call(
        kernel,
        out_shape=outputs,
        in_specs=inputs,
        out_specs=jax.tree.map(lambda _: VMEM, outputs),
        scratch_shapes=scratch,
        cost_estimate=pl.CostEstimate(flops=flops, bytes_accessed=traffic, transcendentals=0),
        compiler_params=pltpu.CompilerParams(vmem_limit_bytes=megabytes << 20),
    )


def pack_kernel(x_ref, packed_ref):
    lane = lanes_of((ROWS, LANES))
    for snap in range(SNAPS):
        packed = jnp.zeros((ROWS, LANES), F32)
        for level in range(LEVELS):
            turned = pltpu.roll(x_ref[snap, level], 16 * level + 3, 1)
            packed = jnp.where((lane >= 16 * level) & (lane < 16 * level + 6), turned, packed)
        packed_ref[pl.ds(ROWS * snap, ROWS), :] = packed


def seam_kernel(x_ref, packed_ref, west_ref, east_ref, seam_ref, low_ref, high_ref):
    packed = packed_ref[...]
    lane = lanes_of(packed.shape) % 16
    west = jnp.where(lane < 3, west_ref[...] - packed, 0.0)
    east = pltpu.roll(jnp.where((lane >= 3) & (lane < 6), east_ref[...] - packed, 0.0), 8, 1)
    seam_ref[...] = west + east
    for snap in range(SNAPS):
        at = pl.ds(8 * snap, 8)
        low = jnp.swapaxes(x_ref[snap, :, pl.ds(0, 8), :], 0, 1)
        high = jnp.swapaxes(x_ref[snap, :, pl.ds(8, 8), :], 0, 1)
        for row in range(3):
            low_ref[row, at, :] = low[row]
            high_ref[row, at, :] = high[5 + row]
        low_ref[3, at, :] = seam_ref[pl.ds(ROWS * snap, 8), :]
        high_ref[3, at, :] = seam_ref[pl.ds(ROWS * snap + 8, 8), :]


def smooth_kernel(x_ref, seam_ref, south_ref, north_ref, order_ref, keep_ref, send_ref, done):
    lat = lax.axis_index("lat")
    not_first = jnp.where(lat == 0, 0, 1)
    not_last = jnp.where(lat == lax.axis_size("lat") - 1, 0, 1)
    row = lax.broadcasted_iota(jnp.int32, (8, LANES), 0)
    lane = lanes_of((8, LANES))
    inside = jnp.where(row < 4, not_last, not_first) == 1
    zero = jnp.zeros((8, LANES), F32)
    wide_lane = lanes_of((ROWS, LANES))

    def along_rows(field):
        tall = jnp.concatenate(field, axis=0)
        near = pltpu.roll(tall, 1, 0) + pltpu.roll(tall, 23, 0)
        return near[0:8], near[8:16], near[16:24]

    def snapshot(snap, carry):
        edges = jnp.swapaxes(
            jnp.stack(
                [north_ref[i, pl.ds(8 * snap, 8), :] for i in range(3)]
                + [zero, zero]
                + [south_ref[i, pl.ds(8 * snap, 8), :] for i in range(3)]
            ),
            0,
            1,
        )
        fields = [
            (x_ref[snap, level, pl.ds(0, 8), :], x_ref[snap, level, pl.ds(8, 8), :], edges[level])
            for level in range(LEVELS)
        ]
        at = pl.ds(pl.multiple_of(8 * snap, 8), 8)
        seam = (
            seam_ref[pl.ds(pl.multiple_of(ROWS * snap, 8), 8), :],
            seam_ref[pl.ds(pl.multiple_of(ROWS * snap + 8, 8), 8), :],
            jnp.where(row < 4, north_ref[3, at, :], south_ref[3, at, :]),
        )
        for sweep in range(3):
            tiles = 3 if sweep < 2 else 2
            fresh_fields = []
            for level in range(LEVELS):
                here = fields[level]
                rows = along_rows(here)
                fresh = []
                for tile in range(tiles):
                    near = rows[tile] + pltpu.roll(here[tile], 1, 1) + pltpu.roll(here[tile], LANES - 1, 1)
                    if level > 0:
                        near = near + fields[level - 1][tile]
                    if level < LEVELS - 1:
                        near = near + fields[level + 1][tile]
                    value = here[tile] + SMOOTH_RATE * (near - 6.0 * here[tile])
                    fresh.append(jnp.where(inside, value, 0.0) if tile == 2 else value)
                fresh_fields.append(tuple(fresh))
            rows = along_rows(seam)
            fresh = []
            for tile in range(tiles):
                here = seam[tile]
                near = rows[tile] + pltpu.roll(here, 1, 1) + pltpu.roll(here, LANES - 1, 1)
                near = near + jnp.where(lane >= 16, pltpu.roll(here, 16, 1), 0.0)
                near = near + jnp.where(lane < LANES - 16, pltpu.roll(here, LANES - 16, 1), 0.0)
                value = here + SMOOTH_RATE * (near - 6.0 * here)
                fresh.append(jnp.where(inside, value, 0.0) if tile == 2 else value)
            fields, seam = fresh_fields, tuple(fresh)
        tall_seam = jnp.concatenate(seam, axis=0)
        for level in range(LEVELS):
            first = pltpu.roll(tall_seam, (LANES - 16 * level - 3) % LANES, 1)
            last = pltpu.roll(tall_seam, (117 - 16 * level) % LANES, 1)
            value = jnp.concatenate(fields[level], axis=0)
            value = value + jnp.where(wide_lane < 3, first, jnp.where(wide_lane >= LANES - 3, last, 0.0))
            done[snap, pl.ds(ROWS * level, ROWS), :] = value
        return carry

    lax.fori_loop(0, SNAPS, snapshot, 0)
    group = lax.axis_index("tm")
    for snap in range(SNAPS):
        keep_ref[snap] = done[snap, pl.ds(pl.multiple_of(HALF_ROWS * group, 8), HALF_ROWS), :]
        send_ref[snap] = done[snap, pl.ds(pl.multiple_of(HALF_ROWS * (1 - group), 8), HALF_ROWS), :]


def pieces(values, count):
    out = []
    for index in range(count):
        piece = values.astype(BF16)
        out.append(piece)
        if index < count - 1:
            values = values - piece.astype(F32)
    return out


def transposed_product(left, right):
    return lax.dot_general(left, right, (((1,), (1,)), ((), ())), preferred_element_type=F32)


def basis_copies(half, q_ref, blocks, sems):
    copies = [
        pltpu.make_async_copy(
            q_ref.at[:, pl.ds(pl.multiple_of(HALF_ROWS * half + QROWS * part, QROWS), QROWS), :],
            blocks.at[part],
            sems.at[part],
        )
        for part in range(HALF_ROWS // QROWS)
    ]
    for copy in copies:
        copy.start()
    return copies


def split_block(block, part, count, stack_ref):
    for sub in range(QROWS // CHUNK):
        turned = jnp.swapaxes(block[:, pl.ds(CHUNK * sub, CHUNK), :], 0, 1)
        for inner in range(CHUNK):
            at = pl.ds(LANES * (QROWS * part + CHUNK * sub + inner), LANES)
            for index, piece in enumerate(pieces(turned[inner], count)):
                stack_ref[pl.ds(EOFS * index, EOFS), at] = piece


def basis_gram_kernel(order_ref, q_ref, stack_ref, gram_ref, blocks, total, sems):
    copies = basis_copies(lax.axis_index("tm"), q_ref, blocks, sems)
    for part, copy in enumerate(copies):
        copy.wait()
        split_block(blocks.at[part], part, 3, stack_ref)
        stack = stack_ref[:, pl.ds(QROWS * LANES * part, QROWS * LANES)]
        product = transposed_product(stack, stack)
        total[...] = product if part == 0 else total[...] + product
    down = total[pl.ds(0, 64), :] + total[pl.ds(64, 64), :] + total[pl.ds(128, 64), :]
    gram_ref[...] = down[:, 0:64] + down[:, 64:128] + down[:, 128:192]


def basis_stack_kernel(order_ref, q_ref, stack_ref, blocks, sems):
    copies = basis_copies(1 - lax.axis_index("tm"), q_ref, blocks, sems)
    for part, copy in enumerate(copies):
        copy.wait()
        split_block(blocks.at[part], part, 2, stack_ref)


def snapshot_columns(ref, start, count):
    turned = jnp.swapaxes(ref[:, pl.ds(start, CHUNK), :], 0, 1)
    return [pieces(turned[i], count) for i in range(CHUNK)]


def in_order(mine, other):
    first = lax.axis_index("tm") == 0
    return jnp.where(first, mine, other), jnp.where(first, other, mine)


def own_gram_kernel(stack_ref, mine_ref, cross_ref, square_ref, pieces_ref):
    def block(step, carry):
        cross, square = carry
        columns = snapshot_columns(mine_ref, pl.multiple_of(CHUNK * step, CHUNK), 3)
        columns = jnp.concatenate([jnp.concatenate(c, axis=0) for c in columns], axis=1)
        width = CHUNK * LANES
        at = pl.ds(pl.multiple_of(width * step, width), width)
        pieces_ref[:, at] = columns
        return cross + transposed_product(stack_ref[:, at], columns), square + transposed_product(columns, columns)

    zeros = (jnp.zeros((192, 24), F32), jnp.zeros((24, 24), F32))
    cross_ref[...], square_ref[...] = lax.fori_loop(0, HALF_ROWS // CHUNK, block, zeros)


def folded(sums, rows):
    down = sums[0:rows] + sums[rows : 2 * rows] + sums[2 * rows : 3 * rows]
    return down[:, 0:8] + down[:, 8:16] + down[:, 16:24]


def snapshot_gram_kernel(
    stack_ref, gram_ref, pieces_ref, other_ref, cross_ref, square_ref, order_ref, own_ref, partner_ref, joined
):
    def block(step, carry):
        cross, square, mixed = carry
        start = pl.multiple_of(CHUNK * step, CHUNK)
        other = snapshot_columns(other_ref, start, 3)
        other = jnp.concatenate([jnp.concatenate(c, axis=0) for c in other], axis=1)
        width = CHUNK * LANES
        at = pl.ds(pl.multiple_of(width * step, width), width)
        return (
            cross + transposed_product(stack_ref[:, at], other),
            square + transposed_product(other, other),
            mixed + transposed_product(pieces_ref[:, at], other),
        )

    zeros = (jnp.zeros((192, 24), F32), jnp.zeros((24, 24), F32), jnp.zeros((24, 24), F32))
    cross, square, mixed = lax.fori_loop(0, HALF_ROWS // CHUNK, block, zeros)
    mixed = folded(mixed, 8)
    projection = jnp.concatenate(in_order(folded(cross_ref[...], 64), folded(cross, 64)), axis=1)
    early, late = in_order(folded(square_ref[...], 8), folded(square, 8))
    upper, _ = in_order(mixed, jnp.transpose(mixed))
    square = jnp.concatenate(
        [jnp.concatenate([early, upper], axis=1), jnp.concatenate([jnp.transpose(upper), late], axis=1)], axis=0
    )
    gram = gram_ref[...]
    low, high = gram[0:32, 0:32], gram[32:64, 32:64]
    row = lax.broadcasted_iota(jnp.int32, (32, 32), 0)
    column = lax.broadcasted_iota(jnp.int32, (32, 32), 1)
    diagonal = jnp.sum(jnp.where(row == column, high, 0.0), axis=0, keepdims=True)
    both = jnp.where(row >= column, low, high)
    below = jnp.concatenate(
        [square, jnp.zeros((16, 16), F32), jnp.broadcast_to(diagonal, (16, 32))], axis=1
    )
    right = jnp.concatenate([jnp.transpose(projection), below], axis=0)
    joined[...] = jnp.concatenate([both, gram[32:64, 0:32], right], axis=1)
    core = lax.axis_index("core")
    own_ref[...] = joined[pl.ds(pl.multiple_of(SIDE * core, 8), SIDE), :]
    partner_ref[...] = joined[pl.ds(pl.multiple_of(SIDE * (1 - core), 8), SIDE), :]


def pair_kernel(one_ref, two_ref, out_ref):
    out_ref[...] = jnp.broadcast_to((one_ref[...] + two_ref[...])[None], out_ref.shape)


def group_kernel(parts_ref, out_ref):
    out_ref[...] = jnp.broadcast_to(jnp.sum(parts_ref[...], axis=0)[None], out_ref.shape)


def factor_kernel(cells, parts_ref, maps_ref, coeffs_ref):
    count = parts_ref.shape[0] // 2
    totals = jnp.concatenate(
        [jnp.sum(parts_ref[pl.ds(count * core, count)], axis=0) for core in range(2)], axis=0
    )
    row = lax.broadcasted_iota(jnp.int32, (EOFS, EOFS), 0)
    column = lax.broadcasted_iota(jnp.int32, (EOFS, EOFS), 1)
    both = totals[:, 0:32]
    once = jnp.concatenate(
        [jnp.concatenate([both, jnp.zeros((32, 32), F32)], axis=1), jnp.concatenate([totals[:, 32:64], both], axis=1)], axis=0
    )
    once = jnp.where(((row < 32) & (row > column)) | ((row >= 32) & ((column < 32) | (row < column))), once, 0.0)
    corner = jnp.concatenate([both, jnp.zeros((32, 32), F32)], axis=1)
    diagonal = jnp.concatenate([corner, jnp.broadcast_to(totals[16:17, 64:128], (32, EOFS))], axis=0)
    basis_gram = once + jnp.transpose(once) + jnp.where(row == column, diagonal, 0.0)
    root = math.sqrt(cells)
    coeffs_t = totals[0:16, 64:128] * (1.0 / root)
    snap_gram = totals[16:32, 64:80]
    coeffs_ref[...] = jnp.where(lax.axis_index("tm") == 0, coeffs_t[0:8, :], coeffs_t[8:16, :])
    mixed = (2.0 * STEP_SIZE * root) * coeffs_t + (STEP_SIZE * STEP_SIZE) * jnp.dot(
        snap_gram, coeffs_t, precision=HIGHEST, preferred_element_type=F32
    )
    grown = lax.dot_general(
        coeffs_t, mixed, (((0,), (0,)), ((), ())), precision=HIGHEST, preferred_element_type=F32
    )
    gram = (basis_gram + grown) * (1.0 / cells)
    rows = lax.broadcasted_iota(jnp.int32, (EOFS, EOFS), 0)
    columns = lax.broadcasted_iota(jnp.int32, (EOFS, EOFS), 1)
    work = jnp.concatenate([gram, (rows == columns).astype(F32)], axis=1)
    blocks = [work[8 * i : 8 * i + 8, :] for i in range(8)]
    results = []
    for panel in range(8):
        lower = blocks[panel:]
        columns = [
            [jnp.broadcast_to(b[:, 8 * panel + k : 8 * panel + k + 1], (8, LANES)) for b in lower] for k in range(8)
        ]
        rows = [lower[0][k : k + 1, :] for k in range(8)]
        for k in range(8):
            pivot = columns[k][0][k : k + 1, :]
            inverse = 1.0 / pivot
            factors = [c * inverse for c in columns[k]]
            for m in range(k + 1, 8):
                entry = columns[m][0][k : k + 1, :]
                columns[m] = [c - f * entry for c, f in zip(columns[m], factors)]
                rows[m] = rows[m] - factors[0][m : m + 1, :] * rows[k]
            for i in range(panel + 1, 8):
                blocks[i] = blocks[i] - factors[i - panel] * rows[k]
            results.append(rows[k] * lax.rsqrt(pivot))
    inverse = jnp.concatenate(results, axis=0)[:, EOFS:]
    update = lax.dot_general(
        inverse, coeffs_t, (((1,), (1,)), ((), ())), precision=HIGHEST, preferred_element_type=F32
    )
    rows = [
        jnp.concatenate([inverse_part, inverse_part, update_part, update_part], axis=1)
        for inverse_part, update_part in zip(pieces(inverse, 2), pieces(STEP_SIZE * update, 2))
    ]
    maps_ref[...] = jnp.concatenate(rows, axis=0)


def final_kernel(maps_ref, near_ref, far_ref, keep_ref, here_ref, send_ref, late_ref, out_ref, blocks, sems):
    group = lax.axis_index("tm")
    steps = HALF_ROWS // FINAL_ROWS
    copies = []
    for step in range(2 * steps):
        near = step < steps
        half = group if near else 1 - group
        local = step % steps
        stack_ref, mine_ref, other_ref = (near_ref, keep_ref, here_ref) if near else (far_ref, send_ref, late_ref)
        for sub in range(FINAL_ROWS // CHUNK):
            start = local * FINAL_ROWS + CHUNK * sub
            at = pl.ds(start, CHUNK)
            early, late = in_order(
                jnp.swapaxes(mine_ref[:, at, :], 0, 1), jnp.swapaxes(other_ref[:, at, :], 0, 1)
            )
            columns = jnp.concatenate(
                [
                    jnp.concatenate(pieces(jnp.concatenate([early[i], late[i]], axis=0), 2), axis=0)
                    for i in range(CHUNK)
                ],
                axis=1,
            )
            stack = stack_ref[pl.ds(0, 2 * EOFS), pl.ds(start * LANES, CHUNK * LANES)]
            both = jnp.dot(maps_ref[...], jnp.concatenate([stack, columns], axis=0), preferred_element_type=F32)
            result = both[0:EOFS, :] + both[EOFS:, :]
            result = jnp.stack([result[:, LANES * i : LANES * (i + 1)] for i in range(CHUNK)])
            blocks[step, :, pl.ds(CHUNK * sub, CHUNK), :] = jnp.swapaxes(result, 0, 1)
        to = pl.ds(pl.multiple_of(HALF_ROWS * half + FINAL_ROWS * local, FINAL_ROWS), FINAL_ROWS)
        copy = pltpu.make_async_copy(blocks.at[step], out_ref.at[:, to, :], sems.at[step])
        copy.start()
        copies.append(copy)
    for copy in copies:
        copy.wait()


def neighbours(values_up, values_down, axis, closed):
    count = lax.axis_size(axis)
    ends = count if closed else count - 1
    from_below = lax.ppermute(values_up, axis, [(i, (i + 1) % count) for i in range(ends)])
    from_above = lax.ppermute(values_down, axis, [((i + 1) % count, i) for i in range(ends)])
    return from_below, from_above


def across(values, axis):
    return lax.ppermute(values, axis, [(0, 1), (1, 0)])


def gathered(values, axes):
    return lax.all_to_all(values, axes, 0, 0)


def update(snapshots, basis):
    lat_count = lax.axis_size("lat")
    cells = CELL_ROWS * LANES * lat_count * lax.axis_size(LON)
    q = pltpu.with_memory_space_constraint(basis.reshape(EOFS, CELL_ROWS, LANES), pltpu.HBM)

    packed = call(pack_kernel, [VMEM], shape(CELL_ROWS, LANES))(snapshots)
    west, east = neighbours(packed, packed, LON, True)
    seam, low, high = call(
        seam_kernel, [VMEM] * 4, (shape(CELL_ROWS, LANES), shape(4, 64, LANES), shape(4, 64, LANES))
    )(snapshots, packed, west, east)
    south, north = neighbours(high, low, "lat", False)
    parts = HALF_ROWS // QROWS
    stack, gram = call(
        basis_gram_kernel,
        [VMEM, ANY],
        (shape(3 * EOFS, HALF_CELLS, dtype=BF16), shape(EOFS, EOFS)),
        [pltpu.VMEM((parts, EOFS, QROWS, LANES), F32), pltpu.VMEM((192, 192), F32), pltpu.SemaphoreType.DMA((parts,))],
        traffic=8 << 20,
    )(seam, q)
    keep, send = call(
        smooth_kernel,
        [VMEM] * 5,
        (shape(SNAPS, HALF_ROWS, LANES),) * 2,
        [pltpu.VMEM((SNAPS, CELL_ROWS, LANES), F32)],
    )(snapshots, seam, south, north, gram)
    here = across(send, "tm")
    far = call(
        basis_stack_kernel,
        [VMEM, ANY],
        shape(2 * EOFS, HALF_CELLS, dtype=BF16),
        [pltpu.VMEM((parts, EOFS, QROWS, LANES), F32), pltpu.SemaphoreType.DMA((parts,))],
        traffic=6 << 20,
    )(keep, q)
    cross, square, split = call(
        own_gram_kernel,
        [VMEM] * 2,
        (shape(192, 24), shape(24, 24), shape(24, HALF_CELLS, dtype=BF16)),
        traffic=4 << 20,
    )(stack, keep)
    side = shape(SIDE, LANES)
    late = across(keep, "tm")
    mine, theirs = call(
        snapshot_gram_kernel, [VMEM] * 7, (side, side), [pltpu.VMEM((PAYLOAD, LANES), F32)]
    )(stack, gram, split, here, cross, square, far)
    group = lax.axis_size(("pair", "tm"))
    spread = call(pair_kernel, [VMEM] * 2, shape(group, SIDE, LANES))(mine, across(theirs, "core"))
    spread = gathered(spread, ("pair", "tm"))
    spread = call(group_kernel, [VMEM], shape(2 * lat_count, SIDE, LANES))(spread)
    spread = gathered(spread, ("core", "lat"))
    maps, coeffs_t = call(
        functools.partial(factor_kernel, cells), [VMEM], (shape(2 * EOFS, 160, dtype=BF16), shape(SNAPS, EOFS))
    )(spread)
    final_steps = CELL_ROWS // FINAL_ROWS
    new_basis = pl.pallas_call(
        final_kernel,
        out_shape=shape(EOFS, CELL_ROWS, LANES),
        in_specs=[VMEM] * 7,
        out_specs=ANY,
        scratch_shapes=[
            pltpu.VMEM((final_steps, EOFS, FINAL_ROWS, LANES), F32),
            pltpu.SemaphoreType.DMA((final_steps,)),
        ],
        compiler_params=pltpu.CompilerParams(vmem_limit_bytes=8 << 20),
    )(maps, stack, far, keep, here, send, late)
    return (new_basis.reshape(basis.shape), coeffs_t.T)


def solution(mesh):
    pairs = mesh.shape["lon"] // 2
    split = Mesh(mesh.devices.reshape(pairs, 2, *mesh.devices.shape[1:]), LON + tuple(mesh.axis_names[1:]))
    fields = P(None, None, "lat", LON)
    return jax.shard_map(
        update,
        mesh=split,
        in_specs=(P("tm", None, "lat", LON), fields),
        out_specs=(fields, P(None, "tm")),
        check_vma=False,
    )
```

```python
import functools
import math

import jax
import jax.numpy as jnp
from jax import lax
from jax.experimental import pallas as pl
from jax.experimental.pallas import tpu as pltpu
from jax.sharding import Mesh, PartitionSpec as P


SMOOTH_RATE = 0.1
STEP_SIZE = 0.25
SNAPS = 8
LEVELS = 8
ROWS = 16
LANES = 128
EOFS = 64
CELL_ROWS = LEVELS * ROWS
HALF_ROWS = CELL_ROWS // 2
HALF_CELLS = HALF_ROWS * LANES
CHUNK = 8
PAYLOAD = 32
SIDE = PAYLOAD // 2
QROWS = 16
FINAL_ROWS = 16
LON = ("pair", "core")
F32 = jnp.float32
BF16 = jnp.bfloat16
HIGHEST = lax.Precision.HIGHEST
VMEM = pl.BlockSpec(memory_space=pltpu.VMEM)
ANY = pl.BlockSpec(memory_space=pl.ANY)


def lanes_of(shape):
    return lax.broadcasted_iota(jnp.int32, shape, len(shape) - 1)


def shape(*dims, dtype=F32):
    return jax.ShapeDtypeStruct(dims, dtype)


def call(kernel, inputs, outputs, scratch=(), flops=1000000, traffic=1000000, megabytes=8):
    return pl.pallas_call(
        kernel,
        out_shape=outputs,
        in_specs=inputs,
        out_specs=jax.tree.map(lambda _: VMEM, outputs),
        scratch_shapes=scratch,
        cost_estimate=pl.CostEstimate(flops=flops, bytes_accessed=traffic, transcendentals=0),
        compiler_params=pltpu.CompilerParams(vmem_limit_bytes=megabytes << 20),
    )


def pack_kernel(x_ref, packed_ref):
    lane = lanes_of((ROWS, LANES))
    for snap in range(SNAPS):
        packed = jnp.zeros((ROWS, LANES), F32)
        for level in range(LEVELS):
            turned = pltpu.roll(x_ref[snap, level], 16 * level + 3, 1)
            packed = jnp.where((lane >= 16 * level) & (lane < 16 * level + 6), turned, packed)
        packed_ref[pl.ds(ROWS * snap, ROWS), :] = packed


def seam_kernel(x_ref, packed_ref, across_ref, beside_ref, seam_ref, one_ref, two_ref):
    packed = packed_ref[...]
    lane = lanes_of(packed.shape) % 16
    eastern = lax.axis_index("core") == 1
    far, near = across_ref[...] - packed, beside_ref[...] - packed
    west = jnp.where(lane < 3, jnp.where(eastern, near, far), 0.0)
    east = pltpu.roll(jnp.where((lane >= 3) & (lane < 6), jnp.where(eastern, far, near), 0.0), 8, 1)
    seam_ref[...] = west + east
    even = lax.axis_index("lat") % 2 == 0
    for snap in range(SNAPS):
        at = pl.ds(8 * snap, 8)
        low = jnp.swapaxes(x_ref[snap, :, pl.ds(0, 8), :], 0, 1)
        high = jnp.swapaxes(x_ref[snap, :, pl.ds(8, 8), :], 0, 1)
        rows = [(low[row], high[5 + row]) for row in range(3)]
        rows.append((seam_ref[pl.ds(ROWS * snap, 8), :], seam_ref[pl.ds(ROWS * snap + 8, 8), :]))
        for row, (low, high) in enumerate(rows):
            one_ref[row, at, :] = jnp.where(even, high, low)
            two_ref[row, at, :] = jnp.where(even, low, high)


def smooth_kernel(x_ref, seam_ref, one_ref, two_ref, order_ref, keep_ref, send_ref, done):
    lat = lax.axis_index("lat")
    even = lat % 2 == 0
    not_first = jnp.where(lat == 0, 0, 1)
    not_last = jnp.where(lat == lax.axis_size("lat") - 1, 0, 1)
    row = lax.broadcasted_iota(jnp.int32, (8, LANES), 0)
    lane = lanes_of((8, LANES))
    inside = jnp.where(row < 4, not_last, not_first) == 1
    zero = jnp.zeros((8, LANES), F32)
    wide_lane = lanes_of((ROWS, LANES))

    def along_rows(field):
        tall = jnp.concatenate(field, axis=0)
        near = pltpu.roll(tall, 1, 0) + pltpu.roll(tall, 23, 0)
        return near[0:8], near[8:16], near[16:24]

    def snapshot(snap, carry):
        at = pl.ds(pl.multiple_of(8 * snap, 8), 8)
        edges = jnp.swapaxes(
            jnp.stack(
                [jnp.where(even, one_ref[i, at, :], two_ref[i, at, :]) for i in range(3)]
                + [zero, zero]
                + [jnp.where(even, two_ref[i, at, :], one_ref[i, at, :]) for i in range(3)]
            ),
            0,
            1,
        )
        fields = [
            (x_ref[snap, level, pl.ds(0, 8), :], x_ref[snap, level, pl.ds(8, 8), :], edges[level])
            for level in range(LEVELS)
        ]
        seam = (
            seam_ref[pl.ds(pl.multiple_of(ROWS * snap, 8), 8), :],
            seam_ref[pl.ds(pl.multiple_of(ROWS * snap + 8, 8), 8), :],
            jnp.where((row < 4) == even, one_ref[3, at, :], two_ref[3, at, :]),
        )
        for sweep in range(3):
            tiles = 3 if sweep < 2 else 2
            fresh_fields = []
            for level in range(LEVELS):
                here = fields[level]
                rows = along_rows(here)
                fresh = []
                for tile in range(tiles):
                    near = rows[tile] + pltpu.roll(here[tile], 1, 1) + pltpu.roll(here[tile], LANES - 1, 1)
                    if level > 0:
                        near = near + fields[level - 1][tile]
                    if level < LEVELS - 1:
                        near = near + fields[level + 1][tile]
                    value = here[tile] + SMOOTH_RATE * (near - 6.0 * here[tile])
                    fresh.append(jnp.where(inside, value, 0.0) if tile == 2 else value)
                fresh_fields.append(tuple(fresh))
            rows = along_rows(seam)
            fresh = []
            for tile in range(tiles):
                here = seam[tile]
                near = rows[tile] + pltpu.roll(here, 1, 1) + pltpu.roll(here, LANES - 1, 1)
                near = near + jnp.where(lane >= 16, pltpu.roll(here, 16, 1), 0.0)
                near = near + jnp.where(lane < LANES - 16, pltpu.roll(here, LANES - 16, 1), 0.0)
                value = here + SMOOTH_RATE * (near - 6.0 * here)
                fresh.append(jnp.where(inside, value, 0.0) if tile == 2 else value)
            fields, seam = fresh_fields, tuple(fresh)
        tall_seam = jnp.concatenate(seam, axis=0)
        for level in range(LEVELS):
            first = pltpu.roll(tall_seam, (LANES - 16 * level - 3) % LANES, 1)
            last = pltpu.roll(tall_seam, (117 - 16 * level) % LANES, 1)
            value = jnp.concatenate(fields[level], axis=0)
            value = value + jnp.where(wide_lane < 3, first, jnp.where(wide_lane >= LANES - 3, last, 0.0))
            done[snap, pl.ds(ROWS * level, ROWS), :] = value
        return carry

    lax.fori_loop(0, SNAPS, snapshot, 0)
    group = lax.axis_index("tm")
    for snap in range(SNAPS):
        keep_ref[snap] = done[snap, pl.ds(pl.multiple_of(HALF_ROWS * group, 8), HALF_ROWS), :]
        send_ref[snap] = done[snap, pl.ds(pl.multiple_of(HALF_ROWS * (1 - group), 8), HALF_ROWS), :]


def pieces(values, count):
    out = []
    for index in range(count):
        piece = values.astype(BF16)
        out.append(piece)
        if index < count - 1:
            values = values - piece.astype(F32)
    return out


def transposed_product(left, right):
    return lax.dot_general(left, right, (((1,), (1,)), ((), ())), preferred_element_type=F32)


def basis_copies(half, q_ref, blocks, sems):
    copies = [
        pltpu.make_async_copy(
            q_ref.at[:, pl.ds(pl.multiple_of(HALF_ROWS * half + QROWS * part, QROWS), QROWS), :],
            blocks.at[part],
            sems.at[part],
        )
        for part in range(HALF_ROWS // QROWS)
    ]
    for copy in copies:
        copy.start()
    return copies


def split_block(block, part, count, stack_ref):
    for sub in range(QROWS // CHUNK):
        turned = jnp.swapaxes(block[:, pl.ds(CHUNK * sub, CHUNK), :], 0, 1)
        for inner in range(CHUNK):
            at = pl.ds(LANES * (QROWS * part + CHUNK * sub + inner), LANES)
            for index, piece in enumerate(pieces(turned[inner], count)):
                stack_ref[pl.ds(EOFS * index, EOFS), at] = piece


def basis_gram_kernel(order_ref, q_ref, stack_ref, gram_ref, blocks, total, sems):
    copies = basis_copies(lax.axis_index("tm"), q_ref, blocks, sems)
    for part, copy in enumerate(copies):
        copy.wait()
        split_block(blocks.at[part], part, 3, stack_ref)
        stack = stack_ref[:, pl.ds(QROWS * LANES * part, QROWS * LANES)]
        product = transposed_product(stack, stack)
        total[...] = product if part == 0 else total[...] + product
    down = total[pl.ds(0, 64), :] + total[pl.ds(64, 64), :] + total[pl.ds(128, 64), :]
    gram_ref[...] = down[:, 0:64] + down[:, 64:128] + down[:, 128:192]


def basis_stack_kernel(order_ref, q_ref, stack_ref, blocks, sems):
    copies = basis_copies(1 - lax.axis_index("tm"), q_ref, blocks, sems)
    for part, copy in enumerate(copies):
        copy.wait()
        split_block(blocks.at[part], part, 2, stack_ref)


def snapshot_columns(ref, start, count):
    turned = jnp.swapaxes(ref[:, pl.ds(start, CHUNK), :], 0, 1)
    return [pieces(turned[i], count) for i in range(CHUNK)]


def in_order(mine, other):
    first = lax.axis_index("tm") == 0
    return jnp.where(first, mine, other), jnp.where(first, other, mine)


def own_gram_kernel(stack_ref, mine_ref, cross_ref, square_ref, pieces_ref):
    def block(step, carry):
        cross, square = carry
        columns = snapshot_columns(mine_ref, pl.multiple_of(CHUNK * step, CHUNK), 3)
        columns = jnp.concatenate([jnp.concatenate(c, axis=0) for c in columns], axis=1)
        width = CHUNK * LANES
        at = pl.ds(pl.multiple_of(width * step, width), width)
        pieces_ref[:, at] = columns
        return cross + transposed_product(stack_ref[:, at], columns), square + transposed_product(columns, columns)

    zeros = (jnp.zeros((192, 24), F32), jnp.zeros((24, 24), F32))
    cross_ref[...], square_ref[...] = lax.fori_loop(0, HALF_ROWS // CHUNK, block, zeros)


def folded(sums, rows):
    down = sums[0:rows] + sums[rows : 2 * rows] + sums[2 * rows : 3 * rows]
    return down[:, 0:8] + down[:, 8:16] + down[:, 16:24]


def snapshot_gram_kernel(
    stack_ref, gram_ref, pieces_ref, other_ref, cross_ref, square_ref, order_ref, own_ref, partner_ref, columns, joined
):
    for step in range(HALF_ROWS // CHUNK):
        other = snapshot_columns(other_ref, CHUNK * step, 3)
        columns[:, pl.ds(CHUNK * LANES * step, CHUNK * LANES)] = jnp.concatenate(
            [jnp.concatenate(c, axis=0) for c in other], axis=1
        )
    cross = transposed_product(stack_ref[...], columns[...])
    square = transposed_product(columns[...], columns[...])
    mixed = transposed_product(pieces_ref[...], columns[...])
    mixed = folded(mixed, 8)
    projection = jnp.concatenate(in_order(folded(cross_ref[...], 64), folded(cross, 64)), axis=1)
    early, late = in_order(folded(square_ref[...], 8), folded(square, 8))
    upper, _ = in_order(mixed, jnp.transpose(mixed))
    square = jnp.concatenate(
        [jnp.concatenate([early, upper], axis=1), jnp.concatenate([jnp.transpose(upper), late], axis=1)], axis=0
    )
    gram = gram_ref[...]
    low, high = gram[0:32, 0:32], gram[32:64, 32:64]
    row = lax.broadcasted_iota(jnp.int32, (32, 32), 0)
    column = lax.broadcasted_iota(jnp.int32, (32, 32), 1)
    diagonal = jnp.sum(jnp.where(row == column, high, 0.0), axis=0, keepdims=True)
    both = jnp.where(row >= column, low, high)
    below = jnp.concatenate(
        [square, jnp.zeros((16, 16), F32), jnp.broadcast_to(diagonal, (16, 32))], axis=1
    )
    right = jnp.concatenate([jnp.transpose(projection), below], axis=0)
    joined[...] = jnp.concatenate([both, gram[32:64, 0:32], right], axis=1)
    core = lax.axis_index("core")
    own_ref[...] = joined[pl.ds(pl.multiple_of(SIDE * core, 8), SIDE), :]
    partner_ref[...] = joined[pl.ds(pl.multiple_of(SIDE * (1 - core), 8), SIDE), :]


def pair_kernel(one_ref, two_ref, out_ref):
    out_ref[...] = jnp.broadcast_to((one_ref[...] + two_ref[...])[None], out_ref.shape)


def group_kernel(parts_ref, out_ref):
    out_ref[...] = jnp.broadcast_to(jnp.sum(parts_ref[...], axis=0)[None], out_ref.shape)


def factor_kernel(cells, parts_ref, maps_ref, coeffs_ref):
    count = parts_ref.shape[0] // 2
    totals = jnp.concatenate(
        [jnp.sum(parts_ref[pl.ds(count * core, count)], axis=0) for core in range(2)], axis=0
    )
    row = lax.broadcasted_iota(jnp.int32, (EOFS, EOFS), 0)
    column = lax.broadcasted_iota(jnp.int32, (EOFS, EOFS), 1)
    both = totals[:, 0:32]
    once = jnp.concatenate(
        [jnp.concatenate([both, jnp.zeros((32, 32), F32)], axis=1), jnp.concatenate([totals[:, 32:64], both], axis=1)], axis=0
    )
    once = jnp.where(((row < 32) & (row > column)) | ((row >= 32) & ((column < 32) | (row < column))), once, 0.0)
    corner = jnp.concatenate([both, jnp.zeros((32, 32), F32)], axis=1)
    diagonal = jnp.concatenate([corner, jnp.broadcast_to(totals[16:17, 64:128], (32, EOFS))], axis=0)
    basis_gram = once + jnp.transpose(once) + jnp.where(row == column, diagonal, 0.0)
    root = math.sqrt(cells)
    coeffs_t = totals[0:16, 64:128] * (1.0 / root)
    snap_gram = totals[16:32, 64:80]
    coeffs_ref[...] = jnp.where(lax.axis_index("tm") == 0, coeffs_t[0:8, :], coeffs_t[8:16, :])
    mixed = (2.0 * STEP_SIZE * root) * coeffs_t + (STEP_SIZE * STEP_SIZE) * jnp.dot(
        snap_gram, coeffs_t, precision=HIGHEST, preferred_element_type=F32
    )
    grown = lax.dot_general(
        coeffs_t, mixed, (((0,), (0,)), ((), ())), precision=HIGHEST, preferred_element_type=F32
    )
    gram = (basis_gram + grown) * (1.0 / cells)
    rows = lax.broadcasted_iota(jnp.int32, (EOFS, EOFS), 0)
    columns = lax.broadcasted_iota(jnp.int32, (EOFS, EOFS), 1)
    work = jnp.concatenate([gram, (rows == columns).astype(F32)], axis=1)
    blocks = [work[8 * i : 8 * i + 8, :] for i in range(8)]
    results = []
    for panel in range(8):
        lower = blocks[panel:]
        columns = [
            [jnp.broadcast_to(b[:, 8 * panel + k : 8 * panel + k + 1], (8, LANES)) for b in lower] for k in range(8)
        ]
        rows = [lower[0][k : k + 1, :] for k in range(8)]
        for k in range(8):
            pivot = columns[k][0][k : k + 1, :]
            if k % 2 == 0:
                corner, upper, side = columns[k + 1][0][k + 1 : k + 2, :], columns[k + 1][0][k : k + 1, :], columns[k][0][k + 1 : k + 2, :]
                inverse = 1.0 / pivot
                following = pivot * (1.0 / (pivot * corner - upper * side))
            else:
                inverse = following
            factors = [c * inverse for c in columns[k]]
            for m in range(k + 1, 8):
                entry = columns[m][0][k : k + 1, :]
                columns[m] = [c - f * entry for c, f in zip(columns[m], factors)]
                rows[m] = rows[m] - factors[0][m : m + 1, :] * rows[k]
            for i in range(panel + 1, 8):
                blocks[i] = blocks[i] - factors[i - panel] * rows[k]
            results.append(rows[k] * lax.rsqrt(pivot))
    inverse = jnp.concatenate(results, axis=0)[:, EOFS:]
    update = lax.dot_general(
        inverse, coeffs_t, (((1,), (1,)), ((), ())), precision=HIGHEST, preferred_element_type=F32
    )
    rows = [
        jnp.concatenate([inverse_part, inverse_part, update_part, update_part], axis=1)
        for inverse_part, update_part in zip(pieces(inverse, 2), pieces(STEP_SIZE * update, 2))
    ]
    maps_ref[...] = jnp.concatenate(rows, axis=0)


def final_kernel(maps_ref, near_ref, far_ref, keep_ref, here_ref, send_ref, late_ref, out_ref, blocks, sems):
    group = lax.axis_index("tm")
    steps = HALF_ROWS // FINAL_ROWS
    copies = []
    for step in range(2 * steps):
        near = step < steps
        half = group if near else 1 - group
        local = step % steps
        stack_ref, mine_ref, other_ref = (near_ref, keep_ref, here_ref) if near else (far_ref, send_ref, late_ref)
        for sub in range(FINAL_ROWS // CHUNK):
            start = local * FINAL_ROWS + CHUNK * sub
            at = pl.ds(start, CHUNK)
            early, late = in_order(
                jnp.swapaxes(mine_ref[:, at, :], 0, 1), jnp.swapaxes(other_ref[:, at, :], 0, 1)
            )
            columns = jnp.concatenate(
                [
                    jnp.concatenate(pieces(jnp.concatenate([early[i], late[i]], axis=0), 2), axis=0)
                    for i in range(CHUNK)
                ],
                axis=1,
            )
            stack = stack_ref[pl.ds(0, 2 * EOFS), pl.ds(start * LANES, CHUNK * LANES)]
            both = jnp.dot(maps_ref[...], jnp.concatenate([stack, columns], axis=0), preferred_element_type=F32)
            result = both[0:EOFS, :] + both[EOFS:, :]
            result = jnp.stack([result[:, LANES * i : LANES * (i + 1)] for i in range(CHUNK)])
            blocks[step, :, pl.ds(CHUNK * sub, CHUNK), :] = jnp.swapaxes(result, 0, 1)
        to = pl.ds(pl.multiple_of(HALF_ROWS * half + FINAL_ROWS * local, FINAL_ROWS), FINAL_ROWS)
        copy = pltpu.make_async_copy(blocks.at[step], out_ref.at[:, to, :], sems.at[step])
        copy.start()
        copies.append(copy)
    for copy in copies:
        copy.wait()


def swapped(values, axis, first):
    count = lax.axis_size(axis)
    pairs = [(i, (i + 1) % count) for i in range(first, count - first % 2 * (axis == "lat"), 2)]
    return lax.ppermute(values, axis, [p for one, two in pairs for p in ((one, two), (two, one))])


def across(values, axis):
    return lax.ppermute(values, axis, [(0, 1), (1, 0)])


def gathered(values, axes):
    return lax.all_to_all(values, axes, 0, 0)


def update(snapshots, basis):
    lat_count = lax.axis_size("lat")
    cells = CELL_ROWS * LANES * lat_count * lax.axis_size(LON)
    q = pltpu.with_memory_space_constraint(basis.reshape(EOFS, CELL_ROWS, LANES), pltpu.HBM)

    packed = call(pack_kernel, [VMEM], shape(CELL_ROWS, LANES))(snapshots)
    chip = swapped(packed, LON, 1)
    beside = across(packed, "core")
    seam, one, two = call(
        seam_kernel, [VMEM] * 4, (shape(CELL_ROWS, LANES), shape(4, 64, LANES), shape(4, 64, LANES))
    )(snapshots, packed, chip, beside)
    one, two = swapped(one, "lat", 0), swapped(two, "lat", 1)
    parts = HALF_ROWS // QROWS
    stack, gram = call(
        basis_gram_kernel,
        [VMEM, ANY],
        (shape(3 * EOFS, HALF_CELLS, dtype=BF16), shape(EOFS, EOFS)),
        [pltpu.VMEM((parts, EOFS, QROWS, LANES), F32), pltpu.VMEM((192, 192), F32), pltpu.SemaphoreType.DMA((parts,))],
        traffic=8 << 20,
    )(seam, q)
    keep, send = call(
        smooth_kernel,
        [VMEM] * 5,
        (shape(SNAPS, HALF_ROWS, LANES),) * 2,
        [pltpu.VMEM((SNAPS, CELL_ROWS, LANES), F32)],
    )(snapshots, seam, one, two, gram)
    here = across(send, "tm")
    far = call(
        basis_stack_kernel,
        [VMEM, ANY],
        shape(2 * EOFS, HALF_CELLS, dtype=BF16),
        [pltpu.VMEM((parts, EOFS, QROWS, LANES), F32), pltpu.SemaphoreType.DMA((parts,))],
        traffic=6 << 20,
    )(keep, q)
    cross, square, split = call(
        own_gram_kernel,
        [VMEM] * 2,
        (shape(192, 24), shape(24, 24), shape(24, HALF_CELLS, dtype=BF16)),
        traffic=4 << 20,
    )(stack, keep)
    side = shape(SIDE, LANES)
    late = across(keep, "tm")
    mine, theirs = call(
        snapshot_gram_kernel, [VMEM] * 7, (side, side), [pltpu.VMEM((24, HALF_CELLS), BF16), pltpu.VMEM((PAYLOAD, LANES), F32)]
    )(stack, gram, split, here, cross, square, far)
    group = lax.axis_size(("pair", "tm"))
    spread = call(pair_kernel, [VMEM] * 2, shape(group, SIDE, LANES))(mine, across(theirs, "core"))
    spread = gathered(spread, ("pair", "tm"))
    spread = call(group_kernel, [VMEM], shape(2 * lat_count, SIDE, LANES))(spread)
    spread = gathered(spread, ("core", "lat"))
    maps, coeffs_t = call(
        functools.partial(factor_kernel, cells), [VMEM], (shape(2 * EOFS, 160, dtype=BF16), shape(SNAPS, EOFS))
    )(spread)
    final_steps = CELL_ROWS // FINAL_ROWS
    new_basis = pl.pallas_call(
        final_kernel,
        out_shape=shape(EOFS, CELL_ROWS, LANES),
        in_specs=[VMEM] * 7,
        out_specs=ANY,
        scratch_shapes=[
            pltpu.VMEM((final_steps, EOFS, FINAL_ROWS, LANES), F32),
            pltpu.SemaphoreType.DMA((final_steps,)),
        ],
        compiler_params=pltpu.CompilerParams(vmem_limit_bytes=8 << 20),
    )(maps, stack, far, keep, here, send, late)
    return (new_basis.reshape(basis.shape), coeffs_t.T)


def solution(mesh):
    pairs = mesh.shape["lon"] // 2
    split = Mesh(mesh.devices.reshape(pairs, 2, *mesh.devices.shape[1:]), LON + tuple(mesh.axis_names[1:]))
    fields = P(None, None, "lat", LON)
    return jax.shard_map(
        update,
        mesh=split,
        in_specs=(P("tm", None, "lat", LON), fields),
        out_specs=(fields, P(None, "tm")),
        check_vma=False,
    )
```

```python
import functools
import math

import jax
import jax.numpy as jnp
from jax import lax
from jax.experimental import pallas as pl
from jax.experimental.pallas import tpu as pltpu
from jax.sharding import Mesh, PartitionSpec as P


SMOOTH_RATE = 0.1
STEP_SIZE = 0.25
SNAPS = 8
LEVELS = 8
ROWS = 16
LANES = 128
EOFS = 64
CELL_ROWS = LEVELS * ROWS
HALF_ROWS = CELL_ROWS // 2
HALF_CELLS = HALF_ROWS * LANES
CHUNK = 8
PAYLOAD = 32
SIDE = PAYLOAD // 2
QROWS = 16
FINAL_ROWS = 16
LON = ("pair", "core")
F32 = jnp.float32
BF16 = jnp.bfloat16
HIGHEST = lax.Precision.HIGHEST
VMEM = pl.BlockSpec(memory_space=pltpu.VMEM)
ANY = pl.BlockSpec(memory_space=pl.ANY)


def lanes_of(shape):
    return lax.broadcasted_iota(jnp.int32, shape, len(shape) - 1)


def shape(*dims, dtype=F32):
    return jax.ShapeDtypeStruct(dims, dtype)


def call(kernel, inputs, outputs, scratch=(), flops=1000000, traffic=1000000, megabytes=8):
    return pl.pallas_call(
        kernel,
        out_shape=outputs,
        in_specs=inputs,
        out_specs=jax.tree.map(lambda _: VMEM, outputs),
        scratch_shapes=scratch,
        cost_estimate=pl.CostEstimate(flops=flops, bytes_accessed=traffic, transcendentals=0),
        compiler_params=pltpu.CompilerParams(vmem_limit_bytes=megabytes << 20),
    )


def pack_kernel(fields_ref, packed_ref, x_ref, sems):
    copies = [pltpu.make_async_copy(fields_ref.at[snap], x_ref.at[snap], sems.at[snap]) for snap in range(SNAPS)]
    for copy in copies:
        copy.start()
    lane = lanes_of((ROWS, LANES))
    for snap, copy in enumerate(copies):
        copy.wait()
        packed = jnp.zeros((ROWS, LANES), F32)
        for level in range(LEVELS):
            turned = pltpu.roll(x_ref[snap, level], 16 * level + 3, 1)
            packed = jnp.where((lane >= 16 * level) & (lane < 16 * level + 6), turned, packed)
        packed_ref[pl.ds(ROWS * snap, ROWS), :] = packed


def seam_kernel(x_ref, packed_ref, across_ref, beside_ref, seam_ref, one_ref, two_ref):
    packed = packed_ref[...]
    lane = lanes_of(packed.shape) % 16
    eastern = lax.axis_index("core") == 1
    far, near = across_ref[...] - packed, beside_ref[...] - packed
    west = jnp.where(lane < 3, jnp.where(eastern, near, far), 0.0)
    east = pltpu.roll(jnp.where((lane >= 3) & (lane < 6), jnp.where(eastern, far, near), 0.0), 8, 1)
    seam_ref[...] = west + east
    even = lax.axis_index("lat") % 2 == 0
    for snap in range(SNAPS):
        at = pl.ds(8 * snap, 8)
        low = jnp.swapaxes(x_ref[snap, :, pl.ds(0, 8), :], 0, 1)
        high = jnp.swapaxes(x_ref[snap, :, pl.ds(8, 8), :], 0, 1)
        for row in range(3):
            one_ref[8 * row + snap] = jnp.where(even, high[5 + row], low[row])
            two_ref[8 * row + snap] = jnp.where(even, low[row], high[5 + row])
    low = jnp.swapaxes(jnp.stack([seam_ref[pl.ds(ROWS * snap, 8), :] for snap in range(SNAPS)]), 0, 1)
    high = jnp.swapaxes(jnp.stack([seam_ref[pl.ds(ROWS * snap + 8, 8), :] for snap in range(SNAPS)]), 0, 1)
    for row in range(3):
        one_ref[24 + row] = jnp.where(even, high[5 + row], low[row])
        two_ref[24 + row] = jnp.where(even, low[row], high[5 + row])


def smooth_kernel(x_ref, seam_ref, one_ref, two_ref, order_ref, keep_ref, send_ref, done, seam_edges):
    lat = lax.axis_index("lat")
    even = lat % 2 == 0
    not_first = jnp.where(lat == 0, 0, 1)
    not_last = jnp.where(lat == lax.axis_size("lat") - 1, 0, 1)
    row = lax.broadcasted_iota(jnp.int32, (8, LANES), 0)
    lane = lanes_of((8, LANES))
    inside = jnp.where(row < 4, not_last, not_first) == 1
    zero = jnp.zeros((8, LANES), F32)
    wide_lane = lanes_of((ROWS, LANES))

    def along_rows(field):
        tall = jnp.concatenate(field, axis=0)
        near = pltpu.roll(tall, 1, 0) + pltpu.roll(tall, 23, 0)
        return near[0:8], near[8:16], near[16:24]

    norths = [jnp.where(even, one_ref[24 + i], two_ref[24 + i]) for i in range(3)]
    souths = [jnp.where(even, two_ref[24 + i], one_ref[24 + i]) for i in range(3)]
    seam_edges[...] = jnp.swapaxes(jnp.stack(norths + [zero, zero] + souths), 0, 1)

    def snapshot(snap, carry):
        edges = jnp.swapaxes(
            jnp.stack(
                [jnp.where(even, one_ref[8 * i + snap], two_ref[8 * i + snap]) for i in range(3)]
                + [zero, zero]
                + [jnp.where(even, two_ref[8 * i + snap], one_ref[8 * i + snap]) for i in range(3)]
            ),
            0,
            1,
        )
        fields = [
            (x_ref[snap, level, pl.ds(0, 8), :], x_ref[snap, level, pl.ds(8, 8), :], edges[level])
            for level in range(LEVELS)
        ]
        seam = (
            seam_ref[pl.ds(pl.multiple_of(ROWS * snap, 8), 8), :],
            seam_ref[pl.ds(pl.multiple_of(ROWS * snap + 8, 8), 8), :],
            seam_edges[snap],
        )
        for sweep in range(3):
            tiles = 3 if sweep < 2 else 2
            fresh_fields = []
            for level in range(LEVELS):
                here = fields[level]
                rows = along_rows(here)
                fresh = []
                for tile in range(tiles):
                    near = rows[tile] + pltpu.roll(here[tile], 1, 1) + pltpu.roll(here[tile], LANES - 1, 1)
                    if level > 0:
                        near = near + fields[level - 1][tile]
                    if level < LEVELS - 1:
                        near = near + fields[level + 1][tile]
                    value = here[tile] + SMOOTH_RATE * (near - 6.0 * here[tile])
                    fresh.append(jnp.where(inside, value, 0.0) if tile == 2 else value)
                fresh_fields.append(tuple(fresh))
            rows = along_rows(seam)
            fresh = []
            for tile in range(tiles):
                here = seam[tile]
                near = rows[tile] + pltpu.roll(here, 1, 1) + pltpu.roll(here, LANES - 1, 1)
                near = near + jnp.where(lane >= 16, pltpu.roll(here, 16, 1), 0.0)
                near = near + jnp.where(lane < LANES - 16, pltpu.roll(here, LANES - 16, 1), 0.0)
                value = here + SMOOTH_RATE * (near - 6.0 * here)
                fresh.append(jnp.where(inside, value, 0.0) if tile == 2 else value)
            fields, seam = fresh_fields, tuple(fresh)
        tall_seam = jnp.concatenate(seam, axis=0)
        for level in range(LEVELS):
            first = pltpu.roll(tall_seam, (LANES - 16 * level - 3) % LANES, 1)
            last = pltpu.roll(tall_seam, (117 - 16 * level) % LANES, 1)
            value = jnp.concatenate(fields[level], axis=0)
            value = value + jnp.where(wide_lane < 3, first, jnp.where(wide_lane >= LANES - 3, last, 0.0))
            done[snap, pl.ds(ROWS * level, ROWS), :] = value
        return carry

    lax.fori_loop(0, SNAPS, snapshot, 0, unroll=2)
    group = lax.axis_index("tm")
    for snap in range(SNAPS):
        keep_ref[snap] = done[snap, pl.ds(pl.multiple_of(HALF_ROWS * group, 8), HALF_ROWS), :]
        send_ref[snap] = done[snap, pl.ds(pl.multiple_of(HALF_ROWS * (1 - group), 8), HALF_ROWS), :]


def pieces(values, count):
    out = []
    for index in range(count):
        piece = values.astype(BF16)
        out.append(piece)
        if index < count - 1:
            values = values - piece.astype(F32)
    return out


def transposed_product(left, right):
    return lax.dot_general(left, right, (((1,), (1,)), ((), ())), preferred_element_type=F32)


def basis_copies(half, q_ref, blocks, sems):
    copies = [
        pltpu.make_async_copy(
            q_ref.at[:, pl.ds(pl.multiple_of(HALF_ROWS * half + QROWS * part, QROWS), QROWS), :],
            blocks.at[part],
            sems.at[part],
        )
        for part in range(HALF_ROWS // QROWS)
    ]
    for copy in copies:
        copy.start()
    return copies


def split_block(block, part, count, stack_ref):
    for sub in range(QROWS // CHUNK):
        turned = jnp.swapaxes(block[:, pl.ds(CHUNK * sub, CHUNK), :], 0, 1)
        for inner in range(CHUNK):
            at = pl.ds(LANES * (QROWS * part + CHUNK * sub + inner), LANES)
            for index, piece in enumerate(pieces(turned[inner], count)):
                stack_ref[pl.ds(EOFS * index, EOFS), at] = piece


def basis_gram_kernel(order_ref, q_ref, stack_ref, gram_ref, blocks, total, sems):
    copies = basis_copies(lax.axis_index("tm"), q_ref, blocks, sems)
    for part, copy in enumerate(copies):
        copy.wait()
        split_block(blocks.at[part], part, 3, stack_ref)
        stack = stack_ref[:, pl.ds(QROWS * LANES * part, QROWS * LANES)]
        product = transposed_product(stack, stack)
        total[...] = product if part == 0 else total[...] + product
    down = total[pl.ds(0, 64), :] + total[pl.ds(64, 64), :] + total[pl.ds(128, 64), :]
    gram_ref[...] = down[:, 0:64] + down[:, 64:128] + down[:, 128:192]


def basis_stack_kernel(order_ref, q_ref, stack_ref, blocks, sems):
    copies = basis_copies(1 - lax.axis_index("tm"), q_ref, blocks, sems)
    for part, copy in enumerate(copies):
        copy.wait()
        split_block(blocks.at[part], part, 2, stack_ref)


def snapshot_columns(ref, start, count):
    turned = jnp.swapaxes(ref[:, pl.ds(start, CHUNK), :], 0, 1)
    return [pieces(turned[i], count) for i in range(CHUNK)]


def in_order(mine, other):
    first = lax.axis_index("tm") == 0
    return jnp.where(first, mine, other), jnp.where(first, other, mine)


def own_gram_kernel(stack_ref, mine_ref, cross_ref, square_ref, pieces_ref):
    def block(step, carry):
        cross, square = carry
        columns = snapshot_columns(mine_ref, pl.multiple_of(CHUNK * step, CHUNK), 3)
        columns = jnp.concatenate([jnp.concatenate(c, axis=0) for c in columns], axis=1)
        width = CHUNK * LANES
        at = pl.ds(pl.multiple_of(width * step, width), width)
        pieces_ref[:, at] = columns
        return cross + transposed_product(stack_ref[:, at], columns), square + transposed_product(columns, columns)

    zeros = (jnp.zeros((192, 24), F32), jnp.zeros((24, 24), F32))
    cross_ref[...], square_ref[...] = lax.fori_loop(0, HALF_ROWS // CHUNK, block, zeros)


def folded(sums, rows):
    down = sums[0:rows] + sums[rows : 2 * rows] + sums[2 * rows : 3 * rows]
    return down[:, 0:8] + down[:, 8:16] + down[:, 16:24]


def snapshot_gram_kernel(
    stack_ref, gram_ref, pieces_ref, other_ref, cross_ref, square_ref, order_ref, own_ref, partner_ref, columns, joined
):
    for step in range(HALF_ROWS // CHUNK):
        other = snapshot_columns(other_ref, CHUNK * step, 3)
        columns[:, pl.ds(CHUNK * LANES * step, CHUNK * LANES)] = jnp.concatenate(
            [jnp.concatenate(c, axis=0) for c in other], axis=1
        )
    cross = transposed_product(stack_ref[...], columns[...])
    square = transposed_product(columns[...], columns[...])
    mixed = transposed_product(pieces_ref[...], columns[...])
    mixed = folded(mixed, 8)
    projection = jnp.concatenate(in_order(folded(cross_ref[...], 64), folded(cross, 64)), axis=1)
    early, late = in_order(folded(square_ref[...], 8), folded(square, 8))
    upper, _ = in_order(mixed, jnp.transpose(mixed))
    square = jnp.concatenate(
        [jnp.concatenate([early, upper], axis=1), jnp.concatenate([jnp.transpose(upper), late], axis=1)], axis=0
    )
    gram = gram_ref[...]
    low, high = gram[0:32, 0:32], gram[32:64, 32:64]
    row = lax.broadcasted_iota(jnp.int32, (32, 32), 0)
    column = lax.broadcasted_iota(jnp.int32, (32, 32), 1)
    diagonal = jnp.sum(jnp.where(row == column, high, 0.0), axis=0, keepdims=True)
    both = jnp.where(row >= column, low, high)
    below = jnp.concatenate(
        [square, jnp.zeros((16, 16), F32), jnp.broadcast_to(diagonal, (16, 32))], axis=1
    )
    right = jnp.concatenate([jnp.transpose(projection), below], axis=0)
    joined[...] = jnp.concatenate([both, gram[32:64, 0:32], right], axis=1)
    core = lax.axis_index("core")
    own_ref[...] = joined[pl.ds(pl.multiple_of(SIDE * core, 8), SIDE), :]
    partner_ref[...] = joined[pl.ds(pl.multiple_of(SIDE * (1 - core), 8), SIDE), :]


def pair_kernel(one_ref, two_ref, out_ref):
    out_ref[...] = jnp.broadcast_to((one_ref[...] + two_ref[...])[None], out_ref.shape)


def group_kernel(parts_ref, out_ref):
    out_ref[...] = jnp.broadcast_to(jnp.sum(parts_ref[...], axis=0)[None], out_ref.shape)


def factor_kernel(cells, parts_ref, maps_ref, coeffs_ref):
    count = parts_ref.shape[0] // 2
    totals = jnp.concatenate(
        [jnp.sum(parts_ref[pl.ds(count * core, count)], axis=0) for core in range(2)], axis=0
    )
    row = lax.broadcasted_iota(jnp.int32, (EOFS, EOFS), 0)
    column = lax.broadcasted_iota(jnp.int32, (EOFS, EOFS), 1)
    both = totals[:, 0:32]
    once = jnp.concatenate(
        [jnp.concatenate([both, jnp.zeros((32, 32), F32)], axis=1), jnp.concatenate([totals[:, 32:64], both], axis=1)], axis=0
    )
    once = jnp.where(((row < 32) & (row > column)) | ((row >= 32) & ((column < 32) | (row < column))), once, 0.0)
    corner = jnp.concatenate([both, jnp.zeros((32, 32), F32)], axis=1)
    diagonal = jnp.concatenate([corner, jnp.broadcast_to(totals[16:17, 64:128], (32, EOFS))], axis=0)
    basis_gram = once + jnp.transpose(once) + jnp.where(row == column, diagonal, 0.0)
    root = math.sqrt(cells)
    coeffs_t = totals[0:16, 64:128] * (1.0 / root)
    snap_gram = totals[16:32, 64:80]
    coeffs_ref[...] = jnp.where(lax.axis_index("tm") == 0, coeffs_t[0:8, :], coeffs_t[8:16, :])
    mixed = (2.0 * STEP_SIZE * root) * coeffs_t + (STEP_SIZE * STEP_SIZE) * jnp.dot(
        snap_gram, coeffs_t, precision=HIGHEST, preferred_element_type=F32
    )
    grown = lax.dot_general(
        coeffs_t, mixed, (((0,), (0,)), ((), ())), precision=HIGHEST, preferred_element_type=F32
    )
    gram = (basis_gram + grown) * (1.0 / cells)
    rows = lax.broadcasted_iota(jnp.int32, (EOFS, EOFS), 0)
    columns = lax.broadcasted_iota(jnp.int32, (EOFS, EOFS), 1)
    work = jnp.concatenate([gram, (rows == columns).astype(F32)], axis=1)
    blocks = [work[8 * i : 8 * i + 8, :] for i in range(8)]
    results = []
    for panel in range(8):
        lower = blocks[panel:]
        columns = [
            [jnp.broadcast_to(b[:, 8 * panel + k : 8 * panel + k + 1], (8, LANES)) for b in lower] for k in range(8)
        ]
        rows = [lower[0][k : k + 1, :] for k in range(8)]
        for k in range(8):
            pivot = columns[k][0][k : k + 1, :]
            if k % 2 == 0:
                corner, upper, side = columns[k + 1][0][k + 1 : k + 2, :], columns[k + 1][0][k : k + 1, :], columns[k][0][k + 1 : k + 2, :]
                inverse = 1.0 / pivot
                following = pivot * (1.0 / (pivot * corner - upper * side))
            else:
                inverse = following
            factors = [c * inverse for c in columns[k]]
            for m in range(k + 1, 8):
                entry = columns[m][0][k : k + 1, :]
                columns[m] = [c - f * entry for c, f in zip(columns[m], factors)]
                rows[m] = rows[m] - factors[0][m : m + 1, :] * rows[k]
            for i in range(panel + 1, 8):
                blocks[i] = blocks[i] - factors[i - panel] * rows[k]
            results.append(rows[k] * lax.rsqrt(pivot))
    inverse = jnp.concatenate(results, axis=0)[:, EOFS:]
    update = lax.dot_general(
        inverse, coeffs_t, (((1,), (1,)), ((), ())), precision=HIGHEST, preferred_element_type=F32
    )
    rows = [
        jnp.concatenate([inverse_part, inverse_part, update_part, update_part], axis=1)
        for inverse_part, update_part in zip(pieces(inverse, 2), pieces(STEP_SIZE * update, 2))
    ]
    maps_ref[...] = jnp.concatenate(rows, axis=0)


def final_kernel(maps_ref, near_ref, far_ref, keep_ref, here_ref, send_ref, late_ref, out_ref, blocks, sems):
    group = lax.axis_index("tm")
    steps = HALF_ROWS // FINAL_ROWS
    copies = []
    for step in range(2 * steps):
        near = step < steps
        half = group if near else 1 - group
        local = step % steps
        stack_ref, mine_ref, other_ref = (near_ref, keep_ref, here_ref) if near else (far_ref, send_ref, late_ref)
        for sub in range(FINAL_ROWS // CHUNK):
            start = local * FINAL_ROWS + CHUNK * sub
            at = pl.ds(start, CHUNK)
            early, late = in_order(
                jnp.swapaxes(mine_ref[:, at, :], 0, 1), jnp.swapaxes(other_ref[:, at, :], 0, 1)
            )
            columns = jnp.concatenate(
                [
                    jnp.concatenate(pieces(jnp.concatenate([early[i], late[i]], axis=0), 2), axis=0)
                    for i in range(CHUNK)
                ],
                axis=1,
            )
            stack = stack_ref[pl.ds(0, 2 * EOFS), pl.ds(start * LANES, CHUNK * LANES)]
            both = jnp.dot(maps_ref[...], jnp.concatenate([stack, columns], axis=0), preferred_element_type=F32)
            result = both[0:EOFS, :] + both[EOFS:, :]
            result = jnp.stack([result[:, LANES * i : LANES * (i + 1)] for i in range(CHUNK)])
            blocks[step, :, pl.ds(CHUNK * sub, CHUNK), :] = jnp.swapaxes(result, 0, 1)
        to = pl.ds(pl.multiple_of(HALF_ROWS * half + FINAL_ROWS * local, FINAL_ROWS), FINAL_ROWS)
        copy = pltpu.make_async_copy(blocks.at[step], out_ref.at[:, to, :], sems.at[step])
        copy.start()
        copies.append(copy)
    for copy in copies:
        copy.wait()


def swapped(values, axis, first):
    count = lax.axis_size(axis)
    pairs = [(i, (i + 1) % count) for i in range(first, count - first % 2 * (axis == "lat"), 2)]
    return lax.ppermute(values, axis, [p for one, two in pairs for p in ((one, two), (two, one))])


def across(values, axis):
    return lax.ppermute(values, axis, [(0, 1), (1, 0)])


def gathered(values, axes):
    return lax.all_to_all(values, axes, 0, 0)


def update(snapshots, basis):
    lat_count = lax.axis_size("lat")
    cells = CELL_ROWS * LANES * lat_count * lax.axis_size(LON)
    q = pltpu.with_memory_space_constraint(basis.reshape(EOFS, CELL_ROWS, LANES), pltpu.HBM)

    packed, x = call(
        pack_kernel,
        [ANY],
        (shape(CELL_ROWS, LANES), shape(*snapshots.shape)),
        [pltpu.SemaphoreType.DMA((SNAPS,))],
    )(pltpu.with_memory_space_constraint(snapshots, pltpu.HBM))
    chip = swapped(packed, LON, 1)
    beside = across(packed, "core")
    seam, one, two = call(
        seam_kernel, [VMEM] * 4, (shape(CELL_ROWS, LANES), shape(27, 8, LANES), shape(27, 8, LANES))
    )(x, packed, chip, beside)
    one, two = swapped(one, "lat", 0), swapped(two, "lat", 1)
    parts = HALF_ROWS // QROWS
    stack, gram = call(
        basis_gram_kernel,
        [VMEM, ANY],
        (shape(3 * EOFS, HALF_CELLS, dtype=BF16), shape(EOFS, EOFS)),
        [pltpu.VMEM((parts, EOFS, QROWS, LANES), F32), pltpu.VMEM((192, 192), F32), pltpu.SemaphoreType.DMA((parts,))],
        traffic=8 << 20,
    )(seam, q)
    keep, send = call(
        smooth_kernel,
        [VMEM] * 5,
        (shape(SNAPS, HALF_ROWS, LANES),) * 2,
        [pltpu.VMEM((SNAPS, CELL_ROWS, LANES), F32), pltpu.VMEM((SNAPS, 8, LANES), F32)],
    )(x, seam, one, two, gram)
    here = across(send, "tm")
    far = call(
        basis_stack_kernel,
        [VMEM, ANY],
        shape(2 * EOFS, HALF_CELLS, dtype=BF16),
        [pltpu.VMEM((parts, EOFS, QROWS, LANES), F32), pltpu.SemaphoreType.DMA((parts,))],
        traffic=6 << 20,
    )(keep, q)
    cross, square, split = call(
        own_gram_kernel,
        [VMEM] * 2,
        (shape(192, 24), shape(24, 24), shape(24, HALF_CELLS, dtype=BF16)),
        traffic=4 << 20,
    )(stack, keep)
    side = shape(SIDE, LANES)
    late = across(keep, "tm")
    mine, theirs = call(
        snapshot_gram_kernel, [VMEM] * 7, (side, side), [pltpu.VMEM((24, HALF_CELLS), BF16), pltpu.VMEM((PAYLOAD, LANES), F32)]
    )(stack, gram, split, here, cross, square, far)
    group = lax.axis_size(("pair", "tm"))
    spread = call(pair_kernel, [VMEM] * 2, shape(group, SIDE, LANES))(mine, across(theirs, "core"))
    spread = gathered(spread, ("pair", "tm"))
    spread = call(group_kernel, [VMEM], shape(2 * lat_count, SIDE, LANES))(spread)
    spread = gathered(spread, ("core", "lat"))
    maps, coeffs_t = call(
        functools.partial(factor_kernel, cells), [VMEM], (shape(2 * EOFS, 160, dtype=BF16), shape(SNAPS, EOFS))
    )(spread)
    final_steps = CELL_ROWS // FINAL_ROWS
    new_basis = pl.pallas_call(
        final_kernel,
        out_shape=shape(EOFS, CELL_ROWS, LANES),
        in_specs=[VMEM] * 7,
        out_specs=ANY,
        scratch_shapes=[
            pltpu.VMEM((final_steps, EOFS, FINAL_ROWS, LANES), F32),
            pltpu.SemaphoreType.DMA((final_steps,)),
        ],
        compiler_params=pltpu.CompilerParams(vmem_limit_bytes=8 << 20),
    )(maps, stack, far, keep, here, send, late)
    return (new_basis.reshape(basis.shape), coeffs_t.T)


def solution(mesh):
    pairs = mesh.shape["lon"] // 2
    split = Mesh(mesh.devices.reshape(pairs, 2, *mesh.devices.shape[1:]), LON + tuple(mesh.axis_names[1:]))
    fields = P(None, None, "lat", LON)
    return jax.shard_map(
        update,
        mesh=split,
        in_specs=(P("tm", None, "lat", LON), fields),
        out_specs=(fields, P(None, "tm")),
        check_vma=False,
    )
```

```python
import functools
import math

import jax
import jax.numpy as jnp
from jax import lax
from jax.experimental import pallas as pl
from jax.experimental.pallas import tpu as pltpu
from jax.sharding import Mesh, PartitionSpec as P


SMOOTH_RATE = 0.1
STEP_SIZE = 0.25
SNAPS = 8
LEVELS = 8
ROWS = 16
LANES = 128
EOFS = 64
CELL_ROWS = LEVELS * ROWS
HALF_ROWS = CELL_ROWS // 2
HALF_CELLS = HALF_ROWS * LANES
CHUNK = 8
PAYLOAD = 32
SIDE = PAYLOAD // 2
QROWS = 16
FINAL_ROWS = 16
LON = ("pair", "core")
F32 = jnp.float32
BF16 = jnp.bfloat16
HIGHEST = lax.Precision.HIGHEST
VMEM = pl.BlockSpec(memory_space=pltpu.VMEM)
ANY = pl.BlockSpec(memory_space=pl.ANY)


def lanes_of(shape):
    return lax.broadcasted_iota(jnp.int32, shape, len(shape) - 1)


def shape(*dims, dtype=F32):
    return jax.ShapeDtypeStruct(dims, dtype)


def call(kernel, inputs, outputs, scratch=(), flops=1000000, traffic=1000000, megabytes=8):
    return pl.pallas_call(
        kernel,
        out_shape=outputs,
        in_specs=inputs,
        out_specs=jax.tree.map(lambda _: VMEM, outputs),
        scratch_shapes=scratch,
        cost_estimate=pl.CostEstimate(flops=flops, bytes_accessed=traffic, transcendentals=0),
        compiler_params=pltpu.CompilerParams(vmem_limit_bytes=megabytes << 20),
    )


def pack_kernel(x_ref, packed_ref):
    lane = lanes_of((ROWS, LANES))
    for snap in range(SNAPS):
        packed = jnp.zeros((ROWS, LANES), F32)
        for level in range(LEVELS):
            turned = pltpu.roll(x_ref[snap, level], 16 * level + 3, 1)
            packed = jnp.where((lane >= 16 * level) & (lane < 16 * level + 6), turned, packed)
        packed_ref[pl.ds(ROWS * snap, ROWS), :] = packed


def seam_kernel(x_ref, packed_ref, across_ref, beside_ref, seam_ref, one_ref, two_ref):
    packed = packed_ref[...]
    lane = lanes_of(packed.shape) % 16
    eastern = lax.axis_index("core") == 1
    far, near = across_ref[...] - packed, beside_ref[...] - packed
    west = jnp.where(lane < 3, jnp.where(eastern, near, far), 0.0)
    east = pltpu.roll(jnp.where((lane >= 3) & (lane < 6), jnp.where(eastern, far, near), 0.0), 8, 1)
    seam_ref[...] = west + east
    even = lax.axis_index("lat") % 2 == 0
    for snap in range(SNAPS):
        at = pl.ds(8 * snap, 8)
        low = jnp.swapaxes(x_ref[snap, :, pl.ds(0, 8), :], 0, 1)
        high = jnp.swapaxes(x_ref[snap, :, pl.ds(8, 8), :], 0, 1)
        for row in range(3):
            one_ref[8 * row + snap] = jnp.where(even, high[5 + row], low[row])
            two_ref[8 * row + snap] = jnp.where(even, low[row], high[5 + row])
    low = jnp.swapaxes(jnp.stack([seam_ref[pl.ds(ROWS * snap, 8), :] for snap in range(SNAPS)]), 0, 1)
    high = jnp.swapaxes(jnp.stack([seam_ref[pl.ds(ROWS * snap + 8, 8), :] for snap in range(SNAPS)]), 0, 1)
    for row in range(3):
        one_ref[24 + row] = jnp.where(even, high[5 + row], low[row])
        two_ref[24 + row] = jnp.where(even, low[row], high[5 + row])


def smooth_kernel(x_ref, seam_ref, one_ref, two_ref, order_ref, keep_ref, send_ref, done, seam_edges):
    lat = lax.axis_index("lat")
    even = lat % 2 == 0
    not_first = jnp.where(lat == 0, 0, 1)
    not_last = jnp.where(lat == lax.axis_size("lat") - 1, 0, 1)
    row = lax.broadcasted_iota(jnp.int32, (8, LANES), 0)
    lane = lanes_of((8, LANES))
    inside = jnp.where(row < 4, not_last, not_first) == 1
    zero = jnp.zeros((8, LANES), F32)
    wide_lane = lanes_of((ROWS, LANES))

    def along_rows(field):
        tall = jnp.concatenate(field, axis=0)
        near = pltpu.roll(tall, 1, 0) + pltpu.roll(tall, 23, 0)
        return near[0:8], near[8:16], near[16:24]

    norths = [jnp.where(even, one_ref[24 + i], two_ref[24 + i]) for i in range(3)]
    souths = [jnp.where(even, two_ref[24 + i], one_ref[24 + i]) for i in range(3)]
    seam_edges[...] = jnp.swapaxes(jnp.stack(norths + [zero, zero] + souths), 0, 1)

    def snapshot(snap, carry):
        edges = jnp.swapaxes(
            jnp.stack(
                [jnp.where(even, one_ref[8 * i + snap], two_ref[8 * i + snap]) for i in range(3)]
                + [zero, zero]
                + [jnp.where(even, two_ref[8 * i + snap], one_ref[8 * i + snap]) for i in range(3)]
            ),
            0,
            1,
        )
        fields = [
            (x_ref[snap, level, pl.ds(0, 8), :], x_ref[snap, level, pl.ds(8, 8), :], edges[level])
            for level in range(LEVELS)
        ]
        seam = (
            seam_ref[pl.ds(pl.multiple_of(ROWS * snap, 8), 8), :],
            seam_ref[pl.ds(pl.multiple_of(ROWS * snap + 8, 8), 8), :],
            seam_edges[snap],
        )
        for sweep in range(3):
            tiles = 3 if sweep < 2 else 2
            fresh_fields = []
            for level in range(LEVELS):
                here = fields[level]
                rows = along_rows(here)
                fresh = []
                for tile in range(tiles):
                    near = rows[tile] + pltpu.roll(here[tile], 1, 1) + pltpu.roll(here[tile], LANES - 1, 1)
                    if level > 0:
                        near = near + fields[level - 1][tile]
                    if level < LEVELS - 1:
                        near = near + fields[level + 1][tile]
                    value = here[tile] + SMOOTH_RATE * (near - 6.0 * here[tile])
                    fresh.append(jnp.where(inside, value, 0.0) if tile == 2 else value)
                fresh_fields.append(tuple(fresh))
            rows = along_rows(seam)
            fresh = []
            for tile in range(tiles):
                here = seam[tile]
                near = rows[tile] + pltpu.roll(here, 1, 1) + pltpu.roll(here, LANES - 1, 1)
                near = near + jnp.where(lane >= 16, pltpu.roll(here, 16, 1), 0.0)
                near = near + jnp.where(lane < LANES - 16, pltpu.roll(here, LANES - 16, 1), 0.0)
                value = here + SMOOTH_RATE * (near - 6.0 * here)
                fresh.append(jnp.where(inside, value, 0.0) if tile == 2 else value)
            fields, seam = fresh_fields, tuple(fresh)
        tall_seam = jnp.concatenate(seam, axis=0)
        for level in range(LEVELS):
            first = pltpu.roll(tall_seam, (LANES - 16 * level - 3) % LANES, 1)
            last = pltpu.roll(tall_seam, (117 - 16 * level) % LANES, 1)
            value = jnp.concatenate(fields[level], axis=0)
            value = value + jnp.where(wide_lane < 3, first, jnp.where(wide_lane >= LANES - 3, last, 0.0))
            done[snap, pl.ds(ROWS * level, ROWS), :] = value
        return carry

    lax.fori_loop(0, SNAPS, snapshot, 0, unroll=2)
    group = lax.axis_index("tm")
    for snap in range(SNAPS):
        keep_ref[snap] = done[snap, pl.ds(pl.multiple_of(HALF_ROWS * group, 8), HALF_ROWS), :]
        send_ref[snap] = done[snap, pl.ds(pl.multiple_of(HALF_ROWS * (1 - group), 8), HALF_ROWS), :]


def pieces(values, count):
    out = []
    for index in range(count):
        piece = values.astype(BF16)
        out.append(piece)
        if index < count - 1:
            values = values - piece.astype(F32)
    return out


def transposed_product(left, right):
    return lax.dot_general(left, right, (((1,), (1,)), ((), ())), preferred_element_type=F32)


def basis_copies(half, q_ref, blocks, sems):
    copies = [
        pltpu.make_async_copy(
            q_ref.at[:, pl.ds(pl.multiple_of(HALF_ROWS * half + QROWS * part, QROWS), QROWS), :],
            blocks.at[part],
            sems.at[part],
        )
        for part in range(HALF_ROWS // QROWS)
    ]
    for copy in copies:
        copy.start()
    return copies


def split_block(block, part, count, stack_ref):
    for sub in range(QROWS // CHUNK):
        turned = jnp.swapaxes(block[:, pl.ds(CHUNK * sub, CHUNK), :], 0, 1)
        for inner in range(CHUNK):
            at = pl.ds(LANES * (QROWS * part + CHUNK * sub + inner), LANES)
            for index, piece in enumerate(pieces(turned[inner], count)):
                stack_ref[pl.ds(EOFS * index, EOFS), at] = piece


def basis_gram_kernel(order_ref, q_ref, stack_ref, gram_ref, blocks, total, sems):
    copies = basis_copies(lax.axis_index("tm"), q_ref, blocks, sems)
    for part, copy in enumerate(copies):
        copy.wait()
        split_block(blocks.at[part], part, 3, stack_ref)
        stack = stack_ref[:, pl.ds(QROWS * LANES * part, QROWS * LANES)]
        product = transposed_product(stack, stack)
        total[...] = product if part == 0 else total[...] + product
    down = total[pl.ds(0, 64), :] + total[pl.ds(64, 64), :] + total[pl.ds(128, 64), :]
    gram_ref[...] = down[:, 0:64] + down[:, 64:128] + down[:, 128:192]


def basis_stack_kernel(order_ref, q_ref, stack_ref, blocks, sems):
    copies = basis_copies(1 - lax.axis_index("tm"), q_ref, blocks, sems)
    for part, copy in enumerate(copies):
        copy.wait()
        split_block(blocks.at[part], part, 2, stack_ref)


def snapshot_columns(ref, start, count):
    turned = jnp.swapaxes(ref[:, pl.ds(start, CHUNK), :], 0, 1)
    return [pieces(turned[i], count) for i in range(CHUNK)]


def in_order(mine, other):
    first = lax.axis_index("tm") == 0
    return jnp.where(first, mine, other), jnp.where(first, other, mine)


def own_gram_kernel(stack_ref, mine_ref, cross_ref, square_ref, pieces_ref):
    def block(step, carry):
        cross, square = carry
        columns = snapshot_columns(mine_ref, pl.multiple_of(CHUNK * step, CHUNK), 3)
        columns = jnp.concatenate([jnp.concatenate(c, axis=0) for c in columns], axis=1)
        width = CHUNK * LANES
        at = pl.ds(pl.multiple_of(width * step, width), width)
        pieces_ref[:, at] = columns
        return cross + transposed_product(stack_ref[:, at], columns), square + transposed_product(columns, columns)

    zeros = (jnp.zeros((192, 24), F32), jnp.zeros((24, 24), F32))
    cross_ref[...], square_ref[...] = lax.fori_loop(0, HALF_ROWS // CHUNK, block, zeros)


def folded(sums, rows):
    down = sums[0:rows] + sums[rows : 2 * rows] + sums[2 * rows : 3 * rows]
    return down[:, 0:8] + down[:, 8:16] + down[:, 16:24]


def snapshot_gram_kernel(
    stack_ref, gram_ref, pieces_ref, other_ref, cross_ref, square_ref, order_ref, own_ref, partner_ref, columns, joined
):
    for step in range(HALF_ROWS // CHUNK):
        other = snapshot_columns(other_ref, CHUNK * step, 3)
        columns[:, pl.ds(CHUNK * LANES * step, CHUNK * LANES)] = jnp.concatenate(
            [jnp.concatenate(c, axis=0) for c in other], axis=1
        )
    cross = transposed_product(stack_ref[...], columns[...])
    square = transposed_product(columns[...], columns[...])
    mixed = transposed_product(pieces_ref[...], columns[...])
    mixed = folded(mixed, 8)
    projection = jnp.concatenate(in_order(folded(cross_ref[...], 64), folded(cross, 64)), axis=1)
    early, late = in_order(folded(square_ref[...], 8), folded(square, 8))
    upper, _ = in_order(mixed, jnp.transpose(mixed))
    square = jnp.concatenate(
        [jnp.concatenate([early, upper], axis=1), jnp.concatenate([jnp.transpose(upper), late], axis=1)], axis=0
    )
    gram = gram_ref[...]
    low, high = gram[0:32, 0:32], gram[32:64, 32:64]
    row = lax.broadcasted_iota(jnp.int32, (32, 32), 0)
    column = lax.broadcasted_iota(jnp.int32, (32, 32), 1)
    diagonal = jnp.sum(jnp.where(row == column, high, 0.0), axis=0, keepdims=True)
    both = jnp.where(row >= column, low, high)
    below = jnp.concatenate(
        [square, jnp.zeros((16, 16), F32), jnp.broadcast_to(diagonal, (16, 32))], axis=1
    )
    right = jnp.concatenate([jnp.transpose(projection), below], axis=0)
    joined[...] = jnp.concatenate([both, gram[32:64, 0:32], right], axis=1)
    core = lax.axis_index("core")
    own_ref[...] = joined[pl.ds(pl.multiple_of(SIDE * core, 8), SIDE), :]
    partner_ref[...] = joined[pl.ds(pl.multiple_of(SIDE * (1 - core), 8), SIDE), :]


def pair_kernel(one_ref, two_ref, out_ref):
    out_ref[...] = jnp.broadcast_to((one_ref[...] + two_ref[...])[None], out_ref.shape)


def group_kernel(parts_ref, out_ref):
    out_ref[...] = jnp.broadcast_to(jnp.sum(parts_ref[...], axis=0)[None], out_ref.shape)


def factor_kernel(cells, parts_ref, maps_ref, coeffs_ref):
    count = parts_ref.shape[0] // 2
    totals = jnp.concatenate(
        [jnp.sum(parts_ref[pl.ds(count * core, count)], axis=0) for core in range(2)], axis=0
    )
    row = lax.broadcasted_iota(jnp.int32, (EOFS, EOFS), 0)
    column = lax.broadcasted_iota(jnp.int32, (EOFS, EOFS), 1)
    both = totals[:, 0:32]
    once = jnp.concatenate(
        [jnp.concatenate([both, jnp.zeros((32, 32), F32)], axis=1), jnp.concatenate([totals[:, 32:64], both], axis=1)], axis=0
    )
    once = jnp.where(((row < 32) & (row > column)) | ((row >= 32) & ((column < 32) | (row < column))), once, 0.0)
    corner = jnp.concatenate([both, jnp.zeros((32, 32), F32)], axis=1)
    diagonal = jnp.concatenate([corner, jnp.broadcast_to(totals[16:17, 64:128], (32, EOFS))], axis=0)
    basis_gram = once + jnp.transpose(once) + jnp.where(row == column, diagonal, 0.0)
    root = math.sqrt(cells)
    coeffs_t = totals[0:16, 64:128] * (1.0 / root)
    snap_gram = totals[16:32, 64:80]
    coeffs_ref[...] = jnp.where(lax.axis_index("tm") == 0, coeffs_t[0:8, :], coeffs_t[8:16, :])
    mixed = (2.0 * STEP_SIZE * root) * coeffs_t + (STEP_SIZE * STEP_SIZE) * jnp.dot(
        snap_gram, coeffs_t, precision=HIGHEST, preferred_element_type=F32
    )
    grown = lax.dot_general(
        coeffs_t, mixed, (((0,), (0,)), ((), ())), precision=HIGHEST, preferred_element_type=F32
    )
    gram = (basis_gram + grown) * (1.0 / cells)
    rows = lax.broadcasted_iota(jnp.int32, (EOFS, EOFS), 0)
    columns = lax.broadcasted_iota(jnp.int32, (EOFS, EOFS), 1)
    work = jnp.concatenate([gram, (rows == columns).astype(F32)], axis=1)
    blocks = [work[8 * i : 8 * i + 8, :] for i in range(8)]
    results = []
    for panel in range(8):
        lower = blocks[panel:]
        columns = [
            [jnp.broadcast_to(b[:, 8 * panel + k : 8 * panel + k + 1], (8, LANES)) for b in lower] for k in range(8)
        ]
        rows = [lower[0][k : k + 1, :] for k in range(8)]
        for k in range(8):
            pivot = columns[k][0][k : k + 1, :]
            if k % 2 == 0:
                corner, upper, side = columns[k + 1][0][k + 1 : k + 2, :], columns[k + 1][0][k : k + 1, :], columns[k][0][k + 1 : k + 2, :]
                inverse = 1.0 / pivot
                following = pivot * (1.0 / (pivot * corner - upper * side))
            else:
                inverse = following
            factors = [c * inverse for c in columns[k]]
            for m in range(k + 1, 8):
                entry = columns[m][0][k : k + 1, :]
                columns[m] = [c - f * entry for c, f in zip(columns[m], factors)]
                rows[m] = rows[m] - factors[0][m : m + 1, :] * rows[k]
            for i in range(panel + 1, 8):
                blocks[i] = blocks[i] - factors[i - panel] * rows[k]
            results.append(rows[k] * lax.rsqrt(pivot))
    inverse = jnp.concatenate(results, axis=0)[:, EOFS:]
    update = lax.dot_general(
        inverse, coeffs_t, (((1,), (1,)), ((), ())), precision=HIGHEST, preferred_element_type=F32
    )
    rows = [
        jnp.concatenate([inverse_part, inverse_part, update_part, update_part], axis=1)
        for inverse_part, update_part in zip(pieces(inverse, 2), pieces(STEP_SIZE * update, 2))
    ]
    maps_ref[...] = jnp.concatenate(rows, axis=0)


def final_kernel(maps_ref, near_ref, far_ref, keep_ref, here_ref, send_ref, late_ref, out_ref, blocks, sems):
    group = lax.axis_index("tm")
    steps = HALF_ROWS // FINAL_ROWS
    copies = []
    for step in range(2 * steps):
        near = step < steps
        half = group if near else 1 - group
        local = step % steps
        stack_ref, mine_ref, other_ref = (near_ref, keep_ref, here_ref) if near else (far_ref, send_ref, late_ref)
        for sub in range(FINAL_ROWS // CHUNK):
            start = local * FINAL_ROWS + CHUNK * sub
            at = pl.ds(start, CHUNK)
            early, late = in_order(
                jnp.swapaxes(mine_ref[:, at, :], 0, 1), jnp.swapaxes(other_ref[:, at, :], 0, 1)
            )
            columns = jnp.concatenate(
                [
                    jnp.concatenate(pieces(jnp.concatenate([early[i], late[i]], axis=0), 2), axis=0)
                    for i in range(CHUNK)
                ],
                axis=1,
            )
            stack = stack_ref[pl.ds(0, 2 * EOFS), pl.ds(start * LANES, CHUNK * LANES)]
            both = jnp.dot(maps_ref[...], jnp.concatenate([stack, columns], axis=0), preferred_element_type=F32)
            result = both[0:EOFS, :] + both[EOFS:, :]
            result = jnp.stack([result[:, LANES * i : LANES * (i + 1)] for i in range(CHUNK)])
            blocks[step, :, pl.ds(CHUNK * sub, CHUNK), :] = jnp.swapaxes(result, 0, 1)
        to = pl.ds(pl.multiple_of(HALF_ROWS * half + FINAL_ROWS * local, FINAL_ROWS), FINAL_ROWS)
        copy = pltpu.make_async_copy(blocks.at[step], out_ref.at[:, to, :], sems.at[step])
        copy.start()
        copies.append(copy)
    for copy in copies:
        copy.wait()


def swapped(values, axis, first):
    count = lax.axis_size(axis)
    pairs = [(i, (i + 1) % count) for i in range(first, count - first % 2 * (axis == "lat"), 2)]
    return lax.ppermute(values, axis, [p for one, two in pairs for p in ((one, two), (two, one))])


def across(values, axis):
    return lax.ppermute(values, axis, [(0, 1), (1, 0)])


def gathered(values, axes):
    return lax.all_to_all(values, axes, 0, 0)


def update(snapshots, basis):
    lat_count = lax.axis_size("lat")
    cells = CELL_ROWS * LANES * lat_count * lax.axis_size(LON)
    q = pltpu.with_memory_space_constraint(basis.reshape(EOFS, CELL_ROWS, LANES), pltpu.HBM)

    packed = call(pack_kernel, [VMEM], shape(CELL_ROWS, LANES))(snapshots)
    chip = swapped(packed, LON, 1)
    beside = across(packed, "core")
    seam, one, two = call(
        seam_kernel, [VMEM] * 4, (shape(CELL_ROWS, LANES), shape(27, 8, LANES), shape(27, 8, LANES))
    )(snapshots, packed, chip, beside)
    one, two = swapped(one, "lat", 0), swapped(two, "lat", 1)
    parts = HALF_ROWS // QROWS
    stack, gram = call(
        basis_gram_kernel,
        [VMEM, ANY],
        (shape(3 * EOFS, HALF_CELLS, dtype=BF16), shape(EOFS, EOFS)),
        [pltpu.VMEM((parts, EOFS, QROWS, LANES), F32), pltpu.VMEM((192, 192), F32), pltpu.SemaphoreType.DMA((parts,))],
        traffic=8 << 20,
    )(seam, q)
    keep, send = call(
        smooth_kernel,
        [VMEM] * 5,
        (shape(SNAPS, HALF_ROWS, LANES),) * 2,
        [pltpu.VMEM((SNAPS, CELL_ROWS, LANES), F32), pltpu.VMEM((SNAPS, 8, LANES), F32)],
    )(snapshots, seam, one, two, gram)
    here = across(send, "tm")
    far = call(
        basis_stack_kernel,
        [VMEM, ANY],
        shape(2 * EOFS, HALF_CELLS, dtype=BF16),
        [pltpu.VMEM((parts, EOFS, QROWS, LANES), F32), pltpu.SemaphoreType.DMA((parts,))],
        traffic=6 << 20,
    )(keep, q)
    cross, square, split = call(
        own_gram_kernel,
        [VMEM] * 2,
        (shape(192, 24), shape(24, 24), shape(24, HALF_CELLS, dtype=BF16)),
        traffic=4 << 20,
    )(stack, keep)
    side = shape(SIDE, LANES)
    late = across(keep, "tm")
    mine, theirs = call(
        snapshot_gram_kernel, [VMEM] * 7, (side, side), [pltpu.VMEM((24, HALF_CELLS), BF16), pltpu.VMEM((PAYLOAD, LANES), F32)]
    )(stack, gram, split, here, cross, square, far)
    group = lax.axis_size(("pair", "tm"))
    spread = call(pair_kernel, [VMEM] * 2, shape(group, SIDE, LANES))(mine, across(theirs, "core"))
    spread = gathered(spread, ("pair", "tm"))
    spread = call(group_kernel, [VMEM], shape(2 * lat_count, SIDE, LANES))(spread)
    spread = gathered(spread, ("core", "lat"))
    maps, coeffs_t = call(
        functools.partial(factor_kernel, cells), [VMEM], (shape(2 * EOFS, 160, dtype=BF16), shape(SNAPS, EOFS))
    )(spread)
    final_steps = CELL_ROWS // FINAL_ROWS
    new_basis = pl.pallas_call(
        final_kernel,
        out_shape=shape(EOFS, CELL_ROWS, LANES),
        in_specs=[VMEM] * 7,
        out_specs=ANY,
        scratch_shapes=[
            pltpu.VMEM((final_steps, EOFS, FINAL_ROWS, LANES), F32),
            pltpu.SemaphoreType.DMA((final_steps,)),
        ],
        compiler_params=pltpu.CompilerParams(vmem_limit_bytes=8 << 20),
    )(maps, stack, far, keep, here, send, late)
    return (new_basis.reshape(basis.shape), coeffs_t.T)


def solution(mesh):
    pairs = mesh.shape["lon"] // 2
    split = Mesh(mesh.devices.reshape(pairs, 2, *mesh.devices.shape[1:]), LON + tuple(mesh.axis_names[1:]))
    fields = P(None, None, "lat", LON)
    return jax.shard_map(
        update,
        mesh=split,
        in_specs=(P("tm", None, "lat", LON), fields),
        out_specs=(fields, P(None, "tm")),
        check_vma=False,
    )
```

```python
import functools
import math

import jax
import jax.numpy as jnp
from jax import lax
from jax.experimental import pallas as pl
from jax.experimental.pallas import tpu as pltpu
from jax.sharding import Mesh, PartitionSpec as P


SMOOTH_RATE = 0.1
STEP_SIZE = 0.25
SNAPS = 8
LEVELS = 8
ROWS = 16
LANES = 128
EOFS = 64
CELL_ROWS = LEVELS * ROWS
HALF_ROWS = CELL_ROWS // 2
HALF_CELLS = HALF_ROWS * LANES
CHUNK = 8
PAYLOAD = 32
SIDE = PAYLOAD // 2
QROWS = 16
FINAL_ROWS = 16
PART = SNAPS // 2
LON = ("pair", "core")
F32 = jnp.float32
BF16 = jnp.bfloat16
HIGHEST = lax.Precision.HIGHEST
VMEM = pl.BlockSpec(memory_space=pltpu.VMEM)
ANY = pl.BlockSpec(memory_space=pl.ANY)


def lanes_of(shape):
    return lax.broadcasted_iota(jnp.int32, shape, len(shape) - 1)


def shape(*dims, dtype=F32):
    return jax.ShapeDtypeStruct(dims, dtype)


def call(kernel, inputs, outputs, scratch=(), flops=1000000, traffic=1000000, megabytes=8):
    return pl.pallas_call(
        kernel,
        out_shape=outputs,
        in_specs=inputs,
        out_specs=jax.tree.map(lambda _: VMEM, outputs),
        scratch_shapes=scratch,
        cost_estimate=pl.CostEstimate(flops=flops, bytes_accessed=traffic, transcendentals=0),
        compiler_params=pltpu.CompilerParams(vmem_limit_bytes=megabytes << 20),
    )


def pack_kernel(x_ref, packed_ref):
    lane = lanes_of((ROWS, LANES))
    for snap in range(SNAPS):
        packed = jnp.zeros((ROWS, LANES), F32)
        for level in range(LEVELS):
            turned = pltpu.roll(x_ref[snap, level], 16 * level + 3, 1)
            packed = jnp.where((lane >= 16 * level) & (lane < 16 * level + 6), turned, packed)
        packed_ref[pl.ds(ROWS * snap, ROWS), :] = packed


def seam_kernel(x_ref, packed_ref, across_ref, beside_ref, seam_ref, one_ref, two_ref):
    packed = packed_ref[...]
    lane = lanes_of(packed.shape) % 16
    eastern = lax.axis_index("core") == 1
    far, near = across_ref[...] - packed, beside_ref[...] - packed
    west = jnp.where(lane < 3, jnp.where(eastern, near, far), 0.0)
    east = pltpu.roll(jnp.where((lane >= 3) & (lane < 6), jnp.where(eastern, far, near), 0.0), 8, 1)
    seam_ref[...] = west + east
    even = lax.axis_index("lat") % 2 == 0
    for snap in range(SNAPS):
        at = pl.ds(8 * snap, 8)
        low = jnp.swapaxes(x_ref[snap, :, pl.ds(0, 8), :], 0, 1)
        high = jnp.swapaxes(x_ref[snap, :, pl.ds(8, 8), :], 0, 1)
        for row in range(3):
            one_ref[8 * row + snap] = jnp.where(even, high[5 + row], low[row])
            two_ref[8 * row + snap] = jnp.where(even, low[row], high[5 + row])
    low = jnp.swapaxes(jnp.stack([seam_ref[pl.ds(ROWS * snap, 8), :] for snap in range(SNAPS)]), 0, 1)
    high = jnp.swapaxes(jnp.stack([seam_ref[pl.ds(ROWS * snap + 8, 8), :] for snap in range(SNAPS)]), 0, 1)
    for row in range(3):
        one_ref[24 + row] = jnp.where(even, high[5 + row], low[row])
        two_ref[24 + row] = jnp.where(even, low[row], high[5 + row])


def smooth_kernel(begin, x_ref, seam_ref, one_ref, two_ref, order_ref, keep_ref, send_ref, done, seam_edges):
    lat = lax.axis_index("lat")
    even = lat % 2 == 0
    not_first = jnp.where(lat == 0, 0, 1)
    not_last = jnp.where(lat == lax.axis_size("lat") - 1, 0, 1)
    row = lax.broadcasted_iota(jnp.int32, (8, LANES), 0)
    lane = lanes_of((8, LANES))
    inside = jnp.where(row < 4, not_last, not_first) == 1
    zero = jnp.zeros((8, LANES), F32)
    wide_lane = lanes_of((ROWS, LANES))

    def along_rows(field):
        tall = jnp.concatenate(field, axis=0)
        near = pltpu.roll(tall, 1, 0) + pltpu.roll(tall, 23, 0)
        return near[0:8], near[8:16], near[16:24]

    norths = [jnp.where(even, one_ref[24 + i], two_ref[24 + i]) for i in range(3)]
    souths = [jnp.where(even, two_ref[24 + i], one_ref[24 + i]) for i in range(3)]
    seam_edges[...] = jnp.swapaxes(jnp.stack(norths + [zero, zero] + souths), 0, 1)

    def snapshot(snap, carry):
        edges = jnp.swapaxes(
            jnp.stack(
                [jnp.where(even, one_ref[8 * i + snap], two_ref[8 * i + snap]) for i in range(3)]
                + [zero, zero]
                + [jnp.where(even, two_ref[8 * i + snap], one_ref[8 * i + snap]) for i in range(3)]
            ),
            0,
            1,
        )
        fields = [
            (x_ref[snap, level, pl.ds(0, 8), :], x_ref[snap, level, pl.ds(8, 8), :], edges[level])
            for level in range(LEVELS)
        ]
        seam = (
            seam_ref[pl.ds(pl.multiple_of(ROWS * snap, 8), 8), :],
            seam_ref[pl.ds(pl.multiple_of(ROWS * snap + 8, 8), 8), :],
            seam_edges[snap],
        )
        for sweep in range(3):
            tiles = 3 if sweep < 2 else 2
            fresh_fields = []
            for level in range(LEVELS):
                here = fields[level]
                rows = along_rows(here)
                fresh = []
                for tile in range(tiles):
                    near = rows[tile] + pltpu.roll(here[tile], 1, 1) + pltpu.roll(here[tile], LANES - 1, 1)
                    if level > 0:
                        near = near + fields[level - 1][tile]
                    if level < LEVELS - 1:
                        near = near + fields[level + 1][tile]
                    value = here[tile] + SMOOTH_RATE * (near - 6.0 * here[tile])
                    fresh.append(jnp.where(inside, value, 0.0) if tile == 2 else value)
                fresh_fields.append(tuple(fresh))
            rows = along_rows(seam)
            fresh = []
            for tile in range(tiles):
                here = seam[tile]
                near = rows[tile] + pltpu.roll(here, 1, 1) + pltpu.roll(here, LANES - 1, 1)
                near = near + jnp.where(lane >= 16, pltpu.roll(here, 16, 1), 0.0)
                near = near + jnp.where(lane < LANES - 16, pltpu.roll(here, LANES - 16, 1), 0.0)
                value = here + SMOOTH_RATE * (near - 6.0 * here)
                fresh.append(jnp.where(inside, value, 0.0) if tile == 2 else value)
            fields, seam = fresh_fields, tuple(fresh)
        tall_seam = jnp.concatenate(seam, axis=0)
        for level in range(LEVELS):
            first = pltpu.roll(tall_seam, (LANES - 16 * level - 3) % LANES, 1)
            last = pltpu.roll(tall_seam, (117 - 16 * level) % LANES, 1)
            value = jnp.concatenate(fields[level], axis=0)
            value = value + jnp.where(wide_lane < 3, first, jnp.where(wide_lane >= LANES - 3, last, 0.0))
            done[snap - begin, pl.ds(ROWS * level, ROWS), :] = value
        return carry

    lax.fori_loop(begin, begin + PART, snapshot, 0, unroll=2)
    group = lax.axis_index("tm")
    for snap in range(PART):
        keep_ref[snap] = done[snap, pl.ds(pl.multiple_of(HALF_ROWS * group, 8), HALF_ROWS), :]
        send_ref[snap] = done[snap, pl.ds(pl.multiple_of(HALF_ROWS * (1 - group), 8), HALF_ROWS), :]


def pieces(values, count):
    out = []
    for index in range(count):
        piece = values.astype(BF16)
        out.append(piece)
        if index < count - 1:
            values = values - piece.astype(F32)
    return out


def transposed_product(left, right):
    return lax.dot_general(left, right, (((1,), (1,)), ((), ())), preferred_element_type=F32)


def basis_copies(half, q_ref, blocks, sems):
    copies = [
        pltpu.make_async_copy(
            q_ref.at[:, pl.ds(pl.multiple_of(HALF_ROWS * half + QROWS * part, QROWS), QROWS), :],
            blocks.at[part],
            sems.at[part],
        )
        for part in range(HALF_ROWS // QROWS)
    ]
    for copy in copies:
        copy.start()
    return copies


def split_block(block, part, count, stack_ref):
    for sub in range(QROWS // CHUNK):
        turned = jnp.swapaxes(block[:, pl.ds(CHUNK * sub, CHUNK), :], 0, 1)
        for inner in range(CHUNK):
            at = pl.ds(LANES * (QROWS * part + CHUNK * sub + inner), LANES)
            for index, piece in enumerate(pieces(turned[inner], count)):
                stack_ref[pl.ds(EOFS * index, EOFS), at] = piece


def basis_gram_kernel(order_ref, q_ref, stack_ref, gram_ref, blocks, total, sems):
    copies = basis_copies(lax.axis_index("tm"), q_ref, blocks, sems)
    for part, copy in enumerate(copies):
        copy.wait()
        split_block(blocks.at[part], part, 3, stack_ref)
        stack = stack_ref[:, pl.ds(QROWS * LANES * part, QROWS * LANES)]
        product = transposed_product(stack, stack)
        total[...] = product if part == 0 else total[...] + product
    down = total[pl.ds(0, 64), :] + total[pl.ds(64, 64), :] + total[pl.ds(128, 64), :]
    gram_ref[...] = down[:, 0:64] + down[:, 64:128] + down[:, 128:192]


def basis_stack_kernel(order_ref, q_ref, stack_ref, blocks, sems):
    copies = basis_copies(1 - lax.axis_index("tm"), q_ref, blocks, sems)
    for part, copy in enumerate(copies):
        copy.wait()
        split_block(blocks.at[part], part, 2, stack_ref)


def rows_of(refs, at):
    return jnp.concatenate([ref[:, at, :] for ref in refs], axis=0)


def snapshot_columns(refs, start, count):
    turned = jnp.swapaxes(rows_of(refs, pl.ds(start, CHUNK)), 0, 1)
    return [pieces(turned[i], count) for i in range(CHUNK)]


def in_order(mine, other):
    first = lax.axis_index("tm") == 0
    return jnp.where(first, mine, other), jnp.where(first, other, mine)


def own_gram_kernel(stack_ref, one_ref, two_ref, cross_ref, square_ref, pieces_ref, mine_ref):
    mine_ref[pl.ds(0, PART)] = one_ref[...]
    mine_ref[pl.ds(PART, PART)] = two_ref[...]

    def block(step, carry):
        cross, square = carry
        columns = snapshot_columns([mine_ref], pl.multiple_of(CHUNK * step, CHUNK), 3)
        columns = jnp.concatenate([jnp.concatenate(c, axis=0) for c in columns], axis=1)
        width = CHUNK * LANES
        at = pl.ds(pl.multiple_of(width * step, width), width)
        pieces_ref[:, at] = columns
        return cross + transposed_product(stack_ref[:, at], columns), square + transposed_product(columns, columns)

    zeros = (jnp.zeros((192, 24), F32), jnp.zeros((24, 24), F32))
    cross_ref[...], square_ref[...] = lax.fori_loop(0, HALF_ROWS // CHUNK, block, zeros)


def folded(sums, rows):
    down = sums[0:rows] + sums[rows : 2 * rows] + sums[2 * rows : 3 * rows]
    return down[:, 0:8] + down[:, 8:16] + down[:, 16:24]


def snapshot_gram_kernel(
    stack_ref, gram_ref, pieces_ref, other_one_ref, other_two_ref, cross_ref, square_ref, order_ref, own_ref, partner_ref, columns, joined
):
    for step in range(HALF_ROWS // CHUNK):
        other = snapshot_columns([other_one_ref, other_two_ref], CHUNK * step, 3)
        columns[:, pl.ds(CHUNK * LANES * step, CHUNK * LANES)] = jnp.concatenate(
            [jnp.concatenate(c, axis=0) for c in other], axis=1
        )
    cross = transposed_product(stack_ref[...], columns[...])
    square = transposed_product(columns[...], columns[...])
    mixed = transposed_product(pieces_ref[...], columns[...])
    mixed = folded(mixed, 8)
    projection = jnp.concatenate(in_order(folded(cross_ref[...], 64), folded(cross, 64)), axis=1)
    early, late = in_order(folded(square_ref[...], 8), folded(square, 8))
    upper, _ = in_order(mixed, jnp.transpose(mixed))
    square = jnp.concatenate(
        [jnp.concatenate([early, upper], axis=1), jnp.concatenate([jnp.transpose(upper), late], axis=1)], axis=0
    )
    gram = gram_ref[...]
    low, high = gram[0:32, 0:32], gram[32:64, 32:64]
    row = lax.broadcasted_iota(jnp.int32, (32, 32), 0)
    column = lax.broadcasted_iota(jnp.int32, (32, 32), 1)
    diagonal = jnp.sum(jnp.where(row == column, high, 0.0), axis=0, keepdims=True)
    both = jnp.where(row >= column, low, high)
    below = jnp.concatenate(
        [square, jnp.zeros((16, 16), F32), jnp.broadcast_to(diagonal, (16, 32))], axis=1
    )
    right = jnp.concatenate([jnp.transpose(projection), below], axis=0)
    joined[...] = jnp.concatenate([both, gram[32:64, 0:32], right], axis=1)
    core = lax.axis_index("core")
    own_ref[...] = joined[pl.ds(pl.multiple_of(SIDE * core, 8), SIDE), :]
    partner_ref[...] = joined[pl.ds(pl.multiple_of(SIDE * (1 - core), 8), SIDE), :]


def pair_kernel(one_ref, two_ref, out_ref):
    out_ref[...] = jnp.broadcast_to((one_ref[...] + two_ref[...])[None], out_ref.shape)


def group_kernel(parts_ref, out_ref):
    out_ref[...] = jnp.broadcast_to(jnp.sum(parts_ref[...], axis=0)[None], out_ref.shape)


def factor_kernel(cells, parts_ref, maps_ref, coeffs_ref):
    count = parts_ref.shape[0] // 2
    totals = jnp.concatenate(
        [jnp.sum(parts_ref[pl.ds(count * core, count)], axis=0) for core in range(2)], axis=0
    )
    row = lax.broadcasted_iota(jnp.int32, (EOFS, EOFS), 0)
    column = lax.broadcasted_iota(jnp.int32, (EOFS, EOFS), 1)
    both = totals[:, 0:32]
    once = jnp.concatenate(
        [jnp.concatenate([both, jnp.zeros((32, 32), F32)], axis=1), jnp.concatenate([totals[:, 32:64], both], axis=1)], axis=0
    )
    once = jnp.where(((row < 32) & (row > column)) | ((row >= 32) & ((column < 32) | (row < column))), once, 0.0)
    corner = jnp.concatenate([both, jnp.zeros((32, 32), F32)], axis=1)
    diagonal = jnp.concatenate([corner, jnp.broadcast_to(totals[16:17, 64:128], (32, EOFS))], axis=0)
    basis_gram = once + jnp.transpose(once) + jnp.where(row == column, diagonal, 0.0)
    root = math.sqrt(cells)
    coeffs_t = totals[0:16, 64:128] * (1.0 / root)
    snap_gram = totals[16:32, 64:80]
    coeffs_ref[...] = jnp.where(lax.axis_index("tm") == 0, coeffs_t[0:8, :], coeffs_t[8:16, :])
    mixed = (2.0 * STEP_SIZE * root) * coeffs_t + (STEP_SIZE * STEP_SIZE) * jnp.dot(
        snap_gram, coeffs_t, precision=HIGHEST, preferred_element_type=F32
    )
    grown = lax.dot_general(
        coeffs_t, mixed, (((0,), (0,)), ((), ())), precision=HIGHEST, preferred_element_type=F32
    )
    gram = (basis_gram + grown) * (1.0 / cells)
    rows = lax.broadcasted_iota(jnp.int32, (EOFS, EOFS), 0)
    columns = lax.broadcasted_iota(jnp.int32, (EOFS, EOFS), 1)
    work = jnp.concatenate([gram, (rows == columns).astype(F32)], axis=1)
    blocks = [work[8 * i : 8 * i + 8, :] for i in range(8)]
    results = []
    for panel in range(8):
        lower = blocks[panel:]
        columns = [
            [jnp.broadcast_to(b[:, 8 * panel + k : 8 * panel + k + 1], (8, LANES)) for b in lower] for k in range(8)
        ]
        rows = [lower[0][k : k + 1, :] for k in range(8)]
        for k in range(8):
            pivot = columns[k][0][k : k + 1, :]
            if k % 2 == 0:
                corner, upper, side = columns[k + 1][0][k + 1 : k + 2, :], columns[k + 1][0][k : k + 1, :], columns[k][0][k + 1 : k + 2, :]
                inverse = 1.0 / pivot
                following = pivot * (1.0 / (pivot * corner - upper * side))
            else:
                inverse = following
            factors = [c * inverse for c in columns[k]]
            for m in range(k + 1, 8):
                entry = columns[m][0][k : k + 1, :]
                columns[m] = [c - f * entry for c, f in zip(columns[m], factors)]
                rows[m] = rows[m] - factors[0][m : m + 1, :] * rows[k]
            for i in range(panel + 1, 8):
                blocks[i] = blocks[i] - factors[i - panel] * rows[k]
            results.append(rows[k] * lax.rsqrt(pivot))
    inverse = jnp.concatenate(results, axis=0)[:, EOFS:]
    update = lax.dot_general(
        inverse, coeffs_t, (((1,), (1,)), ((), ())), precision=HIGHEST, preferred_element_type=F32
    )
    rows = [
        jnp.concatenate([inverse_part, inverse_part, update_part, update_part], axis=1)
        for inverse_part, update_part in zip(pieces(inverse, 2), pieces(STEP_SIZE * update, 2))
    ]
    maps_ref[...] = jnp.concatenate(rows, axis=0)


def final_kernel(
    maps_ref, near_ref, far_ref, keep_ref, here_one_ref, here_two_ref, send_one_ref, send_two_ref, late_ref, out_ref, blocks, sems
):
    near_refs = (near_ref, [keep_ref], [here_one_ref, here_two_ref])
    far_refs = (far_ref, [send_one_ref, send_two_ref], [late_ref])
    group = lax.axis_index("tm")
    steps = HALF_ROWS // FINAL_ROWS
    copies = []
    for step in range(2 * steps):
        near = step < steps
        half = group if near else 1 - group
        local = step % steps
        stack_ref, mine, other = near_refs if near else far_refs
        for sub in range(FINAL_ROWS // CHUNK):
            start = local * FINAL_ROWS + CHUNK * sub
            at = pl.ds(start, CHUNK)
            early, late = in_order(
                jnp.swapaxes(rows_of(mine, at), 0, 1), jnp.swapaxes(rows_of(other, at), 0, 1)
            )
            columns = jnp.concatenate(
                [
                    jnp.concatenate(pieces(jnp.concatenate([early[i], late[i]], axis=0), 2), axis=0)
                    for i in range(CHUNK)
                ],
                axis=1,
            )
            stack = stack_ref[pl.ds(0, 2 * EOFS), pl.ds(start * LANES, CHUNK * LANES)]
            both = jnp.dot(maps_ref[...], jnp.concatenate([stack, columns], axis=0), preferred_element_type=F32)
            result = both[0:EOFS, :] + both[EOFS:, :]
            result = jnp.stack([result[:, LANES * i : LANES * (i + 1)] for i in range(CHUNK)])
            blocks[step, :, pl.ds(CHUNK * sub, CHUNK), :] = jnp.swapaxes(result, 0, 1)
        to = pl.ds(pl.multiple_of(HALF_ROWS * half + FINAL_ROWS * local, FINAL_ROWS), FINAL_ROWS)
        copy = pltpu.make_async_copy(blocks.at[step], out_ref.at[:, to, :], sems.at[step])
        copy.start()
        copies.append(copy)
    for copy in copies:
        copy.wait()


def swapped(values, axis, first):
    count = lax.axis_size(axis)
    pairs = [(i, (i + 1) % count) for i in range(first, count - first % 2 * (axis == "lat"), 2)]
    return lax.ppermute(values, axis, [p for one, two in pairs for p in ((one, two), (two, one))])


def across(values, axis):
    return lax.ppermute(values, axis, [(0, 1), (1, 0)])


def gathered(values, axes):
    return lax.all_to_all(values, axes, 0, 0)


def update(snapshots, basis):
    lat_count = lax.axis_size("lat")
    cells = CELL_ROWS * LANES * lat_count * lax.axis_size(LON)
    q = pltpu.with_memory_space_constraint(basis.reshape(EOFS, CELL_ROWS, LANES), pltpu.HBM)

    packed = call(pack_kernel, [VMEM], shape(CELL_ROWS, LANES))(snapshots)
    chip = swapped(packed, LON, 1)
    beside = across(packed, "core")
    seam, one, two = call(
        seam_kernel, [VMEM] * 4, (shape(CELL_ROWS, LANES), shape(27, 8, LANES), shape(27, 8, LANES))
    )(snapshots, packed, chip, beside)
    one, two = swapped(one, "lat", 0), swapped(two, "lat", 1)
    parts = HALF_ROWS // QROWS
    stack, gram = call(
        basis_gram_kernel,
        [VMEM, ANY],
        (shape(3 * EOFS, HALF_CELLS, dtype=BF16), shape(EOFS, EOFS)),
        [pltpu.VMEM((parts, EOFS, QROWS, LANES), F32), pltpu.VMEM((192, 192), F32), pltpu.SemaphoreType.DMA((parts,))],
        traffic=8 << 20,
    )(seam, q)
    far = call(
        basis_stack_kernel,
        [VMEM, ANY],
        shape(2 * EOFS, HALF_CELLS, dtype=BF16),
        [pltpu.VMEM((parts, EOFS, QROWS, LANES), F32), pltpu.SemaphoreType.DMA((parts,))],
        traffic=6 << 20,
    )(gram, q)
    order, keep, send, here = far, [], [], []
    for begin in (0, PART):
        kept, sent = call(
            functools.partial(smooth_kernel, begin),
            [VMEM] * 5,
            (shape(PART, HALF_ROWS, LANES),) * 2,
            [pltpu.VMEM((PART, CELL_ROWS, LANES), F32), pltpu.VMEM((SNAPS, 8, LANES), F32)],
        )(snapshots, seam, one, two, order)
        here.append(across(sent, "tm"))
        order = kept
        keep.append(kept)
        send.append(sent)
    cross, square, split, keep = call(
        own_gram_kernel,
        [VMEM] * 3,
        (shape(192, 24), shape(24, 24), shape(24, HALF_CELLS, dtype=BF16), shape(SNAPS, HALF_ROWS, LANES)),
        traffic=4 << 20,
    )(stack, *keep)
    side = shape(SIDE, LANES)
    late = across(keep, "tm")
    mine, theirs = call(
        snapshot_gram_kernel, [VMEM] * 8, (side, side), [pltpu.VMEM((24, HALF_CELLS), BF16), pltpu.VMEM((PAYLOAD, LANES), F32)]
    )(stack, gram, split, *here, cross, square, far)
    group = lax.axis_size(("pair", "tm"))
    spread = call(pair_kernel, [VMEM] * 2, shape(group, SIDE, LANES))(mine, across(theirs, "core"))
    spread = gathered(spread, ("pair", "tm"))
    spread = call(group_kernel, [VMEM], shape(2 * lat_count, SIDE, LANES))(spread)
    spread = gathered(spread, ("core", "lat"))
    maps, coeffs_t = call(
        functools.partial(factor_kernel, cells), [VMEM], (shape(2 * EOFS, 160, dtype=BF16), shape(SNAPS, EOFS))
    )(spread)
    final_steps = CELL_ROWS // FINAL_ROWS
    new_basis = pl.pallas_call(
        final_kernel,
        out_shape=shape(EOFS, CELL_ROWS, LANES),
        in_specs=[VMEM] * 9,
        out_specs=ANY,
        scratch_shapes=[
            pltpu.VMEM((final_steps, EOFS, FINAL_ROWS, LANES), F32),
            pltpu.SemaphoreType.DMA((final_steps,)),
        ],
        compiler_params=pltpu.CompilerParams(vmem_limit_bytes=8 << 20),
    )(maps, stack, far, keep, *here, *send, late)
    return (new_basis.reshape(basis.shape), coeffs_t.T)


def solution(mesh):
    pairs = mesh.shape["lon"] // 2
    split = Mesh(mesh.devices.reshape(pairs, 2, *mesh.devices.shape[1:]), LON + tuple(mesh.axis_names[1:]))
    fields = P(None, None, "lat", LON)
    return jax.shard_map(
        update,
        mesh=split,
        in_specs=(P("tm", None, "lat", LON), fields),
        out_specs=(fields, P(None, "tm")),
        check_vma=False,
    )
```

```python
import functools
import math

import jax
import jax.numpy as jnp
from jax import lax
from jax.experimental import pallas as pl
from jax.experimental.pallas import tpu as pltpu
from jax.sharding import Mesh, PartitionSpec as P


SMOOTH_RATE = 0.1
STEP_SIZE = 0.25
SNAPS = 8
LEVELS = 8
ROWS = 16
LANES = 128
EOFS = 64
CELL_ROWS = LEVELS * ROWS
HALF_ROWS = CELL_ROWS // 2
HALF_CELLS = HALF_ROWS * LANES
CHUNK = 8
PAYLOAD = 32
SIDE = PAYLOAD // 2
QROWS = 16
FINAL_ROWS = 16
PART = SNAPS // 2
LON = ("pair", "core")
F32 = jnp.float32
BF16 = jnp.bfloat16
HIGHEST = lax.Precision.HIGHEST
VMEM = pl.BlockSpec(memory_space=pltpu.VMEM)
ANY = pl.BlockSpec(memory_space=pl.ANY)


def lanes_of(shape):
    return lax.broadcasted_iota(jnp.int32, shape, len(shape) - 1)


def shape(*dims, dtype=F32):
    return jax.ShapeDtypeStruct(dims, dtype)


def call(kernel, inputs, outputs, scratch=(), flops=1000000, traffic=1000000, megabytes=8):
    return pl.pallas_call(
        kernel,
        out_shape=outputs,
        in_specs=inputs,
        out_specs=jax.tree.map(lambda _: VMEM, outputs),
        scratch_shapes=scratch,
        cost_estimate=pl.CostEstimate(flops=flops, bytes_accessed=traffic, transcendentals=0),
        compiler_params=pltpu.CompilerParams(vmem_limit_bytes=megabytes << 20),
    )


def pack_kernel(x_ref, packed_ref):
    lane = lanes_of((ROWS, LANES))
    for snap in range(SNAPS):
        packed = jnp.zeros((ROWS, LANES), F32)
        for level in range(LEVELS):
            turned = pltpu.roll(x_ref[snap, level], 16 * level + 3, 1)
            packed = jnp.where((lane >= 16 * level) & (lane < 16 * level + 6), turned, packed)
        packed_ref[pl.ds(ROWS * snap, ROWS), :] = packed


def seam_kernel(x_ref, packed_ref, across_ref, beside_ref, order_ref, seam_ref, one_ref, two_ref):
    packed = packed_ref[...]
    lane = lanes_of(packed.shape) % 16
    eastern = lax.axis_index("core") == 1
    far, near = across_ref[...] - packed, beside_ref[...] - packed
    west = jnp.where(lane < 3, jnp.where(eastern, near, far), 0.0)
    east = pltpu.roll(jnp.where((lane >= 3) & (lane < 6), jnp.where(eastern, far, near), 0.0), 8, 1)
    seam_ref[...] = west + east
    even = lax.axis_index("lat") % 2 == 0
    for snap in range(SNAPS):
        at = pl.ds(8 * snap, 8)
        low = jnp.swapaxes(x_ref[snap, :, pl.ds(0, 8), :], 0, 1)
        high = jnp.swapaxes(x_ref[snap, :, pl.ds(8, 8), :], 0, 1)
        for row in range(3):
            one_ref[8 * row + snap] = jnp.where(even, high[5 + row], low[row])
            two_ref[8 * row + snap] = jnp.where(even, low[row], high[5 + row])
    low = jnp.swapaxes(jnp.stack([seam_ref[pl.ds(ROWS * snap, 8), :] for snap in range(SNAPS)]), 0, 1)
    high = jnp.swapaxes(jnp.stack([seam_ref[pl.ds(ROWS * snap + 8, 8), :] for snap in range(SNAPS)]), 0, 1)
    for row in range(3):
        one_ref[24 + row] = jnp.where(even, high[5 + row], low[row])
        two_ref[24 + row] = jnp.where(even, low[row], high[5 + row])


def smooth_kernel(begin, x_ref, seam_ref, one_ref, two_ref, order_ref, keep_ref, send_ref, done, seam_edges):
    lat = lax.axis_index("lat")
    even = lat % 2 == 0
    not_first = jnp.where(lat == 0, 0, 1)
    not_last = jnp.where(lat == lax.axis_size("lat") - 1, 0, 1)
    row = lax.broadcasted_iota(jnp.int32, (8, LANES), 0)
    lane = lanes_of((8, LANES))
    inside = jnp.where(row < 4, not_last, not_first) == 1
    zero = jnp.zeros((8, LANES), F32)
    wide_lane = lanes_of((ROWS, LANES))

    def along_rows(field):
        tall = jnp.concatenate(field, axis=0)
        near = pltpu.roll(tall, 1, 0) + pltpu.roll(tall, 23, 0)
        return near[0:8], near[8:16], near[16:24]

    norths = [jnp.where(even, one_ref[24 + i], two_ref[24 + i]) for i in range(3)]
    souths = [jnp.where(even, two_ref[24 + i], one_ref[24 + i]) for i in range(3)]
    seam_edges[...] = jnp.swapaxes(jnp.stack(norths + [zero, zero] + souths), 0, 1)

    def snapshot(snap, carry):
        edges = jnp.swapaxes(
            jnp.stack(
                [jnp.where(even, one_ref[8 * i + snap], two_ref[8 * i + snap]) for i in range(3)]
                + [zero, zero]
                + [jnp.where(even, two_ref[8 * i + snap], one_ref[8 * i + snap]) for i in range(3)]
            ),
            0,
            1,
        )
        fields = [
            (x_ref[snap, level, pl.ds(0, 8), :], x_ref[snap, level, pl.ds(8, 8), :], edges[level])
            for level in range(LEVELS)
        ]
        seam = (
            seam_ref[pl.ds(pl.multiple_of(ROWS * snap, 8), 8), :],
            seam_ref[pl.ds(pl.multiple_of(ROWS * snap + 8, 8), 8), :],
            seam_edges[snap],
        )
        for sweep in range(3):
            tiles = 3 if sweep < 2 else 2
            fresh_fields = []
            for level in range(LEVELS):
                here = fields[level]
                rows = along_rows(here)
                fresh = []
                for tile in range(tiles):
                    near = rows[tile] + pltpu.roll(here[tile], 1, 1) + pltpu.roll(here[tile], LANES - 1, 1)
                    if level > 0:
                        near = near + fields[level - 1][tile]
                    if level < LEVELS - 1:
                        near = near + fields[level + 1][tile]
                    value = here[tile] + SMOOTH_RATE * (near - 6.0 * here[tile])
                    fresh.append(jnp.where(inside, value, 0.0) if tile == 2 else value)
                fresh_fields.append(tuple(fresh))
            rows = along_rows(seam)
            fresh = []
            for tile in range(tiles):
                here = seam[tile]
                near = rows[tile] + pltpu.roll(here, 1, 1) + pltpu.roll(here, LANES - 1, 1)
                near = near + jnp.where(lane >= 16, pltpu.roll(here, 16, 1), 0.0)
                near = near + jnp.where(lane < LANES - 16, pltpu.roll(here, LANES - 16, 1), 0.0)
                value = here + SMOOTH_RATE * (near - 6.0 * here)
                fresh.append(jnp.where(inside, value, 0.0) if tile == 2 else value)
            fields, seam = fresh_fields, tuple(fresh)
        tall_seam = jnp.concatenate(seam, axis=0)
        for level in range(LEVELS):
            first = pltpu.roll(tall_seam, (LANES - 16 * level - 3) % LANES, 1)
            last = pltpu.roll(tall_seam, (117 - 16 * level) % LANES, 1)
            value = jnp.concatenate(fields[level], axis=0)
            value = value + jnp.where(wide_lane < 3, first, jnp.where(wide_lane >= LANES - 3, last, 0.0))
            done[snap - begin, pl.ds(ROWS * level, ROWS), :] = value
        return carry

    lax.fori_loop(begin, begin + PART, snapshot, 0, unroll=2)
    group = lax.axis_index("tm")
    for snap in range(PART):
        keep_ref[snap] = done[snap, pl.ds(pl.multiple_of(HALF_ROWS * group, 8), HALF_ROWS), :]
        send_ref[snap] = done[snap, pl.ds(pl.multiple_of(HALF_ROWS * (1 - group), 8), HALF_ROWS), :]


def pieces(values, count):
    out = []
    for index in range(count):
        piece = values.astype(BF16)
        out.append(piece)
        if index < count - 1:
            values = values - piece.astype(F32)
    return out


def transposed_product(left, right):
    return lax.dot_general(left, right, (((1,), (1,)), ((), ())), preferred_element_type=F32)


def basis_copies(half, q_ref, blocks, sems):
    copies = [
        pltpu.make_async_copy(
            q_ref.at[:, pl.ds(pl.multiple_of(HALF_ROWS * half + QROWS * part, QROWS), QROWS), :],
            blocks.at[part],
            sems.at[part],
        )
        for part in range(HALF_ROWS // QROWS)
    ]
    for copy in copies:
        copy.start()
    return copies


def split_block(block, part, count, stack_ref):
    for sub in range(QROWS // CHUNK):
        turned = jnp.swapaxes(block[:, pl.ds(CHUNK * sub, CHUNK), :], 0, 1)
        for inner in range(CHUNK):
            at = pl.ds(LANES * (QROWS * part + CHUNK * sub + inner), LANES)
            for index, piece in enumerate(pieces(turned[inner], count)):
                stack_ref[pl.ds(EOFS * index, EOFS), at] = piece


def basis_gram_kernel(order_ref, q_ref, stack_ref, gram_ref, blocks, total, sems):
    copies = basis_copies(lax.axis_index("tm"), q_ref, blocks, sems)
    for part, copy in enumerate(copies):
        copy.wait()
        split_block(blocks.at[part], part, 3, stack_ref)
        stack = stack_ref[:, pl.ds(QROWS * LANES * part, QROWS * LANES)]
        product = transposed_product(stack, stack)
        total[...] = product if part == 0 else total[...] + product
    down = total[pl.ds(0, 64), :] + total[pl.ds(64, 64), :] + total[pl.ds(128, 64), :]
    gram_ref[...] = down[:, 0:64] + down[:, 64:128] + down[:, 128:192]


def basis_stack_kernel(order_ref, q_ref, stack_ref, blocks, sems):
    copies = basis_copies(1 - lax.axis_index("tm"), q_ref, blocks, sems)
    for part, copy in enumerate(copies):
        copy.wait()
        split_block(blocks.at[part], part, 2, stack_ref)


def rows_of(refs, at):
    return jnp.concatenate([ref[:, at, :] for ref in refs], axis=0)


def snapshot_columns(refs, start, count):
    turned = jnp.swapaxes(rows_of(refs, pl.ds(start, CHUNK)), 0, 1)
    return [pieces(turned[i], count) for i in range(CHUNK)]


def in_order(mine, other):
    first = lax.axis_index("tm") == 0
    return jnp.where(first, mine, other), jnp.where(first, other, mine)


def own_gram_kernel(stack_ref, one_ref, two_ref, cross_ref, square_ref, pieces_ref, mine_ref):
    mine_ref[pl.ds(0, PART)] = one_ref[...]
    mine_ref[pl.ds(PART, PART)] = two_ref[...]

    def block(step, carry):
        cross, square = carry
        columns = snapshot_columns([mine_ref], pl.multiple_of(CHUNK * step, CHUNK), 3)
        columns = jnp.concatenate([jnp.concatenate(c, axis=0) for c in columns], axis=1)
        width = CHUNK * LANES
        at = pl.ds(pl.multiple_of(width * step, width), width)
        pieces_ref[:, at] = columns
        return cross + transposed_product(stack_ref[:, at], columns), square + transposed_product(columns, columns)

    zeros = (jnp.zeros((192, 24), F32), jnp.zeros((24, 24), F32))
    cross_ref[...], square_ref[...] = lax.fori_loop(0, HALF_ROWS // CHUNK, block, zeros)


def folded(sums, rows):
    down = sums[0:rows] + sums[rows : 2 * rows] + sums[2 * rows : 3 * rows]
    return down[:, 0:8] + down[:, 8:16] + down[:, 16:24]


def snapshot_gram_kernel(
    stack_ref, gram_ref, pieces_ref, other_one_ref, other_two_ref, cross_ref, square_ref, order_ref, own_ref, partner_ref, columns, joined
):
    for step in range(HALF_ROWS // CHUNK):
        other = snapshot_columns([other_one_ref, other_two_ref], CHUNK * step, 3)
        columns[:, pl.ds(CHUNK * LANES * step, CHUNK * LANES)] = jnp.concatenate(
            [jnp.concatenate(c, axis=0) for c in other], axis=1
        )
    cross = transposed_product(stack_ref[...], columns[...])
    square = transposed_product(columns[...], columns[...])
    mixed = transposed_product(pieces_ref[...], columns[...])
    mixed = folded(mixed, 8)
    projection = jnp.concatenate(in_order(folded(cross_ref[...], 64), folded(cross, 64)), axis=1)
    early, late = in_order(folded(square_ref[...], 8), folded(square, 8))
    upper, _ = in_order(mixed, jnp.transpose(mixed))
    square = jnp.concatenate(
        [jnp.concatenate([early, upper], axis=1), jnp.concatenate([jnp.transpose(upper), late], axis=1)], axis=0
    )
    gram = gram_ref[...]
    low, high = gram[0:32, 0:32], gram[32:64, 32:64]
    row = lax.broadcasted_iota(jnp.int32, (32, 32), 0)
    column = lax.broadcasted_iota(jnp.int32, (32, 32), 1)
    diagonal = jnp.sum(jnp.where(row == column, high, 0.0), axis=0, keepdims=True)
    both = jnp.where(row >= column, low, high)
    below = jnp.concatenate(
        [square, jnp.zeros((16, 16), F32), jnp.broadcast_to(diagonal, (16, 32))], axis=1
    )
    right = jnp.concatenate([jnp.transpose(projection), below], axis=0)
    joined[...] = jnp.concatenate([both, gram[32:64, 0:32], right], axis=1)
    core = lax.axis_index("core")
    own_ref[...] = joined[pl.ds(pl.multiple_of(SIDE * core, 8), SIDE), :]
    partner_ref[...] = joined[pl.ds(pl.multiple_of(SIDE * (1 - core), 8), SIDE), :]


def pair_kernel(one_ref, two_ref, out_ref):
    out_ref[...] = jnp.broadcast_to((one_ref[...] + two_ref[...])[None], out_ref.shape)


def group_kernel(parts_ref, out_ref):
    out_ref[...] = jnp.broadcast_to(jnp.sum(parts_ref[...], axis=0)[None], out_ref.shape)


def factor_kernel(cells, parts_ref, maps_ref, coeffs_ref):
    count = parts_ref.shape[0] // 2
    totals = jnp.concatenate(
        [jnp.sum(parts_ref[pl.ds(count * core, count)], axis=0) for core in range(2)], axis=0
    )
    row = lax.broadcasted_iota(jnp.int32, (EOFS, EOFS), 0)
    column = lax.broadcasted_iota(jnp.int32, (EOFS, EOFS), 1)
    both = totals[:, 0:32]
    once = jnp.concatenate(
        [jnp.concatenate([both, jnp.zeros((32, 32), F32)], axis=1), jnp.concatenate([totals[:, 32:64], both], axis=1)], axis=0
    )
    once = jnp.where(((row < 32) & (row > column)) | ((row >= 32) & ((column < 32) | (row < column))), once, 0.0)
    corner = jnp.concatenate([both, jnp.zeros((32, 32), F32)], axis=1)
    diagonal = jnp.concatenate([corner, jnp.broadcast_to(totals[16:17, 64:128], (32, EOFS))], axis=0)
    basis_gram = once + jnp.transpose(once) + jnp.where(row == column, diagonal, 0.0)
    root = math.sqrt(cells)
    coeffs_t = totals[0:16, 64:128] * (1.0 / root)
    snap_gram = totals[16:32, 64:80]
    coeffs_ref[...] = jnp.where(lax.axis_index("tm") == 0, coeffs_t[0:8, :], coeffs_t[8:16, :])
    mixed = (2.0 * STEP_SIZE * root) * coeffs_t + (STEP_SIZE * STEP_SIZE) * jnp.dot(
        snap_gram, coeffs_t, precision=HIGHEST, preferred_element_type=F32
    )
    grown = lax.dot_general(
        coeffs_t, mixed, (((0,), (0,)), ((), ())), precision=HIGHEST, preferred_element_type=F32
    )
    gram = (basis_gram + grown) * (1.0 / cells)
    rows = lax.broadcasted_iota(jnp.int32, (EOFS, EOFS), 0)
    columns = lax.broadcasted_iota(jnp.int32, (EOFS, EOFS), 1)
    work = jnp.concatenate([gram, (rows == columns).astype(F32)], axis=1)
    blocks = [work[8 * i : 8 * i + 8, :] for i in range(8)]
    results = []
    for panel in range(8):
        lower = blocks[panel:]
        columns = [
            [jnp.broadcast_to(b[:, 8 * panel + k : 8 * panel + k + 1], (8, LANES)) for b in lower] for k in range(8)
        ]
        rows = [lower[0][k : k + 1, :] for k in range(8)]
        for k in range(8):
            pivot = columns[k][0][k : k + 1, :]
            if k % 2 == 0:
                corner, upper, side = columns[k + 1][0][k + 1 : k + 2, :], columns[k + 1][0][k : k + 1, :], columns[k][0][k + 1 : k + 2, :]
                inverse = 1.0 / pivot
                following = pivot * (1.0 / (pivot * corner - upper * side))
            else:
                inverse = following
            factors = [c * inverse for c in columns[k]]
            for m in range(k + 1, 8):
                entry = columns[m][0][k : k + 1, :]
                columns[m] = [c - f * entry for c, f in zip(columns[m], factors)]
                rows[m] = rows[m] - factors[0][m : m + 1, :] * rows[k]
            for i in range(panel + 1, 8):
                blocks[i] = blocks[i] - factors[i - panel] * rows[k]
            results.append(rows[k] * lax.rsqrt(pivot))
    inverse = jnp.concatenate(results, axis=0)[:, EOFS:]
    update = lax.dot_general(
        inverse, coeffs_t, (((1,), (1,)), ((), ())), precision=HIGHEST, preferred_element_type=F32
    )
    rows = [
        jnp.concatenate([inverse_part, inverse_part, update_part, update_part], axis=1)
        for inverse_part, update_part in zip(pieces(inverse, 2), pieces(STEP_SIZE * update, 2))
    ]
    maps_ref[...] = jnp.concatenate(rows, axis=0)


def final_kernel(
    maps_ref, near_ref, far_ref, keep_ref, here_one_ref, here_two_ref, send_one_ref, send_two_ref, late_ref, out_ref, blocks, sems
):
    near_refs = (near_ref, [keep_ref], [here_one_ref, here_two_ref])
    far_refs = (far_ref, [send_one_ref, send_two_ref], [late_ref])
    group = lax.axis_index("tm")
    steps = HALF_ROWS // FINAL_ROWS
    copies = []
    for step in range(2 * steps):
        near = step < steps
        half = group if near else 1 - group
        local = step % steps
        stack_ref, mine, other = near_refs if near else far_refs
        for sub in range(FINAL_ROWS // CHUNK):
            start = local * FINAL_ROWS + CHUNK * sub
            at = pl.ds(start, CHUNK)
            early, late = in_order(
                jnp.swapaxes(rows_of(mine, at), 0, 1), jnp.swapaxes(rows_of(other, at), 0, 1)
            )
            columns = jnp.concatenate(
                [
                    jnp.concatenate(pieces(jnp.concatenate([early[i], late[i]], axis=0), 2), axis=0)
                    for i in range(CHUNK)
                ],
                axis=1,
            )
            stack = stack_ref[pl.ds(0, 2 * EOFS), pl.ds(start * LANES, CHUNK * LANES)]
            both = jnp.dot(maps_ref[...], jnp.concatenate([stack, columns], axis=0), preferred_element_type=F32)
            result = both[0:EOFS, :] + both[EOFS:, :]
            result = jnp.stack([result[:, LANES * i : LANES * (i + 1)] for i in range(CHUNK)])
            blocks[step, :, pl.ds(CHUNK * sub, CHUNK), :] = jnp.swapaxes(result, 0, 1)
        to = pl.ds(pl.multiple_of(HALF_ROWS * half + FINAL_ROWS * local, FINAL_ROWS), FINAL_ROWS)
        copy = pltpu.make_async_copy(blocks.at[step], out_ref.at[:, to, :], sems.at[step])
        copy.start()
        copies.append(copy)
    for copy in copies:
        copy.wait()


def swapped(values, axis, first):
    count = lax.axis_size(axis)
    pairs = [(i, (i + 1) % count) for i in range(first, count - first % 2 * (axis == "lat"), 2)]
    return lax.ppermute(values, axis, [p for one, two in pairs for p in ((one, two), (two, one))])


def across(values, axis):
    return lax.ppermute(values, axis, [(0, 1), (1, 0)])


def gathered(values, axes):
    return lax.all_to_all(values, axes, 0, 0)


def update(snapshots, basis):
    lat_count = lax.axis_size("lat")
    cells = CELL_ROWS * LANES * lat_count * lax.axis_size(LON)
    q = pltpu.with_memory_space_constraint(basis.reshape(EOFS, CELL_ROWS, LANES), pltpu.HBM)

    packed = call(pack_kernel, [VMEM], shape(CELL_ROWS, LANES))(snapshots)
    chip = swapped(packed, LON, 1)
    beside = across(packed, "core")
    parts = HALF_ROWS // QROWS
    far = call(
        basis_stack_kernel,
        [VMEM, ANY],
        shape(2 * EOFS, HALF_CELLS, dtype=BF16),
        [pltpu.VMEM((parts, EOFS, QROWS, LANES), F32), pltpu.SemaphoreType.DMA((parts,))],
        traffic=6 << 20,
    )(packed, q)
    seam, one, two = call(
        seam_kernel, [VMEM] * 5, (shape(CELL_ROWS, LANES), shape(27, 8, LANES), shape(27, 8, LANES))
    )(snapshots, packed, chip, beside, far)
    one, two = swapped(one, "lat", 0), swapped(two, "lat", 1)
    stack, gram = call(
        basis_gram_kernel,
        [VMEM, ANY],
        (shape(3 * EOFS, HALF_CELLS, dtype=BF16), shape(EOFS, EOFS)),
        [pltpu.VMEM((parts, EOFS, QROWS, LANES), F32), pltpu.VMEM((192, 192), F32), pltpu.SemaphoreType.DMA((parts,))],
        traffic=8 << 20,
    )(seam, q)
    order, keep, send, here = gram, [], [], []
    for begin in (0, PART):
        kept, sent = call(
            functools.partial(smooth_kernel, begin),
            [VMEM] * 5,
            (shape(PART, HALF_ROWS, LANES),) * 2,
            [pltpu.VMEM((PART, CELL_ROWS, LANES), F32), pltpu.VMEM((SNAPS, 8, LANES), F32)],
        )(snapshots, seam, one, two, order)
        here.append(across(sent, "tm"))
        order = kept
        keep.append(kept)
        send.append(sent)
    cross, square, split, keep = call(
        own_gram_kernel,
        [VMEM] * 3,
        (shape(192, 24), shape(24, 24), shape(24, HALF_CELLS, dtype=BF16), shape(SNAPS, HALF_ROWS, LANES)),
        traffic=4 << 20,
    )(stack, *keep)
    side = shape(SIDE, LANES)
    late = across(keep, "tm")
    mine, theirs = call(
        snapshot_gram_kernel, [VMEM] * 8, (side, side), [pltpu.VMEM((24, HALF_CELLS), BF16), pltpu.VMEM((PAYLOAD, LANES), F32)]
    )(stack, gram, split, *here, cross, square, far)
    group = lax.axis_size(("pair", "tm"))
    spread = call(pair_kernel, [VMEM] * 2, shape(group, SIDE, LANES))(mine, across(theirs, "core"))
    spread = gathered(spread, ("pair", "tm"))
    spread = call(group_kernel, [VMEM], shape(2 * lat_count, SIDE, LANES))(spread)
    spread = gathered(spread, ("core", "lat"))
    maps, coeffs_t = call(
        functools.partial(factor_kernel, cells), [VMEM], (shape(2 * EOFS, 160, dtype=BF16), shape(SNAPS, EOFS))
    )(spread)
    final_steps = CELL_ROWS // FINAL_ROWS
    new_basis = pl.pallas_call(
        final_kernel,
        out_shape=shape(EOFS, CELL_ROWS, LANES),
        in_specs=[VMEM] * 9,
        out_specs=ANY,
        scratch_shapes=[
            pltpu.VMEM((final_steps, EOFS, FINAL_ROWS, LANES), F32),
            pltpu.SemaphoreType.DMA((final_steps,)),
        ],
        compiler_params=pltpu.CompilerParams(vmem_limit_bytes=8 << 20),
    )(maps, stack, far, keep, *here, *send, late)
    return (new_basis.reshape(basis.shape), coeffs_t.T)


def solution(mesh):
    pairs = mesh.shape["lon"] // 2
    split = Mesh(mesh.devices.reshape(pairs, 2, *mesh.devices.shape[1:]), LON + tuple(mesh.axis_names[1:]))
    fields = P(None, None, "lat", LON)
    return jax.shard_map(
        update,
        mesh=split,
        in_specs=(P("tm", None, "lat", LON), fields),
        out_specs=(fields, P(None, "tm")),
        check_vma=False,
    )
```
